256 devices in a mesh: section: 2 (over core), blk: 128 (over z, x, y).
Axes of the slice: x: 4, y: 4, z: 8, core: 2. Of those that a mesh axis runs over, the one named last changes fastest.
Arguments:
- hidden: bfloat16 [2, 384, 3072], P(None, 'blk'), may hold values from -4 to 4
- qkv_weight: bfloat16 [2, 3072, 9216], P('section', None, 'blk'), may hold values from -0.109375 to 0.109375
- out_weight: bfloat16 [2, 3072, 3072], P('section', None, 'blk'), may hold values from -0.109375 to 0.109375
- modulation: float32 [2, 50, 3, 3072], P('section'), may hold values from -3 to 3
- timestep: int32 [1], replicated, may hold values from 0 to 49
- fresh: int32 [2, 2, 128], P('section'), may hold values 0 or 1
- live: int32 [2, 128], replicated, may hold values from 0 to 1, as said below
- k_stale: bfloat16 [2, 2, 384, 3072], P('section', None, 'blk'), may hold values from -6 to 6
- v_stale: bfloat16 [2, 2, 384, 3072], P('section', None, 'blk'), may hold values from -16 to 16
Outputs:
- layer_outputs: bfloat16 [2, 2, 384, 3072], P('section', None, 'blk')
The draws below stay inside these ranges and needn't reach their ends.
Inputs may be any that keep to these rules, and one draw needn't show every extreme that they name: Block 0 of every request is live.
All inputs are finite; a program needn't handle non-finite values. No bound on the sum of `fresh` on one device may be relied on, other than what follows from the above.
Results may differ from the reference program's by a relative error of at most 0.017.
Values may be sent and summed in bfloat16 or wider, within the bound.
A program may use at most 64 MiB of HBM per device.

```python
import jax
import jax.numpy as jnp
from jax import lax

D = 3072
HEADS = 48
HEAD = 64
ROWS = 3
REQS = 2
TSTEPS = 50
NBLOCKS = 128
SEQ = 384


def draw_live(key, part):
    levels = jax.random.randint(key, (REQS, NBLOCKS), 0, 4)
    filled = (levels > 0).astype(jnp.int32)
    leading = (jnp.arange(NBLOCKS) == 0)[None, :]
    return jnp.where(leading, 1, filled).astype(jnp.int32)


def set_ends(entries, own_key, least, largest):
    spot = [jax.random.randint(jax.random.fold_in(own_key, axis), (), 0, length) for axis, length in enumerate(entries.shape)]
    widest = entries.shape.index(max(entries.shape))
    next_to = spot[:widest] + [(spot[widest] + 1) % entries.shape[widest]] + spot[widest + 1:]
    return entries.at[tuple(spot)].set(least).at[tuple(next_to)].set(largest)


def block_levels(key, extent, cuts, smallest, largest):
    factor_of = 1.0
    for position, shards_of in cuts:
        draws = jax.random.uniform(jax.random.fold_in(jax.random.fold_in(key, 6), position), (shards_of,), jnp.float32, smallest / len(cuts), largest / len(cuts))
        factor_of = factor_of * jnp.repeat(jnp.exp(draws), extent[position] // shards_of).reshape((-1,) + (1,) * (len(extent) - 1 - position))
    return factor_of


def scatter_about(rng, shape, scale, most, split=(), kind=jnp.bfloat16):
    level = block_levels(rng, shape, split, -0.22, 0.18) if split else 1.0
    values = jax.random.normal(rng, shape, jnp.float32) * scale * level
    return jnp.minimum(jnp.maximum(values, -most), most).astype(kind)


def setup_inputs(seed: int = 0) -> dict:
    seeds = jax.random.split(jax.random.key(seed), 10)
    return {
        "hidden": scatter_about(seeds[0], (REQS, SEQ, D), 0.3, 4.0, ((1, 128),)),
        "qkv_weight": scatter_about(seeds[1], (2, D, 3 * D), D ** -0.5, 0.109375, ((0, 2), (2, 128))),
        "out_weight": scatter_about(seeds[2], (2, D, D), D ** -0.5, 0.109375, ((0, 2), (2, 128))),
        "modulation": scatter_about(seeds[3], (2, TSTEPS, 3, D), 0.8, 3.0, ((0, 2),), jnp.float32),
        "timestep": jax.random.randint(seeds[4], (1,), 0, TSTEPS).astype(jnp.int32),
        "fresh": set_ends((jax.random.randint(seeds[5], (2, REQS, NBLOCKS), 0, 2) < 1).astype(jnp.int32), jax.random.fold_in(seeds[5], 1), 0, 1),
        "live": draw_live(jax.random.fold_in(seeds[9], 71), 0),
        "k_stale": scatter_about(seeds[7], (2, REQS, SEQ, D), 1.0, 6.0, ((0, 2), (2, 128))),
        "v_stale": scatter_about(seeds[8], (2, REQS, SEQ, D), 3.0, 16.0, ((0, 2), (2, 128))),
    }


def one_layer(stream_in, qkv_w, out_w, modulate, fresh_rows, old_keys, old_values, live):
    stream = stream_in.astype(jnp.float32)
    center = lax.optimization_barrier(jnp.mean(stream, axis=-1, keepdims=True))
    variance = lax.optimization_barrier(jnp.mean((stream - center) ** 2, axis=-1, keepdims=True))
    normed = (stream - center) / jnp.sqrt(variance + 1e-06) * (1.0 + modulate[0]) + modulate[1]
    normed_b = normed.astype(jnp.bfloat16)
    projected = jnp.dot(normed_b.reshape(REQS * SEQ, D), qkv_w, preferred_element_type=jnp.float32)
    projected = projected.astype(jnp.bfloat16).reshape(REQS, SEQ, 3 * D)
    queries = projected[:, :, :D]
    new_keys = projected[:, :, D:2 * D]
    new_values = projected[:, :, 2 * D:]
    use_fresh = jnp.repeat(fresh_rows, ROWS, axis=1)[:, :, None] == 1
    keys = jnp.where(use_fresh, new_keys, old_keys)
    values = jnp.where(use_fresh, new_values, old_values)
    usable = (jnp.repeat(live, ROWS, axis=1) == 1)[:, None, :]

    def split_heads(array):
        return jnp.transpose(array.reshape(REQS, SEQ, HEADS, HEAD), (2, 0, 1, 3))

    def per_head(triple):
        q_head, k_head, v_head = triple
        scores = jnp.einsum('rid,rjd->rij', q_head.astype(jnp.float32), k_head.astype(jnp.float32), precision=lax.Precision.HIGHEST) * 0.125
        scores = jnp.where(usable, scores, -1e+30)
        top_score = lax.optimization_barrier(jnp.max(scores, axis=-1, keepdims=True))
        weights = jnp.where(usable, jnp.exp(scores - top_score), 0.0)
        total = lax.optimization_barrier(jnp.sum(weights, axis=-1, keepdims=True))
        mixed = jnp.einsum('rij,rjd->rid', weights, v_head.astype(jnp.float32), precision=lax.Precision.HIGHEST)
        return mixed / total
    attn = lax.map(per_head, (split_heads(queries), split_heads(keys), split_heads(values)))
    attn = jnp.transpose(attn, (1, 2, 0, 3)).reshape(REQS, SEQ, D).astype(jnp.bfloat16)
    mixed_out = jnp.dot(attn.reshape(REQS * SEQ, D), out_w, preferred_element_type=jnp.float32)
    mixed_out = mixed_out.astype(jnp.bfloat16).reshape(REQS, SEQ, D)
    return (stream + modulate[2] * mixed_out.astype(jnp.float32)).astype(jnp.bfloat16)

def reference(hidden, qkv_weight, out_weight, modulation, timestep, fresh, live, k_stale, v_stale):
    step_idx = timestep[0]
    first_out = one_layer(hidden, qkv_weight[0], out_weight[0], modulation[0, step_idx], fresh[0], k_stale[0], v_stale[0], live)
    second_out = one_layer(first_out, qkv_weight[1], out_weight[1], modulation[1, step_idx], fresh[1], k_stale[1], v_stale[1], live)
    return jnp.stack([first_out, second_out])
```

```python
import functools

import jax
import jax.numpy as jnp
from jax import lax
from jax.experimental import pallas as pl
from jax.experimental.pallas import tpu as pltpu
from jax.sharding import PartitionSpec as P

MESH = pl.DeviceIdType.MESH


def gather_kernel(n, x_ref, o_ref, send_sem, recv_sem, local_sem):
    me = lax.axis_index("blk")
    sec = lax.axis_index("section")
    barrier = pltpu.get_barrier_semaphore()

    def greet(i, carry):
        peer = lax.rem(me + 1 + i, n)
        pl.semaphore_signal(barrier, inc=1, device_id=(sec, peer), device_id_type=MESH)
        return carry

    lax.fori_loop(0, n - 1, greet, 0)
    pl.semaphore_wait(barrier, n - 1)
    local = pltpu.make_async_copy(x_ref, o_ref.at[me], local_sem)
    local.start()

    def remote(i):
        peer = lax.rem(me + 1 + i, n)
        return pltpu.make_async_remote_copy(
            src_ref=x_ref,
            dst_ref=o_ref.at[me],
            send_sem=send_sem.at[i],
            recv_sem=recv_sem.at[me],
            device_id=(sec, peer),
            device_id_type=MESH,
        )

    def send(i, carry):
        remote(i).start()
        return carry

    lax.fori_loop(0, n - 1, send, 0)

    def finish(i, carry):
        remote(i).wait_send()
        src = lax.rem(me + n - 1 - i, n)
        pltpu.make_async_remote_copy(
            src_ref=x_ref,
            dst_ref=o_ref.at[src],
            send_sem=send_sem.at[i],
            recv_sem=recv_sem.at[src],
            device_id=(sec, src),
            device_id_type=MESH,
        ).wait_recv()
        return carry

    lax.fori_loop(0, n - 1, finish, 0)
    local.wait()


def gather_blk(x, n, cid):
    return pl.pallas_call(
        functools.partial(gather_kernel, n),
        out_shape=jax.ShapeDtypeStruct((n,) + x.shape, x.dtype),
        in_specs=[pl.BlockSpec(memory_space=pl.ANY)],
        out_specs=pl.BlockSpec(memory_space=pl.ANY),
        scratch_shapes=[
            pltpu.SemaphoreType.DMA((n,)),
            pltpu.SemaphoreType.DMA((n,)),
            pltpu.SemaphoreType.DMA,
        ],
        compiler_params=pltpu.CompilerParams(collective_id=cid, has_side_effects=True),
    )(x)


def gather_rows(x, cid):
    n = lax.axis_size("blk")
    _, rows, width = x.shape
    return gather_blk(x[0], n, cid).reshape(1, n * rows, width)


def from_behind(shard, axis, by):
    count = lax.axis_size(axis)
    pairs = [(i, i + by) for i in range(count) if 0 <= i + by < count]
    return lax.ppermute(shard, axis, pairs)


def attend(layer_in, qkv_cols, out_cols, modulate, fresh_own, old_keys, old_values, live):
    stream = layer_in.astype(jnp.float32)
    center = jnp.mean(stream, axis=-1, keepdims=True)
    variance = jnp.mean((stream - center) ** 2, axis=-1, keepdims=True)
    normed = (stream - center) / jnp.sqrt(variance + 1e-06) * (1.0 + modulate[0]) + modulate[1]
    normed_b = normed.astype(jnp.bfloat16)
    columns = jnp.einsum(
        "rnd,dc->rnc",
        gather_rows(normed_b, 0),
        qkv_cols,
        preferred_element_type=jnp.float32,
    ).astype(jnp.bfloat16)
    projected = lax.all_to_all(columns, "blk", split_axis=1, concat_axis=2, tiled=True)
    num_req, num_rows, width = layer_in.shape
    queries = projected[:, :, :width]
    new_keys = projected[:, :, width : 2 * width]
    new_values = projected[:, :, 2 * width :]
    use_fresh = (fresh_own == 1)[:, None, None]
    keys = jnp.where(use_fresh, new_keys, old_keys)
    values = jnp.where(use_fresh, new_values, old_values)
    num_heads = width // 64
    num_blocks = live.shape[1]
    q_heads = queries.reshape(num_req, num_rows, num_heads, 64)
    live_float = live.astype(jnp.float32)
    run_max = jnp.full((num_req, num_heads, num_rows), -1e30, jnp.float32)
    kv_piece = gather_rows(jnp.concatenate([keys, values], axis=2), 1)
    key_piece = kv_piece[:, :, :width]
    value_piece = kv_piece[:, :, width:]
    piece_rows = key_piece.shape[1]
    key_heads = key_piece.reshape(num_req, piece_rows, num_heads, 64)
    value_heads = value_piece.reshape(num_req, piece_rows, num_heads, 64)
    scores = (
        jnp.einsum("qrhd,qnhd->qhrn", q_heads, key_heads, preferred_element_type=jnp.float32)
        * 0.125
    )
    block_ids = jnp.arange(piece_rows) // num_rows
    one_hot = (block_ids[:, None] == jnp.arange(num_blocks)[None, :]).astype(jnp.float32)
    usable = jnp.einsum("qb,nb->qn", live_float, one_hot) > 0.5
    usable = usable[:, None, None, :]
    scores = jnp.where(usable, scores, -1e30)
    new_max = jnp.maximum(run_max, jnp.max(scores, axis=-1))
    weights = jnp.where(usable, jnp.exp(scores - new_max[..., None]), 0.0)
    new_sum = jnp.sum(weights, axis=-1)
    new_acc = jnp.einsum(
        "qhrn,qnhd->qhrd", weights, value_heads.astype(jnp.float32), precision=lax.Precision.HIGHEST
    )
    attn = new_acc / new_sum[..., None]
    attn = jnp.transpose(attn, (0, 2, 1, 3)).reshape(num_req, num_rows, width).astype(jnp.bfloat16)
    out_part = jnp.einsum(
        "rnd,dc->rnc",
        gather_rows(attn, 0),
        out_cols,
        preferred_element_type=jnp.float32,
    ).astype(jnp.bfloat16)
    mixed_back = lax.all_to_all(out_part, "blk", split_axis=1, concat_axis=2, tiled=True)
    return (stream + modulate[2] * mixed_back.astype(jnp.float32)).astype(jnp.bfloat16)


def pick_request(array, req_idx):
    return lax.dynamic_index_in_dim(array, req_idx, 0, keepdims=True)


def per_device(hidden, qkv_weight, out_weight, modulation, timestep, fresh, live, k_stale, v_stale):
    section_idx = lax.axis_index("section")
    block_idx = lax.axis_index("blk")
    steps_all = modulation.shape[1]
    pick_row = (jnp.arange(steps_all) == timestep[0]).astype(jnp.float32)
    modulate = jnp.einsum("t,tcd->cd", pick_row, modulation[0], precision=lax.Precision.HIGHEST)
    num_blocks = fresh.shape[2]
    own_column = (jnp.arange(num_blocks) == block_idx).astype(jnp.int32)
    fresh_own = jnp.sum(fresh[0] * own_column[None, :], axis=1)
    qkv_cols = qkv_weight[0]
    out_cols = out_weight[0]
    old_keys = k_stale[0]
    old_values = v_stale[0]
    num_req = hidden.shape[0]
    received = jnp.zeros_like(hidden[0:1])
    first_out = []
    second_out = []
    for tick_idx in range(num_req + 1):
        if tick_idx < num_req:
            own_input = hidden[tick_idx : tick_idx + 1]
        else:
            own_input = jnp.zeros_like(hidden[0:1])
        layer_in = jnp.where(section_idx == 0, own_input, received)
        req_idx = jnp.clip(tick_idx - section_idx, 0, num_req - 1)
        layer_out = attend(
            layer_in,
            qkv_cols,
            out_cols,
            modulate,
            pick_request(fresh_own, req_idx),
            pick_request(old_keys, req_idx),
            pick_request(old_values, req_idx),
            pick_request(live, req_idx),
        )
        if tick_idx < num_req:
            first_out.append(layer_out)
            received = from_behind(layer_out, "section", 1)
        if tick_idx >= 1:
            second_out.append(layer_out)
    result = jnp.where(
        section_idx == 0, jnp.concatenate(first_out, axis=0), jnp.concatenate(second_out, axis=0)
    )
    return result[None]


def solution(mesh):
    return jax.shard_map(
        per_device,
        mesh=mesh,
        in_specs=(
            P(None, "blk", None),
            P("section", None, "blk"),
            P("section", None, "blk"),
            P("section", None, None, None),
            P(),
            P("section", None, None),
            P(),
            P("section", None, "blk", None),
            P("section", None, "blk", None),
        ),
        out_specs=P("section", None, "blk", None),
        check_vma=False,
    )
```

```python
import functools

import jax
import jax.numpy as jnp
from jax import lax
from jax.experimental import pallas as pl
from jax.experimental.pallas import tpu as pltpu
from jax.sharding import PartitionSpec as P

MESH = pl.DeviceIdType.MESH


def gather_kernel(n, x_ref, o_ref, send_sem, recv_sem, local_sem):
    me = lax.axis_index("blk")
    sec = lax.axis_index("section")
    barrier = pltpu.get_barrier_semaphore()

    def greet(i, carry):
        peer = lax.rem(me + 1 + i, n)
        pl.semaphore_signal(barrier, inc=1, device_id=(sec, peer), device_id_type=MESH)
        return carry

    lax.fori_loop(0, n - 1, greet, 0)
    pl.semaphore_wait(barrier, n - 1)
    local = pltpu.make_async_copy(x_ref, o_ref.at[me], local_sem)
    local.start()

    def remote(i):
        peer = lax.rem(me + 1 + i, n)
        return pltpu.make_async_remote_copy(
            src_ref=x_ref,
            dst_ref=o_ref.at[me],
            send_sem=send_sem.at[i],
            recv_sem=recv_sem.at[me],
            device_id=(sec, peer),
            device_id_type=MESH,
        )

    def send(i, carry):
        remote(i).start()
        return carry

    lax.fori_loop(0, n - 1, send, 0)

    def finish(i, carry):
        remote(i).wait_send()
        src = lax.rem(me + n - 1 - i, n)
        pltpu.make_async_remote_copy(
            src_ref=x_ref,
            dst_ref=o_ref.at[src],
            send_sem=send_sem.at[i],
            recv_sem=recv_sem.at[src],
            device_id=(sec, src),
            device_id_type=MESH,
        ).wait_recv()
        return carry

    lax.fori_loop(0, n - 1, finish, 0)
    local.wait()


def gather_blk(x, n, cid):
    return pl.pallas_call(
        functools.partial(gather_kernel, n),
        out_shape=jax.ShapeDtypeStruct((n,) + x.shape, x.dtype),
        in_specs=[pl.BlockSpec(memory_space=pl.ANY)],
        out_specs=pl.BlockSpec(memory_space=pl.ANY),
        scratch_shapes=[
            pltpu.SemaphoreType.DMA((n,)),
            pltpu.SemaphoreType.DMA((n,)),
            pltpu.SemaphoreType.DMA,
        ],
        compiler_params=pltpu.CompilerParams(collective_id=cid, has_side_effects=True),
    )(x)


def gather_rows(x, cid):
    n = lax.axis_size("blk")
    _, rows, width = x.shape
    size = rows * width
    tile = 16 * 128
    padded = -(-size // tile) * tile
    flat = jnp.pad(x.reshape(size), (0, padded - size)).reshape(padded // 128, 128)
    out = gather_blk(flat, n, cid).reshape(n, padded)[:, :size]
    return out.reshape(1, n * rows, width)


def from_behind(shard, axis, by):
    count = lax.axis_size(axis)
    pairs = [(i, i + by) for i in range(count) if 0 <= i + by < count]
    return lax.ppermute(shard, axis, pairs)


def attend(layer_in, qkv_cols, out_cols, modulate, fresh_own, old_keys, old_values, live):
    stream = layer_in.astype(jnp.float32)
    center = jnp.mean(stream, axis=-1, keepdims=True)
    variance = jnp.mean((stream - center) ** 2, axis=-1, keepdims=True)
    normed = (stream - center) / jnp.sqrt(variance + 1e-06) * (1.0 + modulate[0]) + modulate[1]
    normed_b = normed.astype(jnp.bfloat16)
    columns = jnp.einsum(
        "rnd,dc->rnc",
        gather_rows(normed_b, 0),
        qkv_cols,
        preferred_element_type=jnp.float32,
    ).astype(jnp.bfloat16)
    projected = lax.all_to_all(columns, "blk", split_axis=1, concat_axis=2, tiled=True)
    num_req, num_rows, width = layer_in.shape
    queries = projected[:, :, :width]
    new_keys = projected[:, :, width : 2 * width]
    new_values = projected[:, :, 2 * width :]
    use_fresh = (fresh_own == 1)[:, None, None]
    keys = jnp.where(use_fresh, new_keys, old_keys)
    values = jnp.where(use_fresh, new_values, old_values)
    num_heads = width // 64
    num_blocks = live.shape[1]
    q_heads = queries.reshape(num_req, num_rows, num_heads, 64)
    live_float = live.astype(jnp.float32)
    run_max = jnp.full((num_req, num_heads, num_rows), -1e30, jnp.float32)
    kv_piece = gather_rows(jnp.concatenate([keys, values], axis=2), 1)
    key_piece = kv_piece[:, :, :width]
    value_piece = kv_piece[:, :, width:]
    piece_rows = key_piece.shape[1]
    key_heads = key_piece.reshape(num_req, piece_rows, num_heads, 64)
    value_heads = value_piece.reshape(num_req, piece_rows, num_heads, 64)
    scores = (
        jnp.einsum("qrhd,qnhd->qhrn", q_heads, key_heads, preferred_element_type=jnp.float32)
        * 0.125
    )
    block_ids = jnp.arange(piece_rows) // num_rows
    one_hot = (block_ids[:, None] == jnp.arange(num_blocks)[None, :]).astype(jnp.float32)
    usable = jnp.einsum("qb,nb->qn", live_float, one_hot) > 0.5
    usable = usable[:, None, None, :]
    scores = jnp.where(usable, scores, -1e30)
    new_max = jnp.maximum(run_max, jnp.max(scores, axis=-1))
    weights = jnp.where(usable, jnp.exp(scores - new_max[..., None]), 0.0)
    new_sum = jnp.sum(weights, axis=-1)
    new_acc = jnp.einsum(
        "qhrn,qnhd->qhrd", weights, value_heads.astype(jnp.float32), precision=lax.Precision.HIGHEST
    )
    attn = new_acc / new_sum[..., None]
    attn = jnp.transpose(attn, (0, 2, 1, 3)).reshape(num_req, num_rows, width).astype(jnp.bfloat16)
    out_part = jnp.einsum(
        "rnd,dc->rnc",
        gather_rows(attn, 0),
        out_cols,
        preferred_element_type=jnp.float32,
    ).astype(jnp.bfloat16)
    mixed_back = lax.all_to_all(out_part, "blk", split_axis=1, concat_axis=2, tiled=True)
    return (stream + modulate[2] * mixed_back.astype(jnp.float32)).astype(jnp.bfloat16)


def pick_request(array, req_idx):
    return lax.dynamic_index_in_dim(array, req_idx, 0, keepdims=True)


def per_device(hidden, qkv_weight, out_weight, modulation, timestep, fresh, live, k_stale, v_stale):
    section_idx = lax.axis_index("section")
    block_idx = lax.axis_index("blk")
    steps_all = modulation.shape[1]
    pick_row = (jnp.arange(steps_all) == timestep[0]).astype(jnp.float32)
    modulate = jnp.einsum("t,tcd->cd", pick_row, modulation[0], precision=lax.Precision.HIGHEST)
    num_blocks = fresh.shape[2]
    own_column = (jnp.arange(num_blocks) == block_idx).astype(jnp.int32)
    fresh_own = jnp.sum(fresh[0] * own_column[None, :], axis=1)
    qkv_cols = qkv_weight[0]
    out_cols = out_weight[0]
    old_keys = k_stale[0]
    old_values = v_stale[0]
    num_req = hidden.shape[0]
    received = jnp.zeros_like(hidden[0:1])
    first_out = []
    second_out = []
    for tick_idx in range(num_req + 1):
        if tick_idx < num_req:
            own_input = hidden[tick_idx : tick_idx + 1]
        else:
            own_input = jnp.zeros_like(hidden[0:1])
        layer_in = jnp.where(section_idx == 0, own_input, received)
        req_idx = jnp.clip(tick_idx - section_idx, 0, num_req - 1)
        layer_out = attend(
            layer_in,
            qkv_cols,
            out_cols,
            modulate,
            pick_request(fresh_own, req_idx),
            pick_request(old_keys, req_idx),
            pick_request(old_values, req_idx),
            pick_request(live, req_idx),
        )
        if tick_idx < num_req:
            first_out.append(layer_out)
            received = from_behind(layer_out, "section", 1)
        if tick_idx >= 1:
            second_out.append(layer_out)
    result = jnp.where(
        section_idx == 0, jnp.concatenate(first_out, axis=0), jnp.concatenate(second_out, axis=0)
    )
    return result[None]


def solution(mesh):
    return jax.shard_map(
        per_device,
        mesh=mesh,
        in_specs=(
            P(None, "blk", None),
            P("section", None, "blk"),
            P("section", None, "blk"),
            P("section", None, None, None),
            P(),
            P("section", None, None),
            P(),
            P("section", None, "blk", None),
            P("section", None, "blk", None),
        ),
        out_specs=P("section", None, "blk", None),
        check_vma=False,
    )
```

```python
import functools

import jax
import jax.numpy as jnp
from jax import lax
from jax.experimental import pallas as pl
from jax.experimental.pallas import tpu as pltpu
from jax.sharding import PartitionSpec as P

MESH = pl.DeviceIdType.MESH


def gather_kernel(n, active, x_ref, o_ref, send_sem, recv_sem, local_sem):
    sec = lax.axis_index("section")
    if active is None:
        gather_body(n, sec, x_ref, o_ref, send_sem, recv_sem, local_sem)
    else:
        pl.when(sec == active)(
            lambda: gather_body(n, sec, x_ref, o_ref, send_sem, recv_sem, local_sem)
        )


def gather_body(n, sec, x_ref, o_ref, send_sem, recv_sem, local_sem):
    me = lax.axis_index("blk")
    barrier = pltpu.get_barrier_semaphore()

    def greet(i, carry):
        peer = lax.rem(me + 1 + i, n)
        pl.semaphore_signal(barrier, inc=1, device_id=(sec, peer), device_id_type=MESH)
        return carry

    lax.fori_loop(0, n - 1, greet, 0)
    pl.semaphore_wait(barrier, n - 1)
    local = pltpu.make_async_copy(x_ref, o_ref.at[me], local_sem)
    local.start()

    def remote(i):
        peer = lax.rem(me + 1 + i, n)
        return pltpu.make_async_remote_copy(
            src_ref=x_ref,
            dst_ref=o_ref.at[me],
            send_sem=send_sem.at[i],
            recv_sem=recv_sem.at[me],
            device_id=(sec, peer),
            device_id_type=MESH,
        )

    def send(i, carry):
        remote(i).start()
        return carry

    lax.fori_loop(0, n - 1, send, 0)

    def finish(i, carry):
        remote(i).wait_send()
        src = lax.rem(me + n - 1 - i, n)
        pltpu.make_async_remote_copy(
            src_ref=x_ref,
            dst_ref=o_ref.at[src],
            send_sem=send_sem.at[i],
            recv_sem=recv_sem.at[src],
            device_id=(sec, src),
            device_id_type=MESH,
        ).wait_recv()
        return carry

    lax.fori_loop(0, n - 1, finish, 0)
    local.wait()


def gather_blk(x, n, cid, active):
    return pl.pallas_call(
        functools.partial(gather_kernel, n, active),
        out_shape=jax.ShapeDtypeStruct((n,) + x.shape, x.dtype),
        in_specs=[pl.BlockSpec(memory_space=pl.ANY)],
        out_specs=pl.BlockSpec(memory_space=pl.ANY),
        scratch_shapes=[
            pltpu.SemaphoreType.DMA((n,)),
            pltpu.SemaphoreType.DMA((n,)),
            pltpu.SemaphoreType.DMA,
        ],
        compiler_params=pltpu.CompilerParams(collective_id=cid, has_side_effects=True),
    )(x)


def gather_rows(x, cid, active):
    n = lax.axis_size("blk")
    _, rows, width = x.shape
    size = rows * width
    tile = 16 * 128
    padded = -(-size // tile) * tile
    flat = jnp.pad(x.reshape(size), (0, padded - size)).reshape(padded // 128, 128)
    out = gather_blk(flat, n, cid + (0 if active is None else 2 + active) * 2, active).reshape(n, padded)[:, :size]
    return out.reshape(1, n * rows, width)


def from_behind(shard, axis, by):
    count = lax.axis_size(axis)
    pairs = [(i, i + by) for i in range(count) if 0 <= i + by < count]
    return lax.ppermute(shard, axis, pairs)


def attend(layer_in, qkv_cols, out_cols, modulate, fresh_own, old_keys, old_values, live, active):
    stream = layer_in.astype(jnp.float32)
    center = jnp.mean(stream, axis=-1, keepdims=True)
    variance = jnp.mean((stream - center) ** 2, axis=-1, keepdims=True)
    normed = (stream - center) / jnp.sqrt(variance + 1e-06) * (1.0 + modulate[0]) + modulate[1]
    normed_b = normed.astype(jnp.bfloat16)
    columns = jnp.einsum(
        "rnd,dc->rnc",
        gather_rows(normed_b, 0, active),
        qkv_cols,
        preferred_element_type=jnp.float32,
    ).astype(jnp.bfloat16)
    projected = lax.all_to_all(columns, "blk", split_axis=1, concat_axis=2, tiled=True)
    num_req, num_rows, width = layer_in.shape
    queries = projected[:, :, :width]
    new_keys = projected[:, :, width : 2 * width]
    new_values = projected[:, :, 2 * width :]
    use_fresh = (fresh_own == 1)[:, None, None]
    keys = jnp.where(use_fresh, new_keys, old_keys)
    values = jnp.where(use_fresh, new_values, old_values)
    num_heads = width // 64
    num_blocks = live.shape[1]
    q_heads = queries.reshape(num_req, num_rows, num_heads, 64)
    live_float = live.astype(jnp.float32)
    run_max = jnp.full((num_req, num_heads, num_rows), -1e30, jnp.float32)
    kv_piece = gather_rows(jnp.concatenate([keys, values], axis=2), 1, active)
    key_piece = kv_piece[:, :, :width]
    value_piece = kv_piece[:, :, width:]
    piece_rows = key_piece.shape[1]
    key_heads = key_piece.reshape(num_req, piece_rows, num_heads, 64)
    value_heads = value_piece.reshape(num_req, piece_rows, num_heads, 64)
    scores = (
        jnp.einsum("qrhd,qnhd->qhrn", q_heads, key_heads, preferred_element_type=jnp.float32)
        * 0.125
    )
    block_ids = jnp.arange(piece_rows) // num_rows
    one_hot = (block_ids[:, None] == jnp.arange(num_blocks)[None, :]).astype(jnp.float32)
    usable = jnp.einsum("qb,nb->qn", live_float, one_hot) > 0.5
    usable = usable[:, None, None, :]
    scores = jnp.where(usable, scores, -1e30)
    new_max = jnp.maximum(run_max, jnp.max(scores, axis=-1))
    weights = jnp.where(usable, jnp.exp(scores - new_max[..., None]), 0.0)
    new_sum = jnp.sum(weights, axis=-1)
    new_acc = jnp.einsum(
        "qhrn,qnhd->qhrd", weights, value_heads.astype(jnp.float32), precision=lax.Precision.HIGHEST
    )
    attn = new_acc / new_sum[..., None]
    attn = jnp.transpose(attn, (0, 2, 1, 3)).reshape(num_req, num_rows, width).astype(jnp.bfloat16)
    out_part = jnp.einsum(
        "rnd,dc->rnc",
        gather_rows(attn, 0, active),
        out_cols,
        preferred_element_type=jnp.float32,
    ).astype(jnp.bfloat16)
    mixed_back = lax.all_to_all(out_part, "blk", split_axis=1, concat_axis=2, tiled=True)
    return (stream + modulate[2] * mixed_back.astype(jnp.float32)).astype(jnp.bfloat16)


def pick_request(array, req_idx):
    return lax.dynamic_index_in_dim(array, req_idx, 0, keepdims=True)


def per_device(hidden, qkv_weight, out_weight, modulation, timestep, fresh, live, k_stale, v_stale):
    section_idx = lax.axis_index("section")
    block_idx = lax.axis_index("blk")
    steps_all = modulation.shape[1]
    pick_row = (jnp.arange(steps_all) == timestep[0]).astype(jnp.float32)
    modulate = jnp.einsum("t,tcd->cd", pick_row, modulation[0], precision=lax.Precision.HIGHEST)
    num_blocks = fresh.shape[2]
    own_column = (jnp.arange(num_blocks) == block_idx).astype(jnp.int32)
    fresh_own = jnp.sum(fresh[0] * own_column[None, :], axis=1)
    qkv_cols = qkv_weight[0]
    out_cols = out_weight[0]
    old_keys = k_stale[0]
    old_values = v_stale[0]
    num_req = hidden.shape[0]
    received = jnp.zeros_like(hidden[0:1])
    first_out = []
    second_out = []
    for tick_idx in range(num_req + 1):
        if tick_idx < num_req:
            own_input = hidden[tick_idx : tick_idx + 1]
        else:
            own_input = jnp.zeros_like(hidden[0:1])
        layer_in = jnp.where(section_idx == 0, own_input, received)
        req_idx = jnp.clip(tick_idx - section_idx, 0, num_req - 1)
        layer_out = attend(
            layer_in,
            qkv_cols,
            out_cols,
            modulate,
            pick_request(fresh_own, req_idx),
            pick_request(old_keys, req_idx),
            pick_request(old_values, req_idx),
            pick_request(live, req_idx),
            0 if tick_idx == 0 else (1 if tick_idx == num_req else None),
        )
        if tick_idx < num_req:
            first_out.append(layer_out)
            received = from_behind(layer_out, "section", 1)
        if tick_idx >= 1:
            second_out.append(layer_out)
    result = jnp.where(
        section_idx == 0, jnp.concatenate(first_out, axis=0), jnp.concatenate(second_out, axis=0)
    )
    return result[None]


def solution(mesh):
    return jax.shard_map(
        per_device,
        mesh=mesh,
        in_specs=(
            P(None, "blk", None),
            P("section", None, "blk"),
            P("section", None, "blk"),
            P("section", None, None, None),
            P(),
            P("section", None, None),
            P(),
            P("section", None, "blk", None),
            P("section", None, "blk", None),
        ),
        out_specs=P("section", None, "blk", None),
        check_vma=False,
    )
```

```python
import functools

import jax
import jax.numpy as jnp
from jax import lax
from jax.experimental import pallas as pl
from jax.experimental.pallas import tpu as pltpu
from jax.sharding import PartitionSpec as P

MESH = pl.DeviceIdType.MESH


PLANE = 16


def gather_kernel(n, active, x_ref, o_ref, send1, recv1, send2, recv2, local_sem):
    sec = lax.axis_index("section")
    args = (n, sec, x_ref, o_ref, send1, recv1, send2, recv2, local_sem)
    if active is None:
        gather_body(*args)
    else:
        pl.when(sec == active)(lambda: gather_body(*args))


def gather_body(n, sec, x_ref, o_ref, send1, recv1, send2, recv2, local_sem):
    nz = n // PLANE
    me = lax.axis_index("blk")
    zme = me // PLANE
    xy = me % PLANE
    barrier = pltpu.get_barrier_semaphore()

    def z_peer(i):
        return lax.rem(zme + 1 + i, nz)

    def xy_peer(i):
        return lax.rem(xy + 1 + i, PLANE)

    def greet_z(i, carry):
        pl.semaphore_signal(barrier, inc=1, device_id=(sec, z_peer(i) * PLANE + xy), device_id_type=MESH)
        return carry

    def greet_xy(i, carry):
        pl.semaphore_signal(barrier, inc=1, device_id=(sec, zme * PLANE + xy_peer(i)), device_id_type=MESH)
        return carry

    lax.fori_loop(0, nz - 1, greet_z, 0)
    lax.fori_loop(0, PLANE - 1, greet_xy, 0)
    pl.semaphore_wait(barrier, nz - 1 + PLANE - 1)

    local = pltpu.make_async_copy(x_ref, o_ref.at[xy, zme], local_sem)
    local.start()

    def copy1(i, src_z):
        return pltpu.make_async_remote_copy(
            src_ref=x_ref,
            dst_ref=o_ref.at[xy, src_z],
            send_sem=send1.at[i],
            recv_sem=recv1.at[src_z],
            device_id=(sec, z_peer(i) * PLANE + xy),
            device_id_type=MESH,
        )

    def send1_step(i, carry):
        copy1(i, zme).start()
        return carry

    lax.fori_loop(0, nz - 1, send1_step, 0)

    def finish1(i, carry):
        copy1(i, zme).wait_send()
        copy1(i, lax.rem(zme + nz - 1 - i, nz)).wait_recv()
        return carry

    lax.fori_loop(0, nz - 1, finish1, 0)
    local.wait()

    def copy2(i, src_xy):
        return pltpu.make_async_remote_copy(
            src_ref=o_ref.at[src_xy],
            dst_ref=o_ref.at[src_xy],
            send_sem=send2.at[i],
            recv_sem=recv2.at[src_xy],
            device_id=(sec, zme * PLANE + xy_peer(i)),
            device_id_type=MESH,
        )

    def send2_step(i, carry):
        copy2(i, xy).start()
        return carry

    lax.fori_loop(0, PLANE - 1, send2_step, 0)

    def finish2(i, carry):
        copy2(i, xy).wait_send()
        copy2(i, lax.rem(xy + PLANE - 1 - i, PLANE)).wait_recv()
        return carry

    lax.fori_loop(0, PLANE - 1, finish2, 0)


def gather_blk(x, n, cid, active):
    nz = n // PLANE
    out = pl.pallas_call(
        functools.partial(gather_kernel, n, active),
        out_shape=jax.ShapeDtypeStruct((PLANE, nz) + x.shape, x.dtype),
        in_specs=[pl.BlockSpec(memory_space=pl.ANY)],
        out_specs=pl.BlockSpec(memory_space=pl.ANY),
        scratch_shapes=[
            pltpu.SemaphoreType.DMA((nz,)),
            pltpu.SemaphoreType.DMA((nz,)),
            pltpu.SemaphoreType.DMA((PLANE,)),
            pltpu.SemaphoreType.DMA((PLANE,)),
            pltpu.SemaphoreType.DMA,
        ],
        compiler_params=pltpu.CompilerParams(collective_id=cid, has_side_effects=True),
    )(x)
    return jnp.swapaxes(out, 0, 1).reshape((n,) + x.shape)


def gather_rows(x, cid, active):
    n = lax.axis_size("blk")
    _, rows, width = x.shape
    size = rows * width
    tile = 16 * 128
    padded = -(-size // tile) * tile
    flat = jnp.pad(x.reshape(size), (0, padded - size)).reshape(padded // 128, 128)
    out = gather_blk(flat, n, cid + (0 if active is None else 2 + active) * 2, active).reshape(n, padded)[:, :size]
    return out.reshape(1, n * rows, width)


def from_behind(shard, axis, by):
    count = lax.axis_size(axis)
    pairs = [(i, i + by) for i in range(count) if 0 <= i + by < count]
    return lax.ppermute(shard, axis, pairs)


def attend(layer_in, qkv_cols, out_cols, modulate, fresh_own, old_keys, old_values, live, active):
    stream = layer_in.astype(jnp.float32)
    center = jnp.mean(stream, axis=-1, keepdims=True)
    variance = jnp.mean((stream - center) ** 2, axis=-1, keepdims=True)
    normed = (stream - center) / jnp.sqrt(variance + 1e-06) * (1.0 + modulate[0]) + modulate[1]
    normed_b = normed.astype(jnp.bfloat16)
    columns = jnp.einsum(
        "rnd,dc->rnc",
        gather_rows(normed_b, 0, active),
        qkv_cols,
        preferred_element_type=jnp.float32,
    ).astype(jnp.bfloat16)
    projected = lax.all_to_all(columns, "blk", split_axis=1, concat_axis=2, tiled=True)
    num_req, num_rows, width = layer_in.shape
    queries = projected[:, :, :width]
    new_keys = projected[:, :, width : 2 * width]
    new_values = projected[:, :, 2 * width :]
    use_fresh = (fresh_own == 1)[:, None, None]
    keys = jnp.where(use_fresh, new_keys, old_keys)
    values = jnp.where(use_fresh, new_values, old_values)
    num_heads = width // 64
    num_blocks = live.shape[1]
    q_heads = queries.reshape(num_req, num_rows, num_heads, 64)
    live_float = live.astype(jnp.float32)
    run_max = jnp.full((num_req, num_heads, num_rows), -1e30, jnp.float32)
    kv_piece = gather_rows(jnp.concatenate([keys, values], axis=2), 1, active)
    key_piece = kv_piece[:, :, :width]
    value_piece = kv_piece[:, :, width:]
    piece_rows = key_piece.shape[1]
    key_heads = key_piece.reshape(num_req, piece_rows, num_heads, 64)
    value_heads = value_piece.reshape(num_req, piece_rows, num_heads, 64)
    scores = (
        jnp.einsum("qrhd,qnhd->qhrn", q_heads, key_heads, preferred_element_type=jnp.float32)
        * 0.125
    )
    block_ids = jnp.arange(piece_rows) // num_rows
    one_hot = (block_ids[:, None] == jnp.arange(num_blocks)[None, :]).astype(jnp.float32)
    usable = jnp.einsum("qb,nb->qn", live_float, one_hot) > 0.5
    usable = usable[:, None, None, :]
    scores = jnp.where(usable, scores, -1e30)
    new_max = jnp.maximum(run_max, jnp.max(scores, axis=-1))
    weights = jnp.where(usable, jnp.exp(scores - new_max[..., None]), 0.0)
    new_sum = jnp.sum(weights, axis=-1)
    new_acc = jnp.einsum(
        "qhrn,qnhd->qhrd", weights, value_heads.astype(jnp.float32), precision=lax.Precision.HIGHEST
    )
    attn = new_acc / new_sum[..., None]
    attn = jnp.transpose(attn, (0, 2, 1, 3)).reshape(num_req, num_rows, width).astype(jnp.bfloat16)
    out_part = jnp.einsum(
        "rnd,dc->rnc",
        gather_rows(attn, 0, active),
        out_cols,
        preferred_element_type=jnp.float32,
    ).astype(jnp.bfloat16)
    mixed_back = lax.all_to_all(out_part, "blk", split_axis=1, concat_axis=2, tiled=True)
    return (stream + modulate[2] * mixed_back.astype(jnp.float32)).astype(jnp.bfloat16)


def pick_request(array, req_idx):
    return lax.dynamic_index_in_dim(array, req_idx, 0, keepdims=True)


def per_device(hidden, qkv_weight, out_weight, modulation, timestep, fresh, live, k_stale, v_stale):
    section_idx = lax.axis_index("section")
    block_idx = lax.axis_index("blk")
    steps_all = modulation.shape[1]
    pick_row = (jnp.arange(steps_all) == timestep[0]).astype(jnp.float32)
    modulate = jnp.einsum("t,tcd->cd", pick_row, modulation[0], precision=lax.Precision.HIGHEST)
    num_blocks = fresh.shape[2]
    own_column = (jnp.arange(num_blocks) == block_idx).astype(jnp.int32)
    fresh_own = jnp.sum(fresh[0] * own_column[None, :], axis=1)
    qkv_cols = qkv_weight[0]
    out_cols = out_weight[0]
    old_keys = k_stale[0]
    old_values = v_stale[0]
    num_req = hidden.shape[0]
    received = jnp.zeros_like(hidden[0:1])
    first_out = []
    second_out = []
    for tick_idx in range(num_req + 1):
        if tick_idx < num_req:
            own_input = hidden[tick_idx : tick_idx + 1]
        else:
            own_input = jnp.zeros_like(hidden[0:1])
        layer_in = jnp.where(section_idx == 0, own_input, received)
        req_idx = jnp.clip(tick_idx - section_idx, 0, num_req - 1)
        layer_out = attend(
            layer_in,
            qkv_cols,
            out_cols,
            modulate,
            pick_request(fresh_own, req_idx),
            pick_request(old_keys, req_idx),
            pick_request(old_values, req_idx),
            pick_request(live, req_idx),
            0 if tick_idx == 0 else (1 if tick_idx == num_req else None),
        )
        if tick_idx < num_req:
            first_out.append(layer_out)
            received = from_behind(layer_out, "section", 1)
        if tick_idx >= 1:
            second_out.append(layer_out)
    result = jnp.where(
        section_idx == 0, jnp.concatenate(first_out, axis=0), jnp.concatenate(second_out, axis=0)
    )
    return result[None]


def solution(mesh):
    return jax.shard_map(
        per_device,
        mesh=mesh,
        in_specs=(
            P(None, "blk", None),
            P("section", None, "blk"),
            P("section", None, "blk"),
            P("section", None, None, None),
            P(),
            P("section", None, None),
            P(),
            P("section", None, "blk", None),
            P("section", None, "blk", None),
        ),
        out_specs=P("section", None, "blk", None),
        check_vma=False,
    )
```

```python
import functools

import jax
import jax.numpy as jnp
from jax import lax
from jax.experimental import pallas as pl
from jax.experimental.pallas import tpu as pltpu
from jax.sharding import PartitionSpec as P

MESH = pl.DeviceIdType.MESH


PLANE = 16


def gather_kernel(n, active, x_ref, o_ref, send1, recv1, send2, recv2, local_sem):
    sec = lax.axis_index("section")
    args = (n, sec, x_ref, o_ref, send1, recv1, send2, recv2, local_sem)
    if active is None:
        gather_body(*args)
    else:
        pl.when(sec == active)(lambda: gather_body(*args))


def gather_body(n, sec, x_ref, o_ref, send1, recv1, send2, recv2, local_sem):
    nz = n // PLANE
    me = lax.axis_index("blk")
    zme = me // PLANE
    xy = me % PLANE
    barrier = pltpu.get_barrier_semaphore()

    def z_peer(i):
        return lax.rem(zme + 1 + i, nz)

    def xy_peer(i):
        return lax.rem(xy + 1 + i, PLANE)

    def greet_z(i, carry):
        pl.semaphore_signal(barrier, inc=1, device_id=(sec, z_peer(i) * PLANE + xy), device_id_type=MESH)
        return carry

    def greet_xy(i, carry):
        pl.semaphore_signal(barrier, inc=1, device_id=(sec, zme * PLANE + xy_peer(i)), device_id_type=MESH)
        return carry

    lax.fori_loop(0, nz - 1, greet_z, 0)
    lax.fori_loop(0, PLANE - 1, greet_xy, 0)
    pl.semaphore_wait(barrier, nz - 1 + PLANE - 1)

    local = pltpu.make_async_copy(x_ref, o_ref.at[xy, zme], local_sem)
    local.start()

    def copy1(i, src_z):
        return pltpu.make_async_remote_copy(
            src_ref=x_ref,
            dst_ref=o_ref.at[xy, src_z],
            send_sem=send1.at[i],
            recv_sem=recv1.at[src_z],
            device_id=(sec, z_peer(i) * PLANE + xy),
            device_id_type=MESH,
        )

    def send1_step(i, carry):
        copy1(i, zme).start()
        return carry

    lax.fori_loop(0, nz - 1, send1_step, 0)

    def finish1(i, carry):
        copy1(i, zme).wait_send()
        copy1(i, lax.rem(zme + nz - 1 - i, nz)).wait_recv()
        return carry

    lax.fori_loop(0, nz - 1, finish1, 0)
    local.wait()

    def copy2(i, src_xy):
        return pltpu.make_async_remote_copy(
            src_ref=o_ref.at[src_xy],
            dst_ref=o_ref.at[src_xy],
            send_sem=send2.at[i],
            recv_sem=recv2.at[src_xy],
            device_id=(sec, zme * PLANE + xy_peer(i)),
            device_id_type=MESH,
        )

    def send2_step(i, carry):
        copy2(i, xy).start()
        return carry

    lax.fori_loop(0, PLANE - 1, send2_step, 0)

    def finish2(i, carry):
        copy2(i, xy).wait_send()
        copy2(i, lax.rem(xy + PLANE - 1 - i, PLANE)).wait_recv()
        return carry

    lax.fori_loop(0, PLANE - 1, finish2, 0)


def gather_blk(x, n, cid, active):
    nz = n // PLANE
    out = pl.pallas_call(
        functools.partial(gather_kernel, n, active),
        out_shape=jax.ShapeDtypeStruct((PLANE, nz) + x.shape, x.dtype),
        in_specs=[pl.BlockSpec(memory_space=pl.ANY)],
        out_specs=pl.BlockSpec(memory_space=pl.ANY),
        scratch_shapes=[
            pltpu.SemaphoreType.DMA((nz,)),
            pltpu.SemaphoreType.DMA((nz,)),
            pltpu.SemaphoreType.DMA((PLANE,)),
            pltpu.SemaphoreType.DMA((PLANE,)),
            pltpu.SemaphoreType.DMA,
        ],
        compiler_params=pltpu.CompilerParams(collective_id=cid, has_side_effects=True),
    )(x)
    return jnp.swapaxes(out, 0, 1).reshape((n,) + x.shape)


def gather_rows(x, cid, active):
    n = lax.axis_size("blk")
    _, rows, width = x.shape
    size = rows * width
    tile = 16 * 128
    padded = -(-size // tile) * tile
    flat = jnp.pad(x.reshape(size), (0, padded - size)).reshape(padded // 128, 128)
    out = gather_blk(flat, n, cid + (0 if active is None else 2 + active) * 2, active).reshape(n, padded)[:, :size]
    return out.reshape(1, n * rows, width)


def from_behind(shard, axis, by):
    count = lax.axis_size(axis)
    pairs = [(i, i + by) for i in range(count) if 0 <= i + by < count]
    return lax.ppermute(shard, axis, pairs)


def attend(layer_in, qkv_cols, out_cols, modulate, fresh_own, old_keys, old_values, live, active):
    stream = layer_in.astype(jnp.float32)
    center = jnp.mean(stream, axis=-1, keepdims=True)
    variance = jnp.mean((stream - center) ** 2, axis=-1, keepdims=True)
    normed = (stream - center) / jnp.sqrt(variance + 1e-06) * (1.0 + modulate[0]) + modulate[1]
    normed_b = normed.astype(jnp.bfloat16)
    columns = jnp.einsum(
        "rnd,dc->rnc",
        gather_rows(normed_b, 0, active),
        qkv_cols,
        preferred_element_type=jnp.float32,
    ).astype(jnp.bfloat16)
    projected = lax.all_to_all(columns, "blk", split_axis=1, concat_axis=2, tiled=True)
    num_req, num_rows, width = layer_in.shape
    queries = projected[:, :, :width]
    new_keys = projected[:, :, width : 2 * width]
    new_values = projected[:, :, 2 * width :]
    use_fresh = (fresh_own == 1)[:, None, None]
    keys = jnp.where(use_fresh, new_keys, old_keys)
    values = jnp.where(use_fresh, new_values, old_values)
    num_heads = width // 64
    num_blocks = live.shape[1]
    q_heads = queries.reshape(num_req, num_rows, num_heads, 64)
    live_float = live.astype(jnp.float32)
    run_max = jnp.full((num_req, num_heads, num_rows), -1e30, jnp.float32)
    kv_piece = gather_rows(jnp.concatenate([keys, values], axis=2), 1, active)
    key_piece = kv_piece[:, :, :width]
    value_piece = kv_piece[:, :, width:]
    piece_rows = key_piece.shape[1]
    key_heads = key_piece.reshape(num_req, piece_rows, num_heads, 64)
    value_heads = value_piece.reshape(num_req, piece_rows, num_heads, 64)
    scores = (
        jnp.einsum("qrhd,qnhd->qhrn", q_heads, key_heads, preferred_element_type=jnp.float32)
        * 0.125
    )
    block_ids = jnp.arange(piece_rows) // num_rows
    one_hot = (block_ids[:, None] == jnp.arange(num_blocks)[None, :]).astype(jnp.float32)
    usable = jnp.einsum("qb,nb->qn", live_float, one_hot) > 0.5
    usable = usable[:, None, None, :]
    scores = jnp.where(usable, scores, -1e30)
    new_max = jnp.maximum(run_max, jnp.max(scores, axis=-1))
    weights = jnp.where(usable, jnp.exp(scores - new_max[..., None]), 0.0)
    new_sum = jnp.sum(weights, axis=-1)
    new_acc = jnp.einsum(
        "qhrn,qnhd->qhrd", weights, value_heads.astype(jnp.float32), precision=lax.Precision.HIGHEST
    )
    attn = new_acc / new_sum[..., None]
    attn = jnp.transpose(attn, (0, 2, 1, 3)).reshape(num_req, num_rows, width).astype(jnp.bfloat16)
    out_part = jnp.einsum(
        "rnd,dc->rnc",
        gather_rows(attn, 0, active),
        out_cols,
        preferred_element_type=jnp.float32,
    ).astype(jnp.bfloat16)
    mixed_back = lax.all_to_all(out_part, "blk", split_axis=1, concat_axis=2, tiled=True)
    return (stream + modulate[2] * mixed_back.astype(jnp.float32)).astype(jnp.bfloat16)


def swap_sections(x):
    return lax.ppermute(x, "section", [(0, 1), (1, 0)])


def per_device(hidden, qkv_weight, out_weight, modulation, timestep, fresh, live, k_stale, v_stale):
    sec = lax.axis_index("section")
    block_idx = lax.axis_index("blk")
    steps_all = modulation.shape[1]
    pick_row = (jnp.arange(steps_all) == timestep[0]).astype(jnp.float32)
    modulate_own = jnp.einsum("t,tcd->cd", pick_row, modulation[0], precision=lax.Precision.HIGHEST)
    num_blocks = fresh.shape[2]
    own_column = (jnp.arange(num_blocks) == block_idx).astype(jnp.int32)
    fresh_own = jnp.sum(fresh[0] * own_column[None, :], axis=1)
    qkv_own = qkv_weight[0]
    out_own = out_weight[0]
    stale_own = jnp.concatenate([k_stale[0], v_stale[0]], axis=2)

    qkv_other = swap_sections(qkv_own)
    out_other = swap_sections(out_own)
    modulate_other = swap_sections(modulate_own)
    fresh_other = swap_sections(fresh_own)
    stale_other = swap_sections(lax.dynamic_index_in_dim(stale_own, 1 - sec, 0, keepdims=True))

    stale_mine = lax.dynamic_index_in_dim(stale_own, sec, 0, keepdims=True)
    fresh_mine = lax.dynamic_index_in_dim(fresh_own, sec, 0, keepdims=True)
    fresh_theirs = lax.dynamic_index_in_dim(fresh_other, sec, 0, keepdims=True)
    live_mine = lax.dynamic_index_in_dim(live, sec, 0, keepdims=True)
    width = hidden.shape[2]

    layer_in = lax.dynamic_index_in_dim(hidden, sec, 0, keepdims=True)
    outs = []
    for layer in range(2):
        own = sec == layer
        stale = jnp.where(own, stale_mine, stale_other)
        layer_in = attend(
            layer_in,
            jnp.where(own, qkv_own, qkv_other),
            jnp.where(own, out_own, out_other),
            jnp.where(own, modulate_own, modulate_other),
            jnp.where(own, fresh_mine, fresh_theirs),
            stale[:, :, :width],
            stale[:, :, width:],
            live_mine,
            None,
        )
        outs.append(layer_in)
    first_req1 = lax.ppermute(outs[0], "section", [(1, 0)])
    second_req0 = lax.ppermute(outs[1], "section", [(0, 1)])
    result = jnp.where(
        sec == 0,
        jnp.concatenate([outs[0], first_req1], axis=0),
        jnp.concatenate([second_req0, outs[1]], axis=0),
    )
    return result[None]


def solution(mesh):
    return jax.shard_map(
        per_device,
        mesh=mesh,
        in_specs=(
            P(None, "blk", None),
            P("section", None, "blk"),
            P("section", None, "blk"),
            P("section", None, None, None),
            P(),
            P("section", None, None),
            P(),
            P("section", None, "blk", None),
            P("section", None, "blk", None),
        ),
        out_specs=P("section", None, "blk", None),
        check_vma=False,
    )
```

```python
import functools

import jax
import jax.numpy as jnp
from jax import lax
from jax.experimental import pallas as pl
from jax.experimental.pallas import tpu as pltpu
from jax.sharding import PartitionSpec as P

MESH = pl.DeviceIdType.MESH


PLANE = 16


def gather_kernel(n, active, x_ref, o_ref, send1, recv1, send2, recv2, local_sem):
    sec = lax.axis_index("section")
    args = (n, sec, x_ref, o_ref, send1, recv1, send2, recv2, local_sem)
    if active is None:
        gather_body(*args)
    else:
        pl.when(sec == active)(lambda: gather_body(*args))


def gather_body(n, sec, x_ref, o_ref, send1, recv1, send2, recv2, local_sem):
    nz = n // PLANE
    me = lax.axis_index("blk")
    zme = me // PLANE
    xy = me % PLANE
    barrier = pltpu.get_barrier_semaphore()

    def z_peer(i):
        return lax.rem(zme + 1 + i, nz)

    def xy_peer(i):
        return lax.rem(xy + 1 + i, PLANE)

    def greet_z(i, carry):
        pl.semaphore_signal(barrier, inc=1, device_id=(sec, z_peer(i) * PLANE + xy), device_id_type=MESH)
        return carry

    def greet_xy(i, carry):
        pl.semaphore_signal(barrier, inc=1, device_id=(sec, zme * PLANE + xy_peer(i)), device_id_type=MESH)
        return carry

    lax.fori_loop(0, nz - 1, greet_z, 0)
    lax.fori_loop(0, PLANE - 1, greet_xy, 0)
    pl.semaphore_wait(barrier, nz - 1 + PLANE - 1)

    local = pltpu.make_async_copy(x_ref, o_ref.at[xy, zme], local_sem)
    local.start()

    def copy1(i, src_z):
        return pltpu.make_async_remote_copy(
            src_ref=x_ref,
            dst_ref=o_ref.at[xy, src_z],
            send_sem=send1.at[i],
            recv_sem=recv1.at[src_z],
            device_id=(sec, z_peer(i) * PLANE + xy),
            device_id_type=MESH,
        )

    def send1_step(i, carry):
        copy1(i, zme).start()
        return carry

    lax.fori_loop(0, nz - 1, send1_step, 0)

    def finish1(i, carry):
        copy1(i, zme).wait_send()
        copy1(i, lax.rem(zme + nz - 1 - i, nz)).wait_recv()
        return carry

    lax.fori_loop(0, nz - 1, finish1, 0)
    local.wait()

    def copy2(i, src_xy):
        return pltpu.make_async_remote_copy(
            src_ref=o_ref.at[src_xy],
            dst_ref=o_ref.at[src_xy],
            send_sem=send2.at[i],
            recv_sem=recv2.at[src_xy],
            device_id=(sec, zme * PLANE + xy_peer(i)),
            device_id_type=MESH,
        )

    def send2_step(i, carry):
        copy2(i, xy).start()
        return carry

    lax.fori_loop(0, PLANE - 1, send2_step, 0)

    def finish2(i, carry):
        copy2(i, xy).wait_send()
        copy2(i, lax.rem(xy + PLANE - 1 - i, PLANE)).wait_recv()
        return carry

    lax.fori_loop(0, PLANE - 1, finish2, 0)


def gather_blk(x, n, cid, active):
    nz = n // PLANE
    out = pl.pallas_call(
        functools.partial(gather_kernel, n, active),
        out_shape=jax.ShapeDtypeStruct((PLANE, nz) + x.shape, x.dtype),
        in_specs=[pl.BlockSpec(memory_space=pl.ANY)],
        out_specs=pl.BlockSpec(memory_space=pl.ANY),
        scratch_shapes=[
            pltpu.SemaphoreType.DMA((nz,)),
            pltpu.SemaphoreType.DMA((nz,)),
            pltpu.SemaphoreType.DMA((PLANE,)),
            pltpu.SemaphoreType.DMA((PLANE,)),
            pltpu.SemaphoreType.DMA,
        ],
        compiler_params=pltpu.CompilerParams(collective_id=cid, has_side_effects=True),
    )(x)
    return jnp.swapaxes(out, 0, 1).reshape((n,) + x.shape)


def exchange_kernel(n, x_ref, o_ref, send_sem, recv_sem, local_sem):
    sec = lax.axis_index("section")
    me = lax.axis_index("blk")
    barrier = pltpu.get_barrier_semaphore()

    def greet(i, carry):
        peer = lax.rem(me + 1 + i, n)
        pl.semaphore_signal(barrier, inc=1, device_id=(sec, peer), device_id_type=MESH)
        return carry

    lax.fori_loop(0, n - 1, greet, 0)
    pl.semaphore_wait(barrier, n - 1)
    local = pltpu.make_async_copy(x_ref.at[me], o_ref.at[me], local_sem)
    local.start()

    def remote(i, dst_slot):
        peer = lax.rem(me + 1 + i, n)
        return pltpu.make_async_remote_copy(
            src_ref=x_ref.at[peer],
            dst_ref=o_ref.at[dst_slot],
            send_sem=send_sem.at[i],
            recv_sem=recv_sem.at[dst_slot],
            device_id=(sec, peer),
            device_id_type=MESH,
        )

    def send(i, carry):
        remote(i, me).start()
        return carry

    lax.fori_loop(0, n - 1, send, 0)

    def finish(i, carry):
        remote(i, me).wait_send()
        remote(i, lax.rem(me + n - 1 - i, n)).wait_recv()
        return carry

    lax.fori_loop(0, n - 1, finish, 0)
    local.wait()


def exchange_blk(x, cid):
    n = x.shape[0]
    return pl.pallas_call(
        functools.partial(exchange_kernel, n),
        out_shape=jax.ShapeDtypeStruct(x.shape, x.dtype),
        in_specs=[pl.BlockSpec(memory_space=pl.ANY)],
        out_specs=pl.BlockSpec(memory_space=pl.ANY),
        scratch_shapes=[
            pltpu.SemaphoreType.DMA((n,)),
            pltpu.SemaphoreType.DMA((n,)),
            pltpu.SemaphoreType.DMA,
        ],
        compiler_params=pltpu.CompilerParams(collective_id=cid, has_side_effects=True),
    )(x)


def cols_to_rows(columns, cid):
    n = lax.axis_size("blk")
    _, total, cols = columns.shape
    rows = total // n
    pieces = columns.reshape(n, rows, cols)
    pr = -(-rows // 16) * 16
    pc = -(-cols // 128) * 128
    pieces = jnp.pad(pieces, ((0, 0), (0, pr - rows), (0, pc - cols)))
    got = exchange_blk(pieces, cid)[:, :rows, :cols]
    return jnp.transpose(got, (1, 0, 2)).reshape(1, rows, n * cols)


def gather_rows(x, cid, active):
    n = lax.axis_size("blk")
    _, rows, width = x.shape
    size = rows * width
    tile = 16 * 128
    padded = -(-size // tile) * tile
    flat = jnp.pad(x.reshape(size), (0, padded - size)).reshape(padded // 128, 128)
    out = gather_blk(flat, n, cid + (0 if active is None else 2 + active) * 2, active).reshape(n, padded)[:, :size]
    return out.reshape(1, n * rows, width)


def from_behind(shard, axis, by):
    count = lax.axis_size(axis)
    pairs = [(i, i + by) for i in range(count) if 0 <= i + by < count]
    return lax.ppermute(shard, axis, pairs)


def attend(layer_in, qkv_cols, out_cols, modulate, fresh_own, old_keys, old_values, live, active):
    stream = layer_in.astype(jnp.float32)
    center = jnp.mean(stream, axis=-1, keepdims=True)
    variance = jnp.mean((stream - center) ** 2, axis=-1, keepdims=True)
    normed = (stream - center) / jnp.sqrt(variance + 1e-06) * (1.0 + modulate[0]) + modulate[1]
    normed_b = normed.astype(jnp.bfloat16)
    columns = jnp.einsum(
        "rnd,dc->rnc",
        gather_rows(normed_b, 0, active),
        qkv_cols,
        preferred_element_type=jnp.float32,
    ).astype(jnp.bfloat16)
    projected = cols_to_rows(columns, 8)
    num_req, num_rows, width = layer_in.shape
    queries = projected[:, :, :width]
    new_keys = projected[:, :, width : 2 * width]
    new_values = projected[:, :, 2 * width :]
    use_fresh = (fresh_own == 1)[:, None, None]
    keys = jnp.where(use_fresh, new_keys, old_keys)
    values = jnp.where(use_fresh, new_values, old_values)
    num_heads = width // 64
    num_blocks = live.shape[1]
    q_heads = queries.reshape(num_req, num_rows, num_heads, 64)
    live_float = live.astype(jnp.float32)
    run_max = jnp.full((num_req, num_heads, num_rows), -1e30, jnp.float32)
    kv_piece = gather_rows(jnp.concatenate([keys, values], axis=2), 1, active)
    key_piece = kv_piece[:, :, :width]
    value_piece = kv_piece[:, :, width:]
    piece_rows = key_piece.shape[1]
    key_heads = key_piece.reshape(num_req, piece_rows, num_heads, 64)
    value_heads = value_piece.reshape(num_req, piece_rows, num_heads, 64)
    scores = (
        jnp.einsum("qrhd,qnhd->qhrn", q_heads, key_heads, preferred_element_type=jnp.float32)
        * 0.125
    )
    block_ids = jnp.arange(piece_rows) // num_rows
    one_hot = (block_ids[:, None] == jnp.arange(num_blocks)[None, :]).astype(jnp.float32)
    usable = jnp.einsum("qb,nb->qn", live_float, one_hot) > 0.5
    usable = usable[:, None, None, :]
    scores = jnp.where(usable, scores, -1e30)
    new_max = jnp.maximum(run_max, jnp.max(scores, axis=-1))
    weights = jnp.where(usable, jnp.exp(scores - new_max[..., None]), 0.0)
    new_sum = jnp.sum(weights, axis=-1)
    new_acc = jnp.einsum(
        "qhrn,qnhd->qhrd", weights, value_heads.astype(jnp.float32), precision=lax.Precision.HIGHEST
    )
    attn = new_acc / new_sum[..., None]
    attn = jnp.transpose(attn, (0, 2, 1, 3)).reshape(num_req, num_rows, width).astype(jnp.bfloat16)
    out_part = jnp.einsum(
        "rnd,dc->rnc",
        gather_rows(attn, 0, active),
        out_cols,
        preferred_element_type=jnp.float32,
    ).astype(jnp.bfloat16)
    mixed_back = cols_to_rows(out_part, 9)
    return (stream + modulate[2] * mixed_back.astype(jnp.float32)).astype(jnp.bfloat16)


def swap_sections(x):
    return lax.ppermute(x, "section", [(0, 1), (1, 0)])


def per_device(hidden, qkv_weight, out_weight, modulation, timestep, fresh, live, k_stale, v_stale):
    sec = lax.axis_index("section")
    block_idx = lax.axis_index("blk")
    steps_all = modulation.shape[1]
    pick_row = (jnp.arange(steps_all) == timestep[0]).astype(jnp.float32)
    modulate_own = jnp.einsum("t,tcd->cd", pick_row, modulation[0], precision=lax.Precision.HIGHEST)
    num_blocks = fresh.shape[2]
    own_column = (jnp.arange(num_blocks) == block_idx).astype(jnp.int32)
    fresh_own = jnp.sum(fresh[0] * own_column[None, :], axis=1)
    qkv_own = qkv_weight[0]
    out_own = out_weight[0]
    stale_own = jnp.concatenate([k_stale[0], v_stale[0]], axis=2)

    qkv_other = swap_sections(qkv_own)
    out_other = swap_sections(out_own)
    modulate_other = swap_sections(modulate_own)
    fresh_other = swap_sections(fresh_own)
    stale_other = swap_sections(lax.dynamic_index_in_dim(stale_own, 1 - sec, 0, keepdims=True))

    stale_mine = lax.dynamic_index_in_dim(stale_own, sec, 0, keepdims=True)
    fresh_mine = lax.dynamic_index_in_dim(fresh_own, sec, 0, keepdims=True)
    fresh_theirs = lax.dynamic_index_in_dim(fresh_other, sec, 0, keepdims=True)
    live_mine = lax.dynamic_index_in_dim(live, sec, 0, keepdims=True)
    width = hidden.shape[2]

    layer_in = lax.dynamic_index_in_dim(hidden, sec, 0, keepdims=True)
    outs = []
    for layer in range(2):
        own = sec == layer
        stale = jnp.where(own, stale_mine, stale_other)
        layer_in = attend(
            layer_in,
            jnp.where(own, qkv_own, qkv_other),
            jnp.where(own, out_own, out_other),
            jnp.where(own, modulate_own, modulate_other),
            jnp.where(own, fresh_mine, fresh_theirs),
            stale[:, :, :width],
            stale[:, :, width:],
            live_mine,
            None,
        )
        outs.append(layer_in)
    first_req1 = lax.ppermute(outs[0], "section", [(1, 0)])
    second_req0 = lax.ppermute(outs[1], "section", [(0, 1)])
    result = jnp.where(
        sec == 0,
        jnp.concatenate([outs[0], first_req1], axis=0),
        jnp.concatenate([second_req0, outs[1]], axis=0),
    )
    return result[None]


def solution(mesh):
    return jax.shard_map(
        per_device,
        mesh=mesh,
        in_specs=(
            P(None, "blk", None),
            P("section", None, "blk"),
            P("section", None, "blk"),
            P("section", None, None, None),
            P(),
            P("section", None, None),
            P(),
            P("section", None, "blk", None),
            P("section", None, "blk", None),
        ),
        out_specs=P("section", None, "blk", None),
        check_vma=False,
    )
```

```python
import functools

import jax
import jax.numpy as jnp
from jax import lax
from jax.experimental import pallas as pl
from jax.experimental.pallas import tpu as pltpu
from jax.sharding import PartitionSpec as P

MESH = pl.DeviceIdType.MESH


PLANE = 16


def gather_kernel(n, active, x_ref, o_ref, send1, recv1, send2, recv2, local_sem):
    sec = lax.axis_index("section")
    args = (n, sec, x_ref, o_ref, send1, recv1, send2, recv2, local_sem)
    if active is None:
        gather_body(*args)
    else:
        pl.when(sec == active)(lambda: gather_body(*args))


def gather_body(n, sec, x_ref, o_ref, send1, recv1, send2, recv2, local_sem):
    nz = n // PLANE
    me = lax.axis_index("blk")
    zme = me // PLANE
    xy = me % PLANE
    barrier = pltpu.get_barrier_semaphore()

    def z_peer(i):
        return lax.rem(zme + 1 + i, nz)

    def xy_peer(i):
        return lax.rem(xy + 1 + i, PLANE)

    def greet_z(i, carry):
        pl.semaphore_signal(barrier, inc=1, device_id=(sec, z_peer(i) * PLANE + xy), device_id_type=MESH)
        return carry

    def greet_xy(i, carry):
        pl.semaphore_signal(barrier, inc=1, device_id=(sec, zme * PLANE + xy_peer(i)), device_id_type=MESH)
        return carry

    lax.fori_loop(0, nz - 1, greet_z, 0)
    lax.fori_loop(0, PLANE - 1, greet_xy, 0)
    pl.semaphore_wait(barrier, nz - 1 + PLANE - 1)

    local = pltpu.make_async_copy(x_ref, o_ref.at[xy, zme], local_sem)
    local.start()

    def copy1(i, src_z):
        return pltpu.make_async_remote_copy(
            src_ref=x_ref,
            dst_ref=o_ref.at[xy, src_z],
            send_sem=send1.at[i],
            recv_sem=recv1.at[src_z],
            device_id=(sec, z_peer(i) * PLANE + xy),
            device_id_type=MESH,
        )

    def send1_step(i, carry):
        copy1(i, zme).start()
        return carry

    lax.fori_loop(0, nz - 1, send1_step, 0)

    def finish1(i, carry):
        copy1(i, zme).wait_send()
        copy1(i, lax.rem(zme + nz - 1 - i, nz)).wait_recv()
        return carry

    lax.fori_loop(0, nz - 1, finish1, 0)
    local.wait()

    def copy2(i, src_xy):
        return pltpu.make_async_remote_copy(
            src_ref=o_ref.at[src_xy],
            dst_ref=o_ref.at[src_xy],
            send_sem=send2.at[i],
            recv_sem=recv2.at[src_xy],
            device_id=(sec, zme * PLANE + xy_peer(i)),
            device_id_type=MESH,
        )

    def send2_step(i, carry):
        copy2(i, xy).start()
        return carry

    lax.fori_loop(0, PLANE - 1, send2_step, 0)

    def finish2(i, carry):
        copy2(i, xy).wait_send()
        copy2(i, lax.rem(xy + PLANE - 1 - i, PLANE)).wait_recv()
        return carry

    lax.fori_loop(0, PLANE - 1, finish2, 0)


def gather_blk(x, n, cid, active):
    nz = n // PLANE
    out = pl.pallas_call(
        functools.partial(gather_kernel, n, active),
        out_shape=jax.ShapeDtypeStruct((PLANE, nz) + x.shape, x.dtype),
        in_specs=[pl.BlockSpec(memory_space=pl.ANY)],
        out_specs=pl.BlockSpec(memory_space=pl.ANY),
        scratch_shapes=[
            pltpu.SemaphoreType.DMA((nz,)),
            pltpu.SemaphoreType.DMA((nz,)),
            pltpu.SemaphoreType.DMA((PLANE,)),
            pltpu.SemaphoreType.DMA((PLANE,)),
            pltpu.SemaphoreType.DMA,
        ],
        compiler_params=pltpu.CompilerParams(collective_id=cid, has_side_effects=True),
    )(x)
    return out.reshape((n,) + x.shape)


def gather_rows(x, cid, active):
    n = lax.axis_size("blk")
    _, rows, width = x.shape
    size = rows * width
    tile = 16 * 128
    padded = -(-size // tile) * tile
    flat = x.reshape(size)
    if padded != size:
        flat = jnp.pad(flat, (0, padded - size))
    flat = flat.reshape(padded // 128, 128)
    cid = cid + (0 if active is None else 2 + active) * 2
    out = gather_blk(flat, n, cid, active).reshape(n, padded)
    if padded != size:
        out = out[:, :size]
    return out.reshape(n * rows, width)


def to_blk_order(rows_in_gather_order, n):
    total, cols = rows_in_gather_order.shape
    nz = n // PLANE
    parts = rows_in_gather_order.reshape(PLANE, nz, total // n, cols)
    return jnp.swapaxes(parts, 0, 1).reshape(1, total, cols)


def blk_of_gather_slot(n):
    nz = n // PLANE
    slot = jnp.arange(n)
    return (slot % nz) * PLANE + slot // nz


def from_behind(shard, axis, by):
    count = lax.axis_size(axis)
    pairs = [(i, i + by) for i in range(count) if 0 <= i + by < count]
    return lax.ppermute(shard, axis, pairs)


def attend(layer_in, qkv_cols, out_cols, modulate, fresh_own, old_keys, old_values, live, active):
    n = lax.axis_size("blk")
    stream = layer_in.astype(jnp.float32)
    center = jnp.mean(stream, axis=-1, keepdims=True)
    variance = jnp.mean((stream - center) ** 2, axis=-1, keepdims=True)
    normed = (stream - center) / jnp.sqrt(variance + 1e-06) * (1.0 + modulate[0]) + modulate[1]
    normed_b = normed.astype(jnp.bfloat16)
    columns = jnp.dot(
        gather_rows(normed_b, 0, active), qkv_cols, preferred_element_type=jnp.float32
    ).astype(jnp.bfloat16)
    projected = lax.all_to_all(to_blk_order(columns, n), "blk", split_axis=1, concat_axis=2, tiled=True)
    num_req, num_rows, width = layer_in.shape
    queries = projected[0, :, :width]
    new_keys = projected[:, :, width : 2 * width]
    new_values = projected[:, :, 2 * width :]
    use_fresh = (fresh_own == 1)[:, None, None]
    keys = jnp.where(use_fresh, new_keys, old_keys)
    values = jnp.where(use_fresh, new_values, old_values)
    kv_all = gather_rows(jnp.concatenate([keys, values], axis=2), 1, active)
    key_all = kv_all[:, :width]
    value_all = kv_all[:, width:]
    key_blk = jnp.repeat(blk_of_gather_slot(n), num_rows)
    usable = (jnp.take(live[0], key_blk) == 1)[None, None, :]
    num_heads = width // 64
    head_of_col = jnp.arange(width) // 64
    in_head = head_of_col[None, :] == jnp.arange(num_heads)[:, None]
    q_diag = jnp.where(in_head[None], queries[:, None, :], jnp.zeros((), queries.dtype))
    scores = jnp.einsum("qhc,kc->qhk", q_diag, key_all, preferred_element_type=jnp.float32) * 0.125
    scores = jnp.where(usable, scores, -1e30)
    top = jnp.max(scores, axis=-1, keepdims=True)
    weights = jnp.where(usable, jnp.exp(scores - top), 0.0)
    total = jnp.sum(weights, axis=-1)
    mixed_all = jnp.einsum(
        "qhk,kc->qhc", weights, value_all.astype(jnp.float32), precision=lax.Precision.HIGHEST
    )
    own_head = jnp.sum(jnp.where(in_head[None], mixed_all, 0.0), axis=1)
    attn = (own_head / jnp.take(total, head_of_col, axis=1)).astype(jnp.bfloat16)[None]
    out_part = jnp.dot(
        gather_rows(attn, 0, active), out_cols, preferred_element_type=jnp.float32
    ).astype(jnp.bfloat16)
    mixed_back = lax.all_to_all(to_blk_order(out_part, n), "blk", split_axis=1, concat_axis=2, tiled=True)
    return (stream + modulate[2] * mixed_back.astype(jnp.float32)).astype(jnp.bfloat16)


def swap_sections(x):
    return lax.ppermute(x, "section", [(0, 1), (1, 0)])


def per_device(hidden, qkv_weight, out_weight, modulation, timestep, fresh, live, k_stale, v_stale):
    sec = lax.axis_index("section")
    block_idx = lax.axis_index("blk")
    steps_all = modulation.shape[1]
    pick_row = (jnp.arange(steps_all) == timestep[0]).astype(jnp.float32)
    modulate_own = jnp.einsum("t,tcd->cd", pick_row, modulation[0], precision=lax.Precision.HIGHEST)
    num_blocks = fresh.shape[2]
    own_column = (jnp.arange(num_blocks) == block_idx).astype(jnp.int32)
    fresh_own = jnp.sum(fresh[0] * own_column[None, :], axis=1)
    qkv_own = qkv_weight[0]
    out_own = out_weight[0]
    stale_own = jnp.concatenate([k_stale[0], v_stale[0]], axis=2)

    qkv_other = swap_sections(qkv_own)
    out_other = swap_sections(out_own)
    modulate_other = swap_sections(modulate_own)
    fresh_other = swap_sections(fresh_own)
    stale_other = swap_sections(lax.dynamic_index_in_dim(stale_own, 1 - sec, 0, keepdims=True))

    stale_mine = lax.dynamic_index_in_dim(stale_own, sec, 0, keepdims=True)
    fresh_mine = lax.dynamic_index_in_dim(fresh_own, sec, 0, keepdims=True)
    fresh_theirs = lax.dynamic_index_in_dim(fresh_other, sec, 0, keepdims=True)
    live_mine = lax.dynamic_index_in_dim(live, sec, 0, keepdims=True)
    width = hidden.shape[2]

    layer_in = lax.dynamic_index_in_dim(hidden, sec, 0, keepdims=True)
    outs = []
    for layer in range(2):
        own = sec == layer
        stale = jnp.where(own, stale_mine, stale_other)
        layer_in = attend(
            layer_in,
            jnp.where(own, qkv_own, qkv_other),
            jnp.where(own, out_own, out_other),
            jnp.where(own, modulate_own, modulate_other),
            jnp.where(own, fresh_mine, fresh_theirs),
            stale[:, :, :width],
            stale[:, :, width:],
            live_mine,
            None,
        )
        outs.append(layer_in)
    first_req1 = lax.ppermute(outs[0], "section", [(1, 0)])
    second_req0 = lax.ppermute(outs[1], "section", [(0, 1)])
    result = jnp.where(
        sec == 0,
        jnp.concatenate([outs[0], first_req1], axis=0),
        jnp.concatenate([second_req0, outs[1]], axis=0),
    )
    return result[None]


def solution(mesh):
    return jax.shard_map(
        per_device,
        mesh=mesh,
        in_specs=(
            P(None, "blk", None),
            P("section", None, "blk"),
            P("section", None, "blk"),
            P("section", None, None, None),
            P(),
            P("section", None, None),
            P(),
            P("section", None, "blk", None),
            P("section", None, "blk", None),
        ),
        out_specs=P("section", None, "blk", None),
        check_vma=False,
    )
```

```python
import functools

import jax
import jax.numpy as jnp
from jax import lax
from jax.experimental import pallas as pl
from jax.experimental.pallas import tpu as pltpu
from jax.sharding import PartitionSpec as P

MESH = pl.DeviceIdType.MESH


PLANE = 16


def gather_kernel(n, active, x_ref, o_ref, send1, recv1, send2, recv2, local_sem):
    sec = lax.axis_index("section")
    args = (n, sec, x_ref, o_ref, send1, recv1, send2, recv2, local_sem)
    if active is None:
        gather_body(*args)
    else:
        pl.when(sec == active)(lambda: gather_body(*args))


def gather_body(n, sec, x_ref, o_ref, send1, recv1, send2, recv2, local_sem):
    nz = n // PLANE
    me = lax.axis_index("blk")
    zme = me // PLANE
    xy = me % PLANE
    barrier = pltpu.get_barrier_semaphore()

    def z_peer(i):
        return lax.rem(zme + 1 + i, nz)

    def xy_peer(i):
        return lax.rem(xy + 1 + i, PLANE)

    def greet_z(i, carry):
        pl.semaphore_signal(barrier, inc=1, device_id=(sec, z_peer(i) * PLANE + xy), device_id_type=MESH)
        return carry

    def greet_xy(i, carry):
        pl.semaphore_signal(barrier, inc=1, device_id=(sec, zme * PLANE + xy_peer(i)), device_id_type=MESH)
        return carry

    lax.fori_loop(0, nz - 1, greet_z, 0)
    lax.fori_loop(0, PLANE - 1, greet_xy, 0)
    pl.semaphore_wait(barrier, nz - 1 + PLANE - 1)

    local = pltpu.make_async_copy(x_ref, o_ref.at[xy, zme], local_sem)
    local.start()

    def copy1(i, src_z):
        return pltpu.make_async_remote_copy(
            src_ref=x_ref,
            dst_ref=o_ref.at[xy, src_z],
            send_sem=send1.at[i],
            recv_sem=recv1.at[src_z],
            device_id=(sec, z_peer(i) * PLANE + xy),
            device_id_type=MESH,
        )

    def send1_step(i, carry):
        copy1(i, zme).start()
        return carry

    lax.fori_loop(0, nz - 1, send1_step, 0)

    def finish1(i, carry):
        copy1(i, zme).wait_send()
        copy1(i, lax.rem(zme + nz - 1 - i, nz)).wait_recv()
        return carry

    lax.fori_loop(0, nz - 1, finish1, 0)
    local.wait()

    def copy2(i, src_xy):
        return pltpu.make_async_remote_copy(
            src_ref=o_ref.at[src_xy],
            dst_ref=o_ref.at[src_xy],
            send_sem=send2.at[i],
            recv_sem=recv2.at[src_xy],
            device_id=(sec, zme * PLANE + xy_peer(i)),
            device_id_type=MESH,
        )

    def send2_step(i, carry):
        copy2(i, xy).start()
        return carry

    lax.fori_loop(0, PLANE - 1, send2_step, 0)

    def finish2(i, carry):
        copy2(i, xy).wait_send()
        copy2(i, lax.rem(xy + PLANE - 1 - i, PLANE)).wait_recv()
        return carry

    lax.fori_loop(0, PLANE - 1, finish2, 0)


def gather_blk(x, n, cid, active):
    nz = n // PLANE
    out = pl.pallas_call(
        functools.partial(gather_kernel, n, active),
        out_shape=jax.ShapeDtypeStruct((PLANE, nz) + x.shape, x.dtype),
        in_specs=[pl.BlockSpec(memory_space=pl.ANY)],
        out_specs=pl.BlockSpec(memory_space=pl.ANY),
        scratch_shapes=[
            pltpu.SemaphoreType.DMA((nz,)),
            pltpu.SemaphoreType.DMA((nz,)),
            pltpu.SemaphoreType.DMA((PLANE,)),
            pltpu.SemaphoreType.DMA((PLANE,)),
            pltpu.SemaphoreType.DMA,
        ],
        compiler_params=pltpu.CompilerParams(collective_id=cid, has_side_effects=True),
    )(x)
    return out.reshape((n,) + x.shape)


def gather_rows(x, cid, active):
    n = lax.axis_size("blk")
    _, rows, width = x.shape
    size = rows * width
    tile = 16 * 128
    padded = -(-size // tile) * tile
    flat = x.reshape(size)
    if padded != size:
        flat = jnp.pad(flat, (0, padded - size))
    flat = flat.reshape(padded // 128, 128)
    cid = cid + (0 if active is None else 2 + active) * 2
    out = gather_blk(flat, n, cid, active).reshape(n, padded)
    if padded != size:
        out = out[:, :size]
    return out.reshape(n * rows, width)


def to_blk_order(rows_in_gather_order, n):
    total, cols = rows_in_gather_order.shape
    nz = n // PLANE
    parts = rows_in_gather_order.reshape(PLANE, nz, total // n, cols)
    return jnp.swapaxes(parts, 0, 1).reshape(1, total, cols)


def from_behind(shard, axis, by):
    count = lax.axis_size(axis)
    pairs = [(i, i + by) for i in range(count) if 0 <= i + by < count]
    return lax.ppermute(shard, axis, pairs)


def attend(layer_in, qkv_cols, out_cols, modulate, fresh_own, old_keys, old_values, live, active):
    n = lax.axis_size("blk")
    stream = layer_in.astype(jnp.float32)
    center = jnp.mean(stream, axis=-1, keepdims=True)
    variance = jnp.mean((stream - center) ** 2, axis=-1, keepdims=True)
    normed = (stream - center) / jnp.sqrt(variance + 1e-06) * (1.0 + modulate[0]) + modulate[1]
    normed_b = normed.astype(jnp.bfloat16)
    columns = jnp.dot(
        gather_rows(normed_b, 0, active), qkv_cols, preferred_element_type=jnp.float32
    ).astype(jnp.bfloat16)
    projected = lax.all_to_all(to_blk_order(columns, n), "blk", split_axis=1, concat_axis=2, tiled=True)
    num_req, num_rows, width = layer_in.shape
    queries = projected[0, :, :width]
    new_keys = projected[:, :, width : 2 * width]
    new_values = projected[:, :, 2 * width :]
    use_fresh = (fresh_own == 1)[:, None, None]
    keys = jnp.where(use_fresh, new_keys, old_keys)
    values = jnp.where(use_fresh, new_values, old_values)
    kv_all = gather_rows(jnp.concatenate([keys, values], axis=2), 1, active)
    key_all = kv_all[:, :width]
    value_all = kv_all[:, width:]
    nz = n // PLANE
    live_by_slot = jnp.swapaxes(live[0].reshape(nz, PLANE), 0, 1).reshape(n)
    usable = (jnp.repeat(live_by_slot, num_rows) == 1)[None, None, :]
    num_heads = width // 64
    head_of_col = jnp.arange(width) // 64
    in_head = head_of_col[None, :] == jnp.arange(num_heads)[:, None]
    q_diag = jnp.where(in_head[None], queries[:, None, :], jnp.zeros((), queries.dtype))
    scores = jnp.einsum("qhc,kc->qhk", q_diag, key_all, preferred_element_type=jnp.float32) * 0.125
    scores = jnp.where(usable, scores, -1e30)
    top = jnp.max(scores, axis=-1, keepdims=True)
    weights = jnp.where(usable, jnp.exp(scores - top), 0.0)
    total = jnp.sum(weights, axis=-1)
    mixed_all = jnp.einsum(
        "qhk,kc->qhc", weights, value_all.astype(jnp.float32), precision=lax.Precision.HIGHEST
    )
    own_head = jnp.sum(jnp.where(in_head[None], mixed_all, 0.0), axis=1)
    total_col = jnp.broadcast_to(total[:, :, None], (num_rows, num_heads, 64)).reshape(num_rows, width)
    attn = (own_head / total_col).astype(jnp.bfloat16)[None]
    out_part = jnp.dot(
        gather_rows(attn, 0, active), out_cols, preferred_element_type=jnp.float32
    ).astype(jnp.bfloat16)
    mixed_back = lax.all_to_all(to_blk_order(out_part, n), "blk", split_axis=1, concat_axis=2, tiled=True)
    return (stream + modulate[2] * mixed_back.astype(jnp.float32)).astype(jnp.bfloat16)


def swap_sections(x):
    return lax.ppermute(x, "section", [(0, 1), (1, 0)])


def per_device(hidden, qkv_weight, out_weight, modulation, timestep, fresh, live, k_stale, v_stale):
    sec = lax.axis_index("section")
    block_idx = lax.axis_index("blk")
    steps_all = modulation.shape[1]
    pick_row = (jnp.arange(steps_all) == timestep[0]).astype(jnp.float32)
    modulate_own = jnp.einsum("t,tcd->cd", pick_row, modulation[0], precision=lax.Precision.HIGHEST)
    num_blocks = fresh.shape[2]
    own_column = (jnp.arange(num_blocks) == block_idx).astype(jnp.int32)
    fresh_own = jnp.sum(fresh[0] * own_column[None, :], axis=1)
    qkv_own = qkv_weight[0]
    out_own = out_weight[0]
    stale_own = jnp.concatenate([k_stale[0], v_stale[0]], axis=2)

    qkv_other = swap_sections(qkv_own)
    out_other = swap_sections(out_own)
    modulate_other = swap_sections(modulate_own)
    fresh_other = swap_sections(fresh_own)
    stale_other = swap_sections(lax.dynamic_index_in_dim(stale_own, 1 - sec, 0, keepdims=True))

    stale_mine = lax.dynamic_index_in_dim(stale_own, sec, 0, keepdims=True)
    fresh_mine = lax.dynamic_index_in_dim(fresh_own, sec, 0, keepdims=True)
    fresh_theirs = lax.dynamic_index_in_dim(fresh_other, sec, 0, keepdims=True)
    live_mine = lax.dynamic_index_in_dim(live, sec, 0, keepdims=True)
    width = hidden.shape[2]

    layer_in = lax.dynamic_index_in_dim(hidden, sec, 0, keepdims=True)
    outs = []
    for layer in range(2):
        own = sec == layer
        stale = jnp.where(own, stale_mine, stale_other)
        layer_in = attend(
            layer_in,
            jnp.where(own, qkv_own, qkv_other),
            jnp.where(own, out_own, out_other),
            jnp.where(own, modulate_own, modulate_other),
            jnp.where(own, fresh_mine, fresh_theirs),
            stale[:, :, :width],
            stale[:, :, width:],
            live_mine,
            None,
        )
        outs.append(layer_in)
    first_req1 = lax.ppermute(outs[0], "section", [(1, 0)])
    second_req0 = lax.ppermute(outs[1], "section", [(0, 1)])
    result = jnp.where(
        sec == 0,
        jnp.concatenate([outs[0], first_req1], axis=0),
        jnp.concatenate([second_req0, outs[1]], axis=0),
    )
    return result[None]


def solution(mesh):
    return jax.shard_map(
        per_device,
        mesh=mesh,
        in_specs=(
            P(None, "blk", None),
            P("section", None, "blk"),
            P("section", None, "blk"),
            P("section", None, None, None),
            P(),
            P("section", None, None),
            P(),
            P("section", None, "blk", None),
            P("section", None, "blk", None),
        ),
        out_specs=P("section", None, "blk", None),
        check_vma=False,
    )
```

```python
import functools

import jax
import jax.numpy as jnp
from jax import lax
from jax.experimental import pallas as pl
from jax.experimental.pallas import tpu as pltpu
from jax.sharding import PartitionSpec as P

MESH = pl.DeviceIdType.MESH


NX = 4
NY = 4
PLANE = NX * NY


def gather_kernel(n, x_ref, o_ref, zs, zr, xs, xr, ys, yr, local_sem):
    sec = lax.axis_index("section")
    nz = n // PLANE
    me = lax.axis_index("blk")
    y = me % NY
    x = (me // NY) % NX
    z = me // PLANE

    def dev(zz, xx, yy):
        return (sec, (zz * NX + xx) * NY + yy)

    xp, xm, x2 = (x + 1) % NX, (x + NX - 1) % NX, (x + 2) % NX
    yp, ym, y2 = (y + 1) % NY, (y + NY - 1) % NY, (y + 2) % NY
    barrier = pltpu.get_barrier_semaphore()

    def z_peer(i):
        return lax.rem(z + 1 + i, nz)

    def greet_z(i, carry):
        pl.semaphore_signal(barrier, inc=1, device_id=dev(z_peer(i), x, y), device_id_type=MESH)
        return carry

    lax.fori_loop(0, nz - 1, greet_z, 0)
    for target in (dev(z, xp, y), dev(z, xm, y), dev(z, x, yp), dev(z, x, ym)):
        pl.semaphore_signal(barrier, inc=1, device_id=target, device_id_type=MESH)
    pl.semaphore_wait(barrier, nz - 1 + 4)

    local = pltpu.make_async_copy(x_ref, o_ref.at[y, x, z], local_sem)
    local.start()

    def copy_z(i, src_z):
        return pltpu.make_async_remote_copy(
            src_ref=x_ref,
            dst_ref=o_ref.at[y, x, src_z],
            send_sem=zs.at[i],
            recv_sem=zr.at[src_z],
            device_id=dev(z_peer(i), x, y),
            device_id_type=MESH,
        )

    def send_z(i, carry):
        copy_z(i, z).start()
        return carry

    lax.fori_loop(0, nz - 1, send_z, 0)

    def finish_z(i, carry):
        copy_z(i, z).wait_send()
        copy_z(i, lax.rem(z + nz - 1 - i, nz)).wait_recv()
        return carry

    lax.fori_loop(0, nz - 1, finish_z, 0)
    local.wait()

    def ring(block, send_sems, recv_sems, up, down, far, count, target_up, target_down):
        def rcopy(ref, k, target):
            return pltpu.make_async_remote_copy(
                src_ref=ref, dst_ref=ref, send_sem=send_sems.at[k], recv_sem=recv_sems.at[k],
                device_id=target, device_id_type=MESH,
            )

        mine_up = rcopy(block(None), 0, target_up)
        mine_down = rcopy(block(None), 1, target_down)
        mine_up.start()
        mine_down.start()
        mine_up.wait_send()
        mine_down.wait_send()
        rcopy(block(down), 0, target_down).wait_recv()
        rcopy(block(up), 1, target_up).wait_recv()
        half = count // 2
        fwd_up = rcopy(block(down).at[pl.ds(0, half)], 2, target_up)
        fwd_down = rcopy(block(up).at[pl.ds(half, count - half)], 3, target_down)
        fwd_up.start()
        fwd_down.start()
        fwd_up.wait_send()
        fwd_down.wait_send()
        rcopy(block(far).at[pl.ds(0, half)], 2, target_down).wait_recv()
        rcopy(block(far).at[pl.ds(half, count - half)], 3, target_up).wait_recv()

    ring(lambda p: o_ref.at[y, x if p is None else p], xs, xr, xp, xm, x2, nz,
         dev(z, xp, y), dev(z, xm, y))
    ring(lambda p: o_ref.at[y if p is None else p], ys, yr, yp, ym, y2, NX,
         dev(z, x, yp), dev(z, x, ym))


def gather_blk(x, n, cid, active=None):
    nz = n // PLANE
    out = pl.pallas_call(
        functools.partial(gather_kernel, n),
        out_shape=jax.ShapeDtypeStruct((NY, NX, nz) + x.shape, x.dtype),
        in_specs=[pl.BlockSpec(memory_space=pl.ANY)],
        out_specs=pl.BlockSpec(memory_space=pl.ANY),
        scratch_shapes=[
            pltpu.SemaphoreType.DMA((nz,)),
            pltpu.SemaphoreType.DMA((nz,)),
            pltpu.SemaphoreType.DMA((4,)),
            pltpu.SemaphoreType.DMA((4,)),
            pltpu.SemaphoreType.DMA((4,)),
            pltpu.SemaphoreType.DMA((4,)),
            pltpu.SemaphoreType.DMA,
        ],
        compiler_params=pltpu.CompilerParams(collective_id=cid, has_side_effects=True),
    )(x)
    return out.reshape((n,) + x.shape)


def gather_rows(x, cid, active):
    n = lax.axis_size("blk")
    _, rows, width = x.shape
    size = rows * width
    tile = 16 * 128
    padded = -(-size // tile) * tile
    flat = x.reshape(size)
    if padded != size:
        flat = jnp.pad(flat, (0, padded - size))
    flat = flat.reshape(padded // 128, 128)
    cid = cid + (0 if active is None else 2 + active) * 2
    out = gather_blk(flat, n, cid, active).reshape(n, padded)
    if padded != size:
        out = out[:, :size]
    return out.reshape(n * rows, width)


def to_blk_order(rows_in_gather_order, n):
    total, cols = rows_in_gather_order.shape
    nz = n // PLANE
    parts = rows_in_gather_order.reshape(NY, NX, nz, total // n, cols)
    return jnp.transpose(parts, (2, 1, 0, 3, 4)).reshape(1, total, cols)


def from_behind(shard, axis, by):
    count = lax.axis_size(axis)
    pairs = [(i, i + by) for i in range(count) if 0 <= i + by < count]
    return lax.ppermute(shard, axis, pairs)


def attend(layer_in, qkv_cols, out_cols, modulate, fresh_own, old_keys, old_values, live, active):
    n = lax.axis_size("blk")
    stream = layer_in.astype(jnp.float32)
    center = jnp.mean(stream, axis=-1, keepdims=True)
    variance = jnp.mean((stream - center) ** 2, axis=-1, keepdims=True)
    normed = (stream - center) / jnp.sqrt(variance + 1e-06) * (1.0 + modulate[0]) + modulate[1]
    normed_b = normed.astype(jnp.bfloat16)
    columns = jnp.dot(
        gather_rows(normed_b, 0, active), qkv_cols, preferred_element_type=jnp.float32
    ).astype(jnp.bfloat16)
    projected = lax.all_to_all(to_blk_order(columns, n), "blk", split_axis=1, concat_axis=2, tiled=True)
    num_req, num_rows, width = layer_in.shape
    queries = projected[0, :, :width]
    new_keys = projected[:, :, width : 2 * width]
    new_values = projected[:, :, 2 * width :]
    use_fresh = (fresh_own == 1)[:, None, None]
    keys = jnp.where(use_fresh, new_keys, old_keys)
    values = jnp.where(use_fresh, new_values, old_values)
    kv_all = gather_rows(jnp.concatenate([keys, values], axis=2), 1, active)
    key_all = kv_all[:, :width]
    value_all = kv_all[:, width:]
    nz = n // PLANE
    live_by_slot = jnp.transpose(live[0].reshape(nz, NX, NY), (2, 1, 0)).reshape(n)
    usable = (jnp.repeat(live_by_slot, num_rows) == 1)[None, None, :]
    num_heads = width // 64
    head_of_col = jnp.arange(width) // 64
    in_head = head_of_col[None, :] == jnp.arange(num_heads)[:, None]
    q_diag = jnp.where(in_head[None], queries[:, None, :], jnp.zeros((), queries.dtype))
    scores = jnp.einsum("qhc,kc->qhk", q_diag, key_all, preferred_element_type=jnp.float32) * 0.125
    scores = jnp.where(usable, scores, -1e30)
    top = jnp.max(scores, axis=-1, keepdims=True)
    weights = jnp.where(usable, jnp.exp(scores - top), 0.0)
    total = jnp.sum(weights, axis=-1)
    mixed_all = jnp.einsum(
        "qhk,kc->qhc", weights, value_all.astype(jnp.float32), precision=lax.Precision.HIGHEST
    )
    own_head = jnp.sum(jnp.where(in_head[None], mixed_all, 0.0), axis=1)
    total_col = jnp.broadcast_to(total[:, :, None], (num_rows, num_heads, 64)).reshape(num_rows, width)
    attn = (own_head / total_col).astype(jnp.bfloat16)[None]
    out_part = jnp.dot(
        gather_rows(attn, 0, active), out_cols, preferred_element_type=jnp.float32
    ).astype(jnp.bfloat16)
    mixed_back = lax.all_to_all(to_blk_order(out_part, n), "blk", split_axis=1, concat_axis=2, tiled=True)
    return (stream + modulate[2] * mixed_back.astype(jnp.float32)).astype(jnp.bfloat16)


def swap_sections(x):
    return lax.ppermute(x, "section", [(0, 1), (1, 0)])


def per_device(hidden, qkv_weight, out_weight, modulation, timestep, fresh, live, k_stale, v_stale):
    sec = lax.axis_index("section")
    block_idx = lax.axis_index("blk")
    steps_all = modulation.shape[1]
    pick_row = (jnp.arange(steps_all) == timestep[0]).astype(jnp.float32)
    modulate_own = jnp.einsum("t,tcd->cd", pick_row, modulation[0], precision=lax.Precision.HIGHEST)
    num_blocks = fresh.shape[2]
    own_column = (jnp.arange(num_blocks) == block_idx).astype(jnp.int32)
    fresh_own = jnp.sum(fresh[0] * own_column[None, :], axis=1)
    qkv_own = qkv_weight[0]
    out_own = out_weight[0]
    stale_own = jnp.concatenate([k_stale[0], v_stale[0]], axis=2)

    qkv_other = swap_sections(qkv_own)
    out_other = swap_sections(out_own)
    modulate_other = swap_sections(modulate_own)
    fresh_other = swap_sections(fresh_own)
    stale_other = swap_sections(lax.dynamic_index_in_dim(stale_own, 1 - sec, 0, keepdims=True))

    stale_mine = lax.dynamic_index_in_dim(stale_own, sec, 0, keepdims=True)
    fresh_mine = lax.dynamic_index_in_dim(fresh_own, sec, 0, keepdims=True)
    fresh_theirs = lax.dynamic_index_in_dim(fresh_other, sec, 0, keepdims=True)
    live_mine = lax.dynamic_index_in_dim(live, sec, 0, keepdims=True)
    width = hidden.shape[2]

    layer_in = lax.dynamic_index_in_dim(hidden, sec, 0, keepdims=True)
    outs = []
    for layer in range(2):
        own = sec == layer
        stale = jnp.where(own, stale_mine, stale_other)
        layer_in = attend(
            layer_in,
            jnp.where(own, qkv_own, qkv_other),
            jnp.where(own, out_own, out_other),
            jnp.where(own, modulate_own, modulate_other),
            jnp.where(own, fresh_mine, fresh_theirs),
            stale[:, :, :width],
            stale[:, :, width:],
            live_mine,
            None,
        )
        outs.append(layer_in)
    first_req1 = lax.ppermute(outs[0], "section", [(1, 0)])
    second_req0 = lax.ppermute(outs[1], "section", [(0, 1)])
    result = jnp.where(
        sec == 0,
        jnp.concatenate([outs[0], first_req1], axis=0),
        jnp.concatenate([second_req0, outs[1]], axis=0),
    )
    return result[None]


def solution(mesh):
    return jax.shard_map(
        per_device,
        mesh=mesh,
        in_specs=(
            P(None, "blk", None),
            P("section", None, "blk"),
            P("section", None, "blk"),
            P("section", None, None, None),
            P(),
            P("section", None, None),
            P(),
            P("section", None, "blk", None),
            P("section", None, "blk", None),
        ),
        out_specs=P("section", None, "blk", None),
        check_vma=False,
    )
```

```python
import functools

import jax
import jax.numpy as jnp
from jax import lax
from jax.experimental import pallas as pl
from jax.experimental.pallas import tpu as pltpu
from jax.sharding import PartitionSpec as P

MESH = pl.DeviceIdType.MESH


NX = 4
NY = 4
PLANE = NX * NY


def gather_kernel(n, x_ref, oa_ref, ob_ref, zbuf, zs, zr, rs, rr, local_sem):
    sec = lax.axis_index("section")
    nz = n // PLANE
    h = nz // 2
    me = lax.axis_index("blk")
    y = me % NY
    x = (me // NY) % NX
    z = me // PLANE

    def dev(zz, xx, yy):
        return (sec, (zz * NX + xx) * NY + yy)

    xp, xm, x2 = (x + 1) % NX, (x + NX - 1) % NX, (x + 2) % NX
    yp, ym, y2 = (y + 1) % NY, (y + NY - 1) % NY, (y + 2) % NY
    barrier = pltpu.get_barrier_semaphore()

    def z_peer(i):
        return lax.rem(z + 1 + i, nz)

    def greet_z(i, carry):
        pl.semaphore_signal(barrier, inc=1, device_id=dev(z_peer(i), x, y), device_id_type=MESH)
        return carry

    lax.fori_loop(0, nz - 1, greet_z, 0)
    for target in (dev(z, xp, y), dev(z, xm, y), dev(z, x, yp), dev(z, x, ym)):
        pl.semaphore_signal(barrier, inc=1, device_id=target, device_id_type=MESH)
    pl.semaphore_wait(barrier, nz - 1 + 4)

    local = pltpu.make_async_copy(x_ref, zbuf.at[z], local_sem.at[0])
    local.start()

    def copy_z(i, src_z):
        return pltpu.make_async_remote_copy(
            src_ref=x_ref,
            dst_ref=zbuf.at[src_z],
            send_sem=zs.at[i],
            recv_sem=zr.at[src_z],
            device_id=dev(z_peer(i), x, y),
            device_id_type=MESH,
        )

    def send_z(i, carry):
        copy_z(i, z).start()
        return carry

    lax.fori_loop(0, nz - 1, send_z, 0)

    def finish_z(i, carry):
        copy_z(i, z).wait_send()
        copy_z(i, lax.rem(z + nz - 1 - i, nz)).wait_recv()
        return carry

    lax.fori_loop(0, nz - 1, finish_z, 0)
    local.wait()
    own_a = pltpu.make_async_copy(zbuf.at[pl.ds(0, h)], oa_ref.at[y, x], local_sem.at[1])
    own_b = pltpu.make_async_copy(zbuf.at[pl.ds(h, nz - h)], ob_ref.at[x, y], local_sem.at[2])
    own_a.start()
    own_b.start()

    def rcopy(stage, src, dst, k, target):
        return pltpu.make_async_remote_copy(
            src_ref=src, dst_ref=dst, send_sem=rs.at[stage, k], recv_sem=rr.at[stage, k],
            device_id=target, device_id_type=MESH,
        )

    class Ring:
        def __init__(self, stage, mine, block, up, down, far, count, target_up, target_down):
            self.stage, self.mine, self.block = stage, mine, block
            self.up, self.down, self.far, self.count = up, down, far, count
            self.target_up, self.target_down = target_up, target_down

        def step1(self):
            s, me_ref = self.stage, self.block(None)
            self.a = rcopy(s, self.mine, me_ref, 0, self.target_up)
            self.b = rcopy(s, self.mine, me_ref, 1, self.target_down)
            self.a.start()
            self.b.start()

        def wait1(self):
            s = self.stage
            self.a.wait_send()
            self.b.wait_send()
            rcopy(s, self.block(self.down), self.block(self.down), 0, self.target_down).wait_recv()
            rcopy(s, self.block(self.up), self.block(self.up), 1, self.target_up).wait_recv()

        def step2(self):
            s, half = self.stage, self.count // 2
            first = self.block(self.down).at[pl.ds(0, half)]
            second = self.block(self.up).at[pl.ds(half, self.count - half)]
            self.c = rcopy(s, first, first, 2, self.target_up)
            self.d = rcopy(s, second, second, 3, self.target_down)
            self.c.start()
            self.d.start()

        def wait2(self):
            s, half = self.stage, self.count // 2
            self.c.wait_send()
            self.d.wait_send()
            first = self.block(self.far).at[pl.ds(0, half)]
            second = self.block(self.far).at[pl.ds(half, self.count - half)]
            rcopy(s, first, first, 2, self.target_down).wait_recv()
            rcopy(s, second, second, 3, self.target_up).wait_recv()

    x_targets = (dev(z, xp, y), dev(z, xm, y))
    y_targets = (dev(z, x, yp), dev(z, x, ym))
    a_x = Ring(0, zbuf.at[pl.ds(0, h)], lambda p: oa_ref.at[y, x if p is None else p],
               xp, xm, x2, h, *x_targets)
    b_y = Ring(1, zbuf.at[pl.ds(h, nz - h)], lambda p: ob_ref.at[x, y if p is None else p],
               yp, ym, y2, nz - h, *y_targets)
    a_y = Ring(2, oa_ref.at[y], lambda p: oa_ref.at[y if p is None else p],
               yp, ym, y2, NX, *y_targets)
    b_x = Ring(3, ob_ref.at[x], lambda p: ob_ref.at[x if p is None else p],
               xp, xm, x2, NY, *x_targets)
    for first, second in ((a_x, b_y), (a_y, b_x)):
        first.step1()
        second.step1()
        first.wait1()
        second.wait1()
        first.step2()
        second.step2()
        first.wait2()
        second.wait2()
        if first is a_x:
            own_a.wait()
            own_b.wait()


def gather_blk(x, n, cid, active=None):
    nz = n // PLANE
    h = nz // 2
    oa, ob = pl.pallas_call(
        functools.partial(gather_kernel, n),
        out_shape=(
            jax.ShapeDtypeStruct((NY, NX, h) + x.shape, x.dtype),
            jax.ShapeDtypeStruct((NX, NY, nz - h) + x.shape, x.dtype),
        ),
        in_specs=[pl.BlockSpec(memory_space=pl.ANY)],
        out_specs=(pl.BlockSpec(memory_space=pl.ANY), pl.BlockSpec(memory_space=pl.ANY)),
        scratch_shapes=[
            pltpu.VMEM((nz,) + x.shape, x.dtype),
            pltpu.SemaphoreType.DMA((nz,)),
            pltpu.SemaphoreType.DMA((nz,)),
            pltpu.SemaphoreType.DMA((4, 4)),
            pltpu.SemaphoreType.DMA((4, 4)),
            pltpu.SemaphoreType.DMA((3,)),
        ],
        compiler_params=pltpu.CompilerParams(collective_id=cid, has_side_effects=True),
    )(x)
    return jnp.concatenate([oa.reshape((-1,) + x.shape), ob.reshape((-1,) + x.shape)], axis=0)


def gather_rows(x, cid, active):
    n = lax.axis_size("blk")
    _, rows, width = x.shape
    size = rows * width
    tile = 16 * 128
    padded = -(-size // tile) * tile
    flat = x.reshape(size)
    if padded != size:
        flat = jnp.pad(flat, (0, padded - size))
    flat = flat.reshape(padded // 128, 128)
    cid = cid + (0 if active is None else 2 + active) * 2
    out = gather_blk(flat, n, cid, active).reshape(n, padded)
    if padded != size:
        out = out[:, :size]
    return out.reshape(n * rows, width)


def to_blk_order(rows_in_gather_order, n):
    total, cols = rows_in_gather_order.shape
    nz = n // PLANE
    h = nz // 2
    rows = total // n
    part_a = rows_in_gather_order[: h * PLANE * rows].reshape(NY, NX, h, rows, cols)
    part_b = rows_in_gather_order[h * PLANE * rows :].reshape(NX, NY, nz - h, rows, cols)
    ordered = jnp.concatenate(
        [jnp.transpose(part_a, (2, 1, 0, 3, 4)), jnp.transpose(part_b, (2, 0, 1, 3, 4))], axis=0
    )
    return ordered.reshape(1, total, cols)


def from_behind(shard, axis, by):
    count = lax.axis_size(axis)
    pairs = [(i, i + by) for i in range(count) if 0 <= i + by < count]
    return lax.ppermute(shard, axis, pairs)


def attend(layer_in, qkv_cols, out_cols, modulate, fresh_own, old_keys, old_values, live, active):
    n = lax.axis_size("blk")
    stream = layer_in.astype(jnp.float32)
    center = jnp.mean(stream, axis=-1, keepdims=True)
    variance = jnp.mean((stream - center) ** 2, axis=-1, keepdims=True)
    normed = (stream - center) / jnp.sqrt(variance + 1e-06) * (1.0 + modulate[0]) + modulate[1]
    normed_b = normed.astype(jnp.bfloat16)
    columns = jnp.dot(
        gather_rows(normed_b, 0, active), qkv_cols, preferred_element_type=jnp.float32
    ).astype(jnp.bfloat16)
    projected = lax.all_to_all(to_blk_order(columns, n), "blk", split_axis=1, concat_axis=2, tiled=True)
    num_req, num_rows, width = layer_in.shape
    queries = projected[0, :, :width]
    new_keys = projected[:, :, width : 2 * width]
    new_values = projected[:, :, 2 * width :]
    use_fresh = (fresh_own == 1)[:, None, None]
    keys = jnp.where(use_fresh, new_keys, old_keys)
    values = jnp.where(use_fresh, new_values, old_values)
    kv_all = gather_rows(jnp.concatenate([keys, values], axis=2), 1, active)
    key_all = kv_all[:, :width]
    value_all = kv_all[:, width:]
    nz = n // PLANE
    live_zxy = live[0].reshape(nz, NX, NY)
    live_by_slot = jnp.concatenate([
        jnp.transpose(live_zxy[: nz // 2], (2, 1, 0)).reshape(-1),
        jnp.transpose(live_zxy[nz // 2 :], (1, 2, 0)).reshape(-1),
    ])
    usable = (jnp.repeat(live_by_slot, num_rows) == 1)[None, None, :]
    num_heads = width // 64
    head_of_col = jnp.arange(width) // 64
    in_head = head_of_col[None, :] == jnp.arange(num_heads)[:, None]
    q_diag = jnp.where(in_head[None], queries[:, None, :], jnp.zeros((), queries.dtype))
    scores = jnp.einsum("qhc,kc->qhk", q_diag, key_all, preferred_element_type=jnp.float32) * 0.125
    scores = jnp.where(usable, scores, -1e30)
    top = jnp.max(scores, axis=-1, keepdims=True)
    weights = jnp.where(usable, jnp.exp(scores - top), 0.0)
    total = jnp.sum(weights, axis=-1)
    mixed_all = jnp.einsum(
        "qhk,kc->qhc", weights, value_all.astype(jnp.float32), precision=lax.Precision.HIGHEST
    )
    own_head = jnp.sum(jnp.where(in_head[None], mixed_all, 0.0), axis=1)
    total_col = jnp.broadcast_to(total[:, :, None], (num_rows, num_heads, 64)).reshape(num_rows, width)
    attn = (own_head / total_col).astype(jnp.bfloat16)[None]
    out_part = jnp.dot(
        gather_rows(attn, 0, active), out_cols, preferred_element_type=jnp.float32
    ).astype(jnp.bfloat16)
    mixed_back = lax.all_to_all(to_blk_order(out_part, n), "blk", split_axis=1, concat_axis=2, tiled=True)
    return (stream + modulate[2] * mixed_back.astype(jnp.float32)).astype(jnp.bfloat16)


def swap_sections(x):
    return lax.ppermute(x, "section", [(0, 1), (1, 0)])


def per_device(hidden, qkv_weight, out_weight, modulation, timestep, fresh, live, k_stale, v_stale):
    sec = lax.axis_index("section")
    block_idx = lax.axis_index("blk")
    steps_all = modulation.shape[1]
    pick_row = (jnp.arange(steps_all) == timestep[0]).astype(jnp.float32)
    modulate_own = jnp.einsum("t,tcd->cd", pick_row, modulation[0], precision=lax.Precision.HIGHEST)
    num_blocks = fresh.shape[2]
    own_column = (jnp.arange(num_blocks) == block_idx).astype(jnp.int32)
    fresh_own = jnp.sum(fresh[0] * own_column[None, :], axis=1)
    qkv_own = qkv_weight[0]
    out_own = out_weight[0]
    stale_own = jnp.concatenate([k_stale[0], v_stale[0]], axis=2)

    qkv_other = swap_sections(qkv_own)
    out_other = swap_sections(out_own)
    modulate_other = swap_sections(modulate_own)
    fresh_other = swap_sections(fresh_own)
    stale_other = swap_sections(lax.dynamic_index_in_dim(stale_own, 1 - sec, 0, keepdims=True))

    stale_mine = lax.dynamic_index_in_dim(stale_own, sec, 0, keepdims=True)
    fresh_mine = lax.dynamic_index_in_dim(fresh_own, sec, 0, keepdims=True)
    fresh_theirs = lax.dynamic_index_in_dim(fresh_other, sec, 0, keepdims=True)
    live_mine = lax.dynamic_index_in_dim(live, sec, 0, keepdims=True)
    width = hidden.shape[2]

    layer_in = lax.dynamic_index_in_dim(hidden, sec, 0, keepdims=True)
    outs = []
    for layer in range(2):
        own = sec == layer
        stale = jnp.where(own, stale_mine, stale_other)
        layer_in = attend(
            layer_in,
            jnp.where(own, qkv_own, qkv_other),
            jnp.where(own, out_own, out_other),
            jnp.where(own, modulate_own, modulate_other),
            jnp.where(own, fresh_mine, fresh_theirs),
            stale[:, :, :width],
            stale[:, :, width:],
            live_mine,
            None,
        )
        outs.append(layer_in)
    first_req1 = lax.ppermute(outs[0], "section", [(1, 0)])
    second_req0 = lax.ppermute(outs[1], "section", [(0, 1)])
    result = jnp.where(
        sec == 0,
        jnp.concatenate([outs[0], first_req1], axis=0),
        jnp.concatenate([second_req0, outs[1]], axis=0),
    )
    return result[None]


def solution(mesh):
    return jax.shard_map(
        per_device,
        mesh=mesh,
        in_specs=(
            P(None, "blk", None),
            P("section", None, "blk"),
            P("section", None, "blk"),
            P("section", None, None, None),
            P(),
            P("section", None, None),
            P(),
            P("section", None, "blk", None),
            P("section", None, "blk", None),
        ),
        out_specs=P("section", None, "blk", None),
        check_vma=False,
    )
```

```python
import functools

import jax
import jax.numpy as jnp
from jax import lax
from jax.experimental import pallas as pl
from jax.experimental.pallas import tpu as pltpu
from jax.sharding import PartitionSpec as P

MESH = pl.DeviceIdType.MESH


NX = 4
NY = 4
PLANE = NX * NY


def gather_kernel(n, x_ref, oa_ref, ob_ref, zbuf, zs, zr, rs, rr, local_sem):
    sec = lax.axis_index("section")
    nz = n // PLANE
    h = nz // 2
    me = lax.axis_index("blk")
    y = me % NY
    x = (me // NY) % NX
    z = me // PLANE

    def dev(zz, xx, yy):
        return (sec, (zz * NX + xx) * NY + yy)

    xp, xm, x2 = (x + 1) % NX, (x + NX - 1) % NX, (x + 2) % NX
    yp, ym, y2 = (y + 1) % NY, (y + NY - 1) % NY, (y + 2) % NY
    barrier = pltpu.get_barrier_semaphore()

    def z_peer(i):
        return lax.rem(z + 1 + i, nz)

    def greet_z(i, carry):
        pl.semaphore_signal(barrier, inc=1, device_id=dev(z_peer(i), x, y), device_id_type=MESH)
        return carry

    lax.fori_loop(0, nz - 1, greet_z, 0)
    for target in (dev(z, xp, y), dev(z, xm, y), dev(z, x, yp), dev(z, x, ym)):
        pl.semaphore_signal(barrier, inc=1, device_id=target, device_id_type=MESH)
    pl.semaphore_wait(barrier, nz - 1 + 4)

    local = pltpu.make_async_copy(x_ref, zbuf.at[z], local_sem.at[0])
    local.start()

    def copy_z(i, src_z):
        return pltpu.make_async_remote_copy(
            src_ref=x_ref,
            dst_ref=zbuf.at[src_z],
            send_sem=zs.at[i],
            recv_sem=zr.at[src_z],
            device_id=dev(z_peer(i), x, y),
            device_id_type=MESH,
        )

    def send_z(i, carry):
        copy_z(i, z).start()
        return carry

    lax.fori_loop(0, nz - 1, send_z, 0)

    def finish_z(i, carry):
        copy_z(i, z).wait_send()
        copy_z(i, lax.rem(z + nz - 1 - i, nz)).wait_recv()
        return carry

    lax.fori_loop(0, nz - 1, finish_z, 0)
    local.wait()
    own_a = pltpu.make_async_copy(zbuf.at[pl.ds(0, h)], oa_ref.at[y, x], local_sem.at[1])
    own_b = pltpu.make_async_copy(zbuf.at[pl.ds(h, nz - h)], ob_ref.at[x, y], local_sem.at[2])
    own_a.start()
    own_b.start()

    def rcopy(stage, src, dst, k, target):
        return pltpu.make_async_remote_copy(
            src_ref=src, dst_ref=dst, send_sem=rs.at[stage, k], recv_sem=rr.at[stage, k],
            device_id=target, device_id_type=MESH,
        )

    class Ring:
        def __init__(self, stage, mine, block, up, down, far, count, target_up, target_down):
            self.stage, self.mine, self.block = stage, mine, block
            self.up, self.down, self.far, self.count = up, down, far, count
            self.target_up, self.target_down = target_up, target_down

        def step1(self):
            s, me_ref = self.stage, self.block(None)
            self.a = rcopy(s, self.mine, me_ref, 0, self.target_up)
            self.b = rcopy(s, self.mine, me_ref, 1, self.target_down)
            self.a.start()
            self.b.start()

        def wait1(self):
            s = self.stage
            self.a.wait_send()
            self.b.wait_send()
            rcopy(s, self.block(self.down), self.block(self.down), 0, self.target_down).wait_recv()
            rcopy(s, self.block(self.up), self.block(self.up), 1, self.target_up).wait_recv()

        def step2(self):
            s, half = self.stage, self.count // 2
            first = self.block(self.down).at[pl.ds(0, half)]
            second = self.block(self.up).at[pl.ds(half, self.count - half)]
            self.c = rcopy(s, first, first, 2, self.target_up)
            self.d = rcopy(s, second, second, 3, self.target_down)
            self.c.start()
            self.d.start()

        def wait2(self):
            s, half = self.stage, self.count // 2
            self.c.wait_send()
            self.d.wait_send()
            first = self.block(self.far).at[pl.ds(0, half)]
            second = self.block(self.far).at[pl.ds(half, self.count - half)]
            rcopy(s, first, first, 2, self.target_down).wait_recv()
            rcopy(s, second, second, 3, self.target_up).wait_recv()

    x_targets = (dev(z, xp, y), dev(z, xm, y))
    y_targets = (dev(z, x, yp), dev(z, x, ym))
    a_x = Ring(0, zbuf.at[pl.ds(0, h)], lambda p: oa_ref.at[y, x if p is None else p],
               xp, xm, x2, h, *x_targets)
    b_y = Ring(1, zbuf.at[pl.ds(h, nz - h)], lambda p: ob_ref.at[x, y if p is None else p],
               yp, ym, y2, nz - h, *y_targets)
    a_y = Ring(2, oa_ref.at[y], lambda p: oa_ref.at[y if p is None else p],
               yp, ym, y2, NX, *y_targets)
    b_x = Ring(3, ob_ref.at[x], lambda p: ob_ref.at[x if p is None else p],
               xp, xm, x2, NY, *x_targets)
    for first, second in ((a_x, b_y), (a_y, b_x)):
        first.step1()
        second.step1()
        first.wait1()
        second.wait1()
        first.step2()
        second.step2()
        first.wait2()
        second.wait2()
        if first is a_x:
            own_a.wait()
            own_b.wait()


def gather_blk(x, n, cid, active=None):
    nz = n // PLANE
    h = nz // 2
    oa, ob = pl.pallas_call(
        functools.partial(gather_kernel, n),
        out_shape=(
            jax.ShapeDtypeStruct((NY, NX, h) + x.shape, x.dtype),
            jax.ShapeDtypeStruct((NX, NY, nz - h) + x.shape, x.dtype),
        ),
        in_specs=[pl.BlockSpec(memory_space=pl.ANY)],
        out_specs=(pl.BlockSpec(memory_space=pl.ANY), pl.BlockSpec(memory_space=pl.ANY)),
        scratch_shapes=[
            pltpu.VMEM((nz,) + x.shape, x.dtype),
            pltpu.SemaphoreType.DMA((nz,)),
            pltpu.SemaphoreType.DMA((nz,)),
            pltpu.SemaphoreType.DMA((4, 4)),
            pltpu.SemaphoreType.DMA((4, 4)),
            pltpu.SemaphoreType.DMA((3,)),
        ],
        compiler_params=pltpu.CompilerParams(collective_id=cid, has_side_effects=True),
    )(x)
    return [oa.reshape((-1,) + x.shape), ob.reshape((-1,) + x.shape)]


def gather_rows(x, cid, active):
    n = lax.axis_size("blk")
    _, rows, width = x.shape
    size = rows * width
    tile = 16 * 128
    padded = -(-size // tile) * tile
    flat = x.reshape(size)
    if padded != size:
        flat = jnp.pad(flat, (0, padded - size))
    flat = flat.reshape(padded // 128, 128)
    cid = cid + (0 if active is None else 2 + active) * 2
    parts = []
    for part in gather_blk(flat, n, cid, active):
        m = part.shape[0]
        part = part.reshape(m, padded)
        if padded != size:
            part = part[:, :size]
        parts.append(part.reshape(m * rows, width))
    return parts


def dot_parts(parts, weight):
    return jnp.concatenate(
        [jnp.dot(p, weight, preferred_element_type=jnp.float32) for p in parts], axis=0
    ).astype(jnp.bfloat16)


def to_blk_order(rows_in_gather_order, n):
    total, cols = rows_in_gather_order.shape
    nz = n // PLANE
    h = nz // 2
    rows = total // n
    part_a = rows_in_gather_order[: h * PLANE * rows].reshape(NY, NX, h, rows, cols)
    part_b = rows_in_gather_order[h * PLANE * rows :].reshape(NX, NY, nz - h, rows, cols)
    ordered = jnp.concatenate(
        [jnp.transpose(part_a, (2, 1, 0, 3, 4)), jnp.transpose(part_b, (2, 0, 1, 3, 4))], axis=0
    )
    return ordered.reshape(1, total, cols)


def from_behind(shard, axis, by):
    count = lax.axis_size(axis)
    pairs = [(i, i + by) for i in range(count) if 0 <= i + by < count]
    return lax.ppermute(shard, axis, pairs)


def attend(layer_in, qkv_cols, out_cols, modulate, fresh_own, old_keys, old_values, live, active):
    n = lax.axis_size("blk")
    stream = layer_in.astype(jnp.float32)
    center = jnp.mean(stream, axis=-1, keepdims=True)
    variance = jnp.mean((stream - center) ** 2, axis=-1, keepdims=True)
    normed = (stream - center) / jnp.sqrt(variance + 1e-06) * (1.0 + modulate[0]) + modulate[1]
    normed_b = normed.astype(jnp.bfloat16)
    columns = dot_parts(gather_rows(normed_b, 0, active), qkv_cols)
    projected = lax.all_to_all(to_blk_order(columns, n), "blk", split_axis=1, concat_axis=2, tiled=True)
    num_req, num_rows, width = layer_in.shape
    queries = projected[0, :, :width]
    new_keys = projected[:, :, width : 2 * width]
    new_values = projected[:, :, 2 * width :]
    use_fresh = (fresh_own == 1)[:, None, None]
    keys = jnp.where(use_fresh, new_keys, old_keys)
    values = jnp.where(use_fresh, new_values, old_values)
    kv_parts = gather_rows(jnp.concatenate([keys, values], axis=2), 1, active)
    nz = n // PLANE
    live_zxy = live[0].reshape(nz, NX, NY)
    live_by_slot = jnp.concatenate([
        jnp.transpose(live_zxy[: nz // 2], (2, 1, 0)).reshape(-1),
        jnp.transpose(live_zxy[nz // 2 :], (1, 2, 0)).reshape(-1),
    ])
    usable = (jnp.repeat(live_by_slot, num_rows) == 1)[None, None, :]
    num_heads = width // 64
    head_of_col = jnp.arange(width) // 64
    in_head = head_of_col[None, :] == jnp.arange(num_heads)[:, None]
    q_diag = jnp.where(in_head[None], queries[:, None, :], jnp.zeros((), queries.dtype))
    scores = jnp.concatenate(
        [jnp.einsum("qhc,kc->qhk", q_diag, p[:, :width], preferred_element_type=jnp.float32) for p in kv_parts],
        axis=-1,
    ) * 0.125
    scores = jnp.where(usable, scores, -1e30)
    top = jnp.max(scores, axis=-1, keepdims=True)
    weights = jnp.where(usable, jnp.exp(scores - top), 0.0)
    total = jnp.sum(weights, axis=-1)
    split = kv_parts[0].shape[0]
    mixed_all = jnp.einsum(
        "qhk,kc->qhc", weights[..., :split], kv_parts[0][:, width:].astype(jnp.float32),
        precision=lax.Precision.HIGHEST,
    ) + jnp.einsum(
        "qhk,kc->qhc", weights[..., split:], kv_parts[1][:, width:].astype(jnp.float32),
        precision=lax.Precision.HIGHEST,
    )
    own_head = jnp.sum(jnp.where(in_head[None], mixed_all, 0.0), axis=1)
    total_col = jnp.broadcast_to(total[:, :, None], (num_rows, num_heads, 64)).reshape(num_rows, width)
    attn = (own_head / total_col).astype(jnp.bfloat16)[None]
    out_part = dot_parts(gather_rows(attn, 0, active), out_cols)
    mixed_back = lax.all_to_all(to_blk_order(out_part, n), "blk", split_axis=1, concat_axis=2, tiled=True)
    return (stream + modulate[2] * mixed_back.astype(jnp.float32)).astype(jnp.bfloat16)


def swap_sections(x):
    return lax.ppermute(x, "section", [(0, 1), (1, 0)])


def per_device(hidden, qkv_weight, out_weight, modulation, timestep, fresh, live, k_stale, v_stale):
    sec = lax.axis_index("section")
    block_idx = lax.axis_index("blk")
    steps_all = modulation.shape[1]
    pick_row = (jnp.arange(steps_all) == timestep[0]).astype(jnp.float32)
    modulate_own = jnp.einsum("t,tcd->cd", pick_row, modulation[0], precision=lax.Precision.HIGHEST)
    num_blocks = fresh.shape[2]
    own_column = (jnp.arange(num_blocks) == block_idx).astype(jnp.int32)
    fresh_own = jnp.sum(fresh[0] * own_column[None, :], axis=1)
    qkv_own = qkv_weight[0]
    out_own = out_weight[0]
    stale_own = jnp.concatenate([k_stale[0], v_stale[0]], axis=2)

    qkv_other = swap_sections(qkv_own)
    out_other = swap_sections(out_own)
    modulate_other = swap_sections(modulate_own)
    fresh_other = swap_sections(fresh_own)
    stale_other = swap_sections(lax.dynamic_index_in_dim(stale_own, 1 - sec, 0, keepdims=True))

    stale_mine = lax.dynamic_index_in_dim(stale_own, sec, 0, keepdims=True)
    fresh_mine = lax.dynamic_index_in_dim(fresh_own, sec, 0, keepdims=True)
    fresh_theirs = lax.dynamic_index_in_dim(fresh_other, sec, 0, keepdims=True)
    live_mine = lax.dynamic_index_in_dim(live, sec, 0, keepdims=True)
    width = hidden.shape[2]

    layer_in = lax.dynamic_index_in_dim(hidden, sec, 0, keepdims=True)
    outs = []
    for layer in range(2):
        own = sec == layer
        stale = jnp.where(own, stale_mine, stale_other)
        layer_in = attend(
            layer_in,
            jnp.where(own, qkv_own, qkv_other),
            jnp.where(own, out_own, out_other),
            jnp.where(own, modulate_own, modulate_other),
            jnp.where(own, fresh_mine, fresh_theirs),
            stale[:, :, :width],
            stale[:, :, width:],
            live_mine,
            None,
        )
        outs.append(layer_in)
    first_req1 = lax.ppermute(outs[0], "section", [(1, 0)])
    second_req0 = lax.ppermute(outs[1], "section", [(0, 1)])
    result = jnp.where(
        sec == 0,
        jnp.concatenate([outs[0], first_req1], axis=0),
        jnp.concatenate([second_req0, outs[1]], axis=0),
    )
    return result[None]


def solution(mesh):
    return jax.shard_map(
        per_device,
        mesh=mesh,
        in_specs=(
            P(None, "blk", None),
            P("section", None, "blk"),
            P("section", None, "blk"),
            P("section", None, None, None),
            P(),
            P("section", None, None),
            P(),
            P("section", None, "blk", None),
            P("section", None, "blk", None),
        ),
        out_specs=P("section", None, "blk", None),
        check_vma=False,
    )
```

```python
import functools

import jax
import jax.numpy as jnp
from jax import lax
from jax.experimental import pallas as pl
from jax.experimental.pallas import tpu as pltpu
from jax.sharding import PartitionSpec as P

MESH = pl.DeviceIdType.MESH


NX = 4
NY = 4
PLANE = NX * NY


def gather_kernel(n, x_ref, oa_ref, ob_ref, zbuf, zs, zr, rs, rr, local_sem):
    sec = lax.axis_index("section")
    nz = n // PLANE
    h = nz // 2
    me = lax.axis_index("blk")
    y = me % NY
    x = (me // NY) % NX
    z = me // PLANE

    def dev(zz, xx, yy):
        return (sec, (zz * NX + xx) * NY + yy)

    xp, xm, x2 = (x + 1) % NX, (x + NX - 1) % NX, (x + 2) % NX
    yp, ym, y2 = (y + 1) % NY, (y + NY - 1) % NY, (y + 2) % NY
    barrier = pltpu.get_barrier_semaphore()

    def z_peer(i):
        return lax.rem(z + 1 + i, nz)

    def greet_z(i, carry):
        pl.semaphore_signal(barrier, inc=1, device_id=dev(z_peer(i), x, y), device_id_type=MESH)
        return carry

    lax.fori_loop(0, nz - 1, greet_z, 0)
    for target in (dev(z, xp, y), dev(z, xm, y), dev(z, x, yp), dev(z, x, ym)):
        pl.semaphore_signal(barrier, inc=1, device_id=target, device_id_type=MESH)
    pl.semaphore_wait(barrier, nz - 1 + 4)

    local = pltpu.make_async_copy(x_ref, zbuf.at[z], local_sem.at[0])
    local.start()

    def copy_z(i, src_z):
        return pltpu.make_async_remote_copy(
            src_ref=x_ref,
            dst_ref=zbuf.at[src_z],
            send_sem=zs.at[i],
            recv_sem=zr.at[src_z],
            device_id=dev(z_peer(i), x, y),
            device_id_type=MESH,
        )

    def send_z(i, carry):
        copy_z(i, z).start()
        return carry

    lax.fori_loop(0, nz - 1, send_z, 0)

    def finish_z(i, carry):
        copy_z(i, z).wait_send()
        copy_z(i, lax.rem(z + nz - 1 - i, nz)).wait_recv()
        return carry

    lax.fori_loop(0, nz - 1, finish_z, 0)
    local.wait()
    own_a = pltpu.make_async_copy(zbuf.at[pl.ds(0, h)], oa_ref.at[y, x], local_sem.at[1])
    own_b = pltpu.make_async_copy(zbuf.at[pl.ds(h, nz - h)], ob_ref.at[x, y], local_sem.at[2])
    own_a.start()
    own_b.start()

    def rcopy(stage, src, dst, k, target):
        return pltpu.make_async_remote_copy(
            src_ref=src, dst_ref=dst, send_sem=rs.at[stage, k], recv_sem=rr.at[stage, k],
            device_id=target, device_id_type=MESH,
        )

    class Ring:
        def __init__(self, stage, mine, block, up, down, far, count, target_up, target_down):
            self.stage, self.mine, self.block = stage, mine, block
            self.up, self.down, self.far, self.count = up, down, far, count
            self.target_up, self.target_down = target_up, target_down

        def step1(self):
            s, me_ref = self.stage, self.block(None)
            self.a = rcopy(s, self.mine, me_ref, 0, self.target_up)
            self.b = rcopy(s, self.mine, me_ref, 1, self.target_down)
            self.a.start()
            self.b.start()

        def wait1(self):
            s = self.stage
            self.a.wait_send()
            self.b.wait_send()
            rcopy(s, self.block(self.down), self.block(self.down), 0, self.target_down).wait_recv()
            rcopy(s, self.block(self.up), self.block(self.up), 1, self.target_up).wait_recv()

        def step2(self):
            s, half = self.stage, self.count // 2
            first = self.block(self.down).at[pl.ds(0, half)]
            second = self.block(self.up).at[pl.ds(half, self.count - half)]
            self.c = rcopy(s, first, first, 2, self.target_up)
            self.d = rcopy(s, second, second, 3, self.target_down)
            self.c.start()
            self.d.start()

        def wait2(self):
            s, half = self.stage, self.count // 2
            self.c.wait_send()
            self.d.wait_send()
            first = self.block(self.far).at[pl.ds(0, half)]
            second = self.block(self.far).at[pl.ds(half, self.count - half)]
            rcopy(s, first, first, 2, self.target_down).wait_recv()
            rcopy(s, second, second, 3, self.target_up).wait_recv()

    x_targets = (dev(z, xp, y), dev(z, xm, y))
    y_targets = (dev(z, x, yp), dev(z, x, ym))
    a_x = Ring(0, zbuf.at[pl.ds(0, h)], lambda p: oa_ref.at[y, x if p is None else p],
               xp, xm, x2, h, *x_targets)
    b_y = Ring(1, zbuf.at[pl.ds(h, nz - h)], lambda p: ob_ref.at[x, y if p is None else p],
               yp, ym, y2, nz - h, *y_targets)
    a_y = Ring(2, oa_ref.at[y], lambda p: oa_ref.at[y if p is None else p],
               yp, ym, y2, NX, *y_targets)
    b_x = Ring(3, ob_ref.at[x], lambda p: ob_ref.at[x if p is None else p],
               xp, xm, x2, NY, *x_targets)
    for first, second in ((a_x, b_y), (a_y, b_x)):
        first.step1()
        second.step1()
        first.wait1()
        second.wait1()
        first.step2()
        second.step2()
        first.wait2()
        second.wait2()
        if first is a_x:
            own_a.wait()
            own_b.wait()


def gather_blk(x, n, cid, active=None):
    nz = n // PLANE
    h = nz // 2
    oa, ob = pl.pallas_call(
        functools.partial(gather_kernel, n),
        out_shape=(
            jax.ShapeDtypeStruct((NY, NX, h) + x.shape, x.dtype),
            jax.ShapeDtypeStruct((NX, NY, nz - h) + x.shape, x.dtype),
        ),
        in_specs=[pl.BlockSpec(memory_space=pl.ANY)],
        out_specs=(pl.BlockSpec(memory_space=pl.ANY), pl.BlockSpec(memory_space=pl.ANY)),
        scratch_shapes=[
            pltpu.VMEM((nz,) + x.shape, x.dtype),
            pltpu.SemaphoreType.DMA((nz,)),
            pltpu.SemaphoreType.DMA((nz,)),
            pltpu.SemaphoreType.DMA((4, 4)),
            pltpu.SemaphoreType.DMA((4, 4)),
            pltpu.SemaphoreType.DMA((3,)),
        ],
        compiler_params=pltpu.CompilerParams(collective_id=cid, has_side_effects=True),
    )(x)
    return jnp.concatenate([oa.reshape((-1,) + x.shape), ob.reshape((-1,) + x.shape)], axis=0)


def gather_rows(x, cid, active):
    n = lax.axis_size("blk")
    _, rows, width = x.shape
    size = rows * width
    tile = 16 * 128
    padded = -(-size // tile) * tile
    flat = x.reshape(size)
    if padded != size:
        flat = jnp.pad(flat, (0, padded - size))
    flat = flat.reshape(padded // 128, 128)
    cid = cid + (0 if active is None else 2 + active) * 2
    out = gather_blk(flat, n, cid, active).reshape(n, padded)
    if padded != size:
        out = out[:, :size]
    return out.reshape(n * rows, width)


def to_blk_order(rows_in_gather_order, n):
    total, cols = rows_in_gather_order.shape
    nz = n // PLANE
    h = nz // 2
    rows = total // n
    part_a = rows_in_gather_order[: h * PLANE * rows].reshape(NY, NX, h, rows, cols)
    part_b = rows_in_gather_order[h * PLANE * rows :].reshape(NX, NY, nz - h, rows, cols)
    ordered = jnp.concatenate(
        [jnp.transpose(part_a, (2, 1, 0, 3, 4)), jnp.transpose(part_b, (2, 0, 1, 3, 4))], axis=0
    )
    return ordered.reshape(1, total, cols)


def from_behind(shard, axis, by):
    count = lax.axis_size(axis)
    pairs = [(i, i + by) for i in range(count) if 0 <= i + by < count]
    return lax.ppermute(shard, axis, pairs)


def attend(layer_in, qkv_cols, out_cols, modulate, fresh_own, old_keys, old_values, live, active):
    n = lax.axis_size("blk")
    stream = layer_in.astype(jnp.float32)
    center = jnp.mean(stream, axis=-1, keepdims=True)
    variance = jnp.mean((stream - center) ** 2, axis=-1, keepdims=True)
    normed = (stream - center) / jnp.sqrt(variance + 1e-06) * (1.0 + modulate[0]) + modulate[1]
    normed_b = normed.astype(jnp.bfloat16)
    columns = jnp.dot(
        gather_rows(normed_b, 0, active), qkv_cols, preferred_element_type=jnp.float32
    ).astype(jnp.bfloat16)
    projected = lax.all_to_all(to_blk_order(columns, n), "blk", split_axis=1, concat_axis=2, tiled=True)
    num_req, num_rows, width = layer_in.shape
    queries = projected[0, :, :width]
    new_keys = projected[:, :, width : 2 * width]
    new_values = projected[:, :, 2 * width :]
    use_fresh = (fresh_own == 1)[:, None, None]
    keys = jnp.where(use_fresh, new_keys, old_keys)
    values = jnp.where(use_fresh, new_values, old_values)
    kv_all = gather_rows(jnp.concatenate([keys, values], axis=2), 1, active)
    key_all = kv_all[:, :width]
    value_all = kv_all[:, width:]
    nz = n // PLANE
    live_zxy = live[0].reshape(nz, NX, NY)
    live_by_slot = jnp.concatenate([
        jnp.transpose(live_zxy[: nz // 2], (2, 1, 0)).reshape(-1),
        jnp.transpose(live_zxy[nz // 2 :], (1, 2, 0)).reshape(-1),
    ])
    usable = (jnp.repeat(live_by_slot, num_rows) == 1)[None, None, :]
    num_heads = width // 64
    head_of_col = jnp.arange(width) // 64
    in_head = head_of_col[None, :] == jnp.arange(num_heads)[:, None]
    q_diag = jnp.where(in_head[None], queries[:, None, :], jnp.zeros((), queries.dtype))
    scores = jnp.einsum("qhc,kc->qhk", q_diag, key_all, preferred_element_type=jnp.float32) * 0.125
    scores = jnp.where(usable, scores, -1e30)
    top = jnp.max(scores, axis=-1, keepdims=True)
    weights = jnp.where(usable, jnp.exp(scores - top), 0.0)
    total = jnp.sum(weights, axis=-1)
    mixed_all = jnp.einsum(
        "qhk,kc->qhc", weights, value_all.astype(jnp.float32), precision=lax.Precision.HIGHEST
    )
    own_head = jnp.sum(jnp.where(in_head[None], mixed_all, 0.0), axis=1)
    total_col = jnp.broadcast_to(total[:, :, None], (num_rows, num_heads, 64)).reshape(num_rows, width)
    attn = (own_head / total_col).astype(jnp.bfloat16)[None]
    out_part = jnp.dot(
        gather_rows(attn, 0, active), out_cols, preferred_element_type=jnp.float32
    ).astype(jnp.bfloat16)
    mixed_back = lax.all_to_all(to_blk_order(out_part, n), "blk", split_axis=1, concat_axis=2, tiled=True)
    return (stream + modulate[2] * mixed_back.astype(jnp.float32)).astype(jnp.bfloat16)


def swap_sections(x):
    return lax.ppermute(x, "section", [(0, 1), (1, 0)])


def per_device(hidden, qkv_weight, out_weight, modulation, timestep, fresh, live, k_stale, v_stale):
    sec = lax.axis_index("section")
    block_idx = lax.axis_index("blk")
    steps_all = modulation.shape[1]
    pick_row = (jnp.arange(steps_all) == timestep[0]).astype(jnp.float32)
    modulate_own = jnp.einsum("t,tcd->cd", pick_row, modulation[0], precision=lax.Precision.HIGHEST)
    num_blocks = fresh.shape[2]
    own_column = (jnp.arange(num_blocks) == block_idx).astype(jnp.int32)
    fresh_own = jnp.sum(fresh[0] * own_column[None, :], axis=1)
    qkv_own = qkv_weight[0]
    out_own = out_weight[0]
    stale_own = jnp.concatenate([k_stale[0], v_stale[0]], axis=2)

    qkv_other = swap_sections(qkv_own)
    out_other = swap_sections(out_own)
    modulate_other = swap_sections(modulate_own)
    fresh_other = swap_sections(fresh_own)
    stale_other = swap_sections(lax.dynamic_index_in_dim(stale_own, 1 - sec, 0, keepdims=True))

    stale_mine = lax.dynamic_index_in_dim(stale_own, sec, 0, keepdims=True)
    fresh_mine = lax.dynamic_index_in_dim(fresh_own, sec, 0, keepdims=True)
    fresh_theirs = lax.dynamic_index_in_dim(fresh_other, sec, 0, keepdims=True)
    live_mine = lax.dynamic_index_in_dim(live, sec, 0, keepdims=True)
    width = hidden.shape[2]

    layer_in = lax.dynamic_index_in_dim(hidden, sec, 0, keepdims=True)

    def run_layer(stream, layer):
        own = sec == layer
        stale = jnp.where(own, stale_mine, stale_other)
        out = attend(
            stream,
            jnp.where(own, qkv_own, qkv_other),
            jnp.where(own, out_own, out_other),
            jnp.where(own, modulate_own, modulate_other),
            jnp.where(own, fresh_mine, fresh_theirs),
            stale[:, :, :width],
            stale[:, :, width:],
            live_mine,
            None,
        )
        return out, out

    _, stacked = lax.scan(run_layer, layer_in, jnp.arange(2))
    outs = [stacked[0], stacked[1]]
    first_req1 = lax.ppermute(outs[0], "section", [(1, 0)])
    second_req0 = lax.ppermute(outs[1], "section", [(0, 1)])
    result = jnp.where(
        sec == 0,
        jnp.concatenate([outs[0], first_req1], axis=0),
        jnp.concatenate([second_req0, outs[1]], axis=0),
    )
    return result[None]


def solution(mesh):
    return jax.shard_map(
        per_device,
        mesh=mesh,
        in_specs=(
            P(None, "blk", None),
            P("section", None, "blk"),
            P("section", None, "blk"),
            P("section", None, None, None),
            P(),
            P("section", None, None),
            P(),
            P("section", None, "blk", None),
            P("section", None, "blk", None),
        ),
        out_specs=P("section", None, "blk", None),
        check_vma=False,
    )
```

```python
import functools

import jax
import jax.numpy as jnp
from jax import lax
from jax.experimental import pallas as pl
from jax.experimental.pallas import tpu as pltpu
from jax.sharding import PartitionSpec as P

MESH = pl.DeviceIdType.MESH


NX = 4
NY = 4
PLANE = NX * NY


def gather_kernel(n, x_ref, oa_ref, ob_ref, zbuf, zs, zr, rs, rr, local_sem):
    sec = lax.axis_index("section")
    nz = n // PLANE
    h = nz // 2
    me = lax.axis_index("blk")
    y = me % NY
    x = (me // NY) % NX
    z = me // PLANE

    def dev(zz, xx, yy):
        return (sec, (zz * NX + xx) * NY + yy)

    xp, xm, x2 = (x + 1) % NX, (x + NX - 1) % NX, (x + 2) % NX
    yp, ym, y2 = (y + 1) % NY, (y + NY - 1) % NY, (y + 2) % NY
    barrier = pltpu.get_barrier_semaphore()

    def z_peer(i):
        return lax.rem(z + 1 + i, nz)

    def greet_z(i, carry):
        pl.semaphore_signal(barrier, inc=1, device_id=dev(z_peer(i), x, y), device_id_type=MESH)
        return carry

    lax.fori_loop(0, nz - 1, greet_z, 0)
    for target in (dev(z, xp, y), dev(z, xm, y), dev(z, x, yp), dev(z, x, ym)):
        pl.semaphore_signal(barrier, inc=1, device_id=target, device_id_type=MESH)
    pl.semaphore_wait(barrier, nz - 1 + 4)

    local = pltpu.make_async_copy(x_ref, zbuf.at[z], local_sem.at[0])
    local.start()

    def copy_z(i, src_z):
        return pltpu.make_async_remote_copy(
            src_ref=x_ref,
            dst_ref=zbuf.at[src_z],
            send_sem=zs.at[i],
            recv_sem=zr.at[src_z],
            device_id=dev(z_peer(i), x, y),
            device_id_type=MESH,
        )

    def send_z(i, carry):
        copy_z(i, z).start()
        return carry

    lax.fori_loop(0, nz - 1, send_z, 0)

    def finish_z(i, carry):
        copy_z(i, z).wait_send()
        copy_z(i, lax.rem(z + nz - 1 - i, nz)).wait_recv()
        return carry

    lax.fori_loop(0, nz - 1, finish_z, 0)
    local.wait()
    own_a = pltpu.make_async_copy(zbuf.at[pl.ds(0, h)], oa_ref.at[y, x], local_sem.at[1])
    own_b = pltpu.make_async_copy(zbuf.at[pl.ds(h, nz - h)], ob_ref.at[x, y], local_sem.at[2])
    own_a.start()
    own_b.start()

    def rcopy(stage, src, dst, k, target):
        return pltpu.make_async_remote_copy(
            src_ref=src, dst_ref=dst, send_sem=rs.at[stage, k], recv_sem=rr.at[stage, k],
            device_id=target, device_id_type=MESH,
        )

    class Ring:
        def __init__(self, stage, mine, block, up, down, far, count, target_up, target_down):
            self.stage, self.mine, self.block = stage, mine, block
            self.up, self.down, self.far, self.count = up, down, far, count
            self.target_up, self.target_down = target_up, target_down

        def step1(self):
            s, me_ref = self.stage, self.block(None)
            self.a = rcopy(s, self.mine, me_ref, 0, self.target_up)
            self.b = rcopy(s, self.mine, me_ref, 1, self.target_down)
            self.a.start()
            self.b.start()

        def wait1(self):
            s = self.stage
            self.a.wait_send()
            self.b.wait_send()
            rcopy(s, self.block(self.down), self.block(self.down), 0, self.target_down).wait_recv()
            rcopy(s, self.block(self.up), self.block(self.up), 1, self.target_up).wait_recv()

        def step2(self):
            s, half = self.stage, self.count // 2
            first = self.block(self.down).at[pl.ds(0, half)]
            second = self.block(self.up).at[pl.ds(half, self.count - half)]
            self.c = rcopy(s, first, first, 2, self.target_up)
            self.d = rcopy(s, second, second, 3, self.target_down)
            self.c.start()
            self.d.start()

        def wait2(self):
            s, half = self.stage, self.count // 2
            self.c.wait_send()
            self.d.wait_send()
            first = self.block(self.far).at[pl.ds(0, half)]
            second = self.block(self.far).at[pl.ds(half, self.count - half)]
            rcopy(s, first, first, 2, self.target_down).wait_recv()
            rcopy(s, second, second, 3, self.target_up).wait_recv()

    x_targets = (dev(z, xp, y), dev(z, xm, y))
    y_targets = (dev(z, x, yp), dev(z, x, ym))
    a_x = Ring(0, zbuf.at[pl.ds(0, h)], lambda p: oa_ref.at[y, x if p is None else p],
               xp, xm, x2, h, *x_targets)
    b_y = Ring(1, zbuf.at[pl.ds(h, nz - h)], lambda p: ob_ref.at[x, y if p is None else p],
               yp, ym, y2, nz - h, *y_targets)
    a_y = Ring(2, oa_ref.at[y], lambda p: oa_ref.at[y if p is None else p],
               yp, ym, y2, NX, *y_targets)
    b_x = Ring(3, ob_ref.at[x], lambda p: ob_ref.at[x if p is None else p],
               xp, xm, x2, NY, *x_targets)
    for first, second in ((a_x, b_y), (a_y, b_x)):
        first.step1()
        second.step1()
        first.wait1()
        second.wait1()
        first.step2()
        second.step2()
        first.wait2()
        second.wait2()
        if first is a_x:
            own_a.wait()
            own_b.wait()


def gather_blk(x, n, cid, active=None):
    nz = n // PLANE
    h = nz // 2
    oa, ob = pl.pallas_call(
        functools.partial(gather_kernel, n),
        out_shape=(
            jax.ShapeDtypeStruct((NY, NX, h) + x.shape, x.dtype),
            jax.ShapeDtypeStruct((NX, NY, nz - h) + x.shape, x.dtype),
        ),
        in_specs=[pl.BlockSpec(memory_space=pl.ANY)],
        out_specs=(pl.BlockSpec(memory_space=pl.ANY), pl.BlockSpec(memory_space=pl.ANY)),
        scratch_shapes=[
            pltpu.VMEM((nz,) + x.shape, x.dtype),
            pltpu.SemaphoreType.DMA((nz,)),
            pltpu.SemaphoreType.DMA((nz,)),
            pltpu.SemaphoreType.DMA((4, 4)),
            pltpu.SemaphoreType.DMA((4, 4)),
            pltpu.SemaphoreType.DMA((3,)),
        ],
        compiler_params=pltpu.CompilerParams(collective_id=cid, has_side_effects=True),
    )(x)
    return jnp.concatenate([oa.reshape((-1,) + x.shape), ob.reshape((-1,) + x.shape)], axis=0)


def gather_rows(x, cid, active):
    n = lax.axis_size("blk")
    _, rows, width = x.shape
    size = rows * width
    tile = 16 * 128
    padded = -(-size // tile) * tile
    flat = x.reshape(size)
    if padded != size:
        flat = jnp.pad(flat, (0, padded - size))
    flat = flat.reshape(padded // 128, 128)
    cid = cid + (0 if active is None else 2 + active) * 2
    out = gather_blk(flat, n, cid, active).reshape(n, padded)
    if padded != size:
        out = out[:, :size]
    return out.reshape(n * rows, width)


def to_blk_order(rows_in_gather_order, n):
    total, cols = rows_in_gather_order.shape
    nz = n // PLANE
    h = nz // 2
    rows = total // n
    part_a = rows_in_gather_order[: h * PLANE * rows].reshape(NY, NX, h, rows, cols)
    part_b = rows_in_gather_order[h * PLANE * rows :].reshape(NX, NY, nz - h, rows, cols)
    ordered = jnp.concatenate(
        [jnp.transpose(part_a, (2, 1, 0, 3, 4)), jnp.transpose(part_b, (2, 0, 1, 3, 4))], axis=0
    )
    return ordered.reshape(1, total, cols)


def from_behind(shard, axis, by):
    count = lax.axis_size(axis)
    pairs = [(i, i + by) for i in range(count) if 0 <= i + by < count]
    return lax.ppermute(shard, axis, pairs)


def norm_rows(stream, modulate):
    center = jnp.mean(stream, axis=-1, keepdims=True)
    variance = jnp.mean((stream - center) ** 2, axis=-1, keepdims=True)
    normed = (stream - center) / jnp.sqrt(variance + 1e-06) * (1.0 + modulate[0]) + modulate[1]
    return normed.astype(jnp.bfloat16)


def attend(normed_all, qkv_cols, out_cols, fresh_own, old_keys, old_values, live, num_rows):
    n = lax.axis_size("blk")
    width = normed_all.shape[1]
    columns = jnp.dot(normed_all, qkv_cols, preferred_element_type=jnp.float32).astype(jnp.bfloat16)
    projected = lax.all_to_all(to_blk_order(columns, n), "blk", split_axis=1, concat_axis=2, tiled=True)
    queries = projected[0, :, :width]
    new_keys = projected[:, :, width : 2 * width]
    new_values = projected[:, :, 2 * width :]
    use_fresh = (fresh_own == 1)[:, None, None]
    keys = jnp.where(use_fresh, new_keys, old_keys)
    values = jnp.where(use_fresh, new_values, old_values)
    kv_all = gather_rows(jnp.concatenate([keys, values], axis=2), 1, None)
    key_all = kv_all[:, :width]
    value_all = kv_all[:, width:]
    nz = n // PLANE
    live_zxy = live[0].reshape(nz, NX, NY)
    live_by_slot = jnp.concatenate([
        jnp.transpose(live_zxy[: nz // 2], (2, 1, 0)).reshape(-1),
        jnp.transpose(live_zxy[nz // 2 :], (1, 2, 0)).reshape(-1),
    ])
    usable = (jnp.repeat(live_by_slot, num_rows) == 1)[None, None, :]
    num_heads = width // 64
    head_of_col = jnp.arange(width) // 64
    in_head = head_of_col[None, :] == jnp.arange(num_heads)[:, None]
    q_diag = jnp.where(in_head[None], queries[:, None, :], jnp.zeros((), queries.dtype))
    scores = jnp.einsum("qhc,kc->qhk", q_diag, key_all, preferred_element_type=jnp.float32) * 0.125
    scores = jnp.where(usable, scores, -1e30)
    top = jnp.max(scores, axis=-1, keepdims=True)
    weights = jnp.where(usable, jnp.exp(scores - top), 0.0)
    total = jnp.sum(weights, axis=-1)
    mixed_all = jnp.einsum(
        "qhk,kc->qhc", weights, value_all.astype(jnp.float32), precision=lax.Precision.HIGHEST
    )
    own_head = jnp.sum(jnp.where(in_head[None], mixed_all, 0.0), axis=1)
    total_col = jnp.broadcast_to(total[:, :, None], (num_rows, num_heads, 64)).reshape(num_rows, width)
    attn = (own_head / total_col).astype(jnp.bfloat16)[None]
    return jnp.dot(
        gather_rows(attn, 0, None), out_cols, preferred_element_type=jnp.float32
    ).astype(jnp.bfloat16)


def own_slot():
    n = lax.axis_size("blk")
    nz = n // PLANE
    h = nz // 2
    me = lax.axis_index("blk")
    y = me % NY
    x = (me // NY) % NX
    z = me // PLANE
    return jnp.where(z < h, (y * NX + x) * h + z, h * PLANE + (x * NY + y) * (nz - h) + (z - h))


def swap_sections(x):
    return lax.ppermute(x, "section", [(0, 1), (1, 0)])


def per_device(hidden, qkv_weight, out_weight, modulation, timestep, fresh, live, k_stale, v_stale):
    sec = lax.axis_index("section")
    block_idx = lax.axis_index("blk")
    steps_all = modulation.shape[1]
    pick_row = (jnp.arange(steps_all) == timestep[0]).astype(jnp.float32)
    modulate_own = jnp.einsum("t,tcd->cd", pick_row, modulation[0], precision=lax.Precision.HIGHEST)
    num_blocks = fresh.shape[2]
    own_column = (jnp.arange(num_blocks) == block_idx).astype(jnp.int32)
    fresh_own = jnp.sum(fresh[0] * own_column[None, :], axis=1)
    qkv_own = qkv_weight[0]
    out_own = out_weight[0]
    stale_own = jnp.concatenate([k_stale[0], v_stale[0]], axis=2)

    qkv_other = swap_sections(qkv_own)
    out_other = swap_sections(out_own)
    modulate_other = swap_sections(modulate_own)
    fresh_other = swap_sections(fresh_own)
    stale_other = swap_sections(lax.dynamic_index_in_dim(stale_own, 1 - sec, 0, keepdims=True))

    stale_mine = lax.dynamic_index_in_dim(stale_own, sec, 0, keepdims=True)
    fresh_mine = lax.dynamic_index_in_dim(fresh_own, sec, 0, keepdims=True)
    fresh_theirs = lax.dynamic_index_in_dim(fresh_other, sec, 0, keepdims=True)
    live_mine = lax.dynamic_index_in_dim(live, sec, 0, keepdims=True)
    width = hidden.shape[2]

    n = lax.axis_size("blk")
    num_rows = hidden.shape[1]
    mods, args = [], []
    for layer in range(2):
        own = sec == layer
        stale = jnp.where(own, stale_mine, stale_other)
        mods.append(jnp.where(own, modulate_own, modulate_other))
        args.append((
            jnp.where(own, qkv_own, qkv_other),
            jnp.where(own, out_own, out_other),
            jnp.where(own, fresh_mine, fresh_theirs),
            stale[:, :, :width],
            stale[:, :, width:],
            live_mine,
            num_rows,
        ))
    hidden_all = gather_rows(lax.dynamic_index_in_dim(hidden, sec, 0, keepdims=True), 0, None)
    stream0 = hidden_all.astype(jnp.float32)
    out_part = attend(norm_rows(stream0, mods[0]), *args[0])
    cols = out_part.shape[1]
    total = out_part.shape[0]
    mixed_parts = gather_rows(out_part[None], 0, None).reshape(n, total * cols)
    mixed_full = jnp.transpose(
        to_blk_order(mixed_parts, n).reshape(n, total, cols), (1, 0, 2)
    ).reshape(total, n * cols)
    first_all = (stream0 + mods[0][2] * mixed_full.astype(jnp.float32)).astype(jnp.bfloat16)
    slot = own_slot()
    first_own = lax.dynamic_slice_in_dim(first_all, slot * num_rows, num_rows, 0)[None]
    stream1 = first_all.astype(jnp.float32)
    out_part1 = attend(norm_rows(stream1, mods[1]), *args[1])
    mixed_back = lax.all_to_all(to_blk_order(out_part1, n), "blk", split_axis=1, concat_axis=2, tiled=True)
    second_own = (
        first_own.astype(jnp.float32) + mods[1][2] * mixed_back.astype(jnp.float32)
    ).astype(jnp.bfloat16)
    outs = [first_own, second_own]
    first_req1 = lax.ppermute(outs[0], "section", [(1, 0)])
    second_req0 = lax.ppermute(outs[1], "section", [(0, 1)])
    result = jnp.where(
        sec == 0,
        jnp.concatenate([outs[0], first_req1], axis=0),
        jnp.concatenate([second_req0, outs[1]], axis=0),
    )
    return result[None]


def solution(mesh):
    return jax.shard_map(
        per_device,
        mesh=mesh,
        in_specs=(
            P(None, "blk", None),
            P("section", None, "blk"),
            P("section", None, "blk"),
            P("section", None, None, None),
            P(),
            P("section", None, None),
            P(),
            P("section", None, "blk", None),
            P("section", None, "blk", None),
        ),
        out_specs=P("section", None, "blk", None),
        check_vma=False,
    )
```

```python
import functools

import jax
import jax.numpy as jnp
from jax import lax
from jax.experimental import pallas as pl
from jax.experimental.pallas import tpu as pltpu
from jax.sharding import PartitionSpec as P

MESH = pl.DeviceIdType.MESH


NX = 4
NY = 4
PLANE = NX * NY


def gather_kernel(n, x_ref, o_ref, zbuf, zs, zr, rs, rr, local_sem):
    oa_ref = o_ref.at[0]
    ob_ref = o_ref.at[1]
    sec = lax.axis_index("section")
    nz = n // PLANE
    h = nz // 2
    me = lax.axis_index("blk")
    y = me % NY
    x = (me // NY) % NX
    z = me // PLANE

    def dev(zz, xx, yy):
        return (sec, (zz * NX + xx) * NY + yy)

    xp, xm, x2 = (x + 1) % NX, (x + NX - 1) % NX, (x + 2) % NX
    yp, ym, y2 = (y + 1) % NY, (y + NY - 1) % NY, (y + 2) % NY
    barrier = pltpu.get_barrier_semaphore()

    def z_peer(i):
        return lax.rem(z + 1 + i, nz)

    def greet_z(i, carry):
        pl.semaphore_signal(barrier, inc=1, device_id=dev(z_peer(i), x, y), device_id_type=MESH)
        return carry

    lax.fori_loop(0, nz - 1, greet_z, 0)
    for target in (dev(z, xp, y), dev(z, xm, y), dev(z, x, yp), dev(z, x, ym)):
        pl.semaphore_signal(barrier, inc=1, device_id=target, device_id_type=MESH)
    pl.semaphore_wait(barrier, nz - 1 + 4)

    local = pltpu.make_async_copy(x_ref, zbuf.at[z], local_sem.at[0])
    local.start()

    def copy_z(i, src_z):
        return pltpu.make_async_remote_copy(
            src_ref=x_ref,
            dst_ref=zbuf.at[src_z],
            send_sem=zs.at[i],
            recv_sem=zr.at[src_z],
            device_id=dev(z_peer(i), x, y),
            device_id_type=MESH,
        )

    def send_z(i, carry):
        copy_z(i, z).start()
        return carry

    lax.fori_loop(0, nz - 1, send_z, 0)

    def finish_z(i, carry):
        copy_z(i, z).wait_send()
        copy_z(i, lax.rem(z + nz - 1 - i, nz)).wait_recv()
        return carry

    lax.fori_loop(0, nz - 1, finish_z, 0)
    local.wait()
    own_a = pltpu.make_async_copy(zbuf.at[pl.ds(0, h)], oa_ref.at[y, x], local_sem.at[1])
    own_b = pltpu.make_async_copy(zbuf.at[pl.ds(h, nz - h)], ob_ref.at[x, y], local_sem.at[2])
    own_a.start()
    own_b.start()

    def rcopy(stage, src, dst, k, target):
        return pltpu.make_async_remote_copy(
            src_ref=src, dst_ref=dst, send_sem=rs.at[stage, k], recv_sem=rr.at[stage, k],
            device_id=target, device_id_type=MESH,
        )

    class Ring:
        def __init__(self, stage, mine, block, up, down, far, count, target_up, target_down):
            self.stage, self.mine, self.block = stage, mine, block
            self.up, self.down, self.far, self.count = up, down, far, count
            self.target_up, self.target_down = target_up, target_down

        def step1(self):
            s, me_ref = self.stage, self.block(None)
            self.a = rcopy(s, self.mine, me_ref, 0, self.target_up)
            self.b = rcopy(s, self.mine, me_ref, 1, self.target_down)
            self.a.start()
            self.b.start()

        def wait1(self):
            s = self.stage
            self.a.wait_send()
            self.b.wait_send()
            rcopy(s, self.block(self.down), self.block(self.down), 0, self.target_down).wait_recv()
            rcopy(s, self.block(self.up), self.block(self.up), 1, self.target_up).wait_recv()

        def step2(self):
            s, half = self.stage, self.count // 2
            first = self.block(self.down).at[pl.ds(0, half)]
            second = self.block(self.up).at[pl.ds(half, self.count - half)]
            self.c = rcopy(s, first, first, 2, self.target_up)
            self.d = rcopy(s, second, second, 3, self.target_down)
            self.c.start()
            self.d.start()

        def wait2(self):
            s, half = self.stage, self.count // 2
            self.c.wait_send()
            self.d.wait_send()
            first = self.block(self.far).at[pl.ds(0, half)]
            second = self.block(self.far).at[pl.ds(half, self.count - half)]
            rcopy(s, first, first, 2, self.target_down).wait_recv()
            rcopy(s, second, second, 3, self.target_up).wait_recv()

    x_targets = (dev(z, xp, y), dev(z, xm, y))
    y_targets = (dev(z, x, yp), dev(z, x, ym))
    a_x = Ring(0, zbuf.at[pl.ds(0, h)], lambda p: oa_ref.at[y, x if p is None else p],
               xp, xm, x2, h, *x_targets)
    b_y = Ring(1, zbuf.at[pl.ds(h, nz - h)], lambda p: ob_ref.at[x, y if p is None else p],
               yp, ym, y2, nz - h, *y_targets)
    a_y = Ring(2, oa_ref.at[y], lambda p: oa_ref.at[y if p is None else p],
               yp, ym, y2, NX, *y_targets)
    b_x = Ring(3, ob_ref.at[x], lambda p: ob_ref.at[x if p is None else p],
               xp, xm, x2, NY, *x_targets)
    for first, second in ((a_x, b_y), (a_y, b_x)):
        first.step1()
        second.step1()
        first.wait1()
        second.wait1()
        first.step2()
        second.step2()
        first.wait2()
        second.wait2()
        if first is a_x:
            own_a.wait()
            own_b.wait()


def gather_blk(x, n, cid, active=None):
    nz = n // PLANE
    h = nz // 2
    assert NX == NY and nz == 2 * h
    out = pl.pallas_call(
        functools.partial(gather_kernel, n),
        out_shape=jax.ShapeDtypeStruct((2, NY, NX, h) + x.shape, x.dtype),
        in_specs=[pl.BlockSpec(memory_space=pl.ANY)],
        out_specs=pl.BlockSpec(memory_space=pl.ANY),
        scratch_shapes=[
            pltpu.VMEM((nz,) + x.shape, x.dtype),
            pltpu.SemaphoreType.DMA((nz,)),
            pltpu.SemaphoreType.DMA((nz,)),
            pltpu.SemaphoreType.DMA((4, 4)),
            pltpu.SemaphoreType.DMA((4, 4)),
            pltpu.SemaphoreType.DMA((3,)),
        ],
        compiler_params=pltpu.CompilerParams(collective_id=cid, has_side_effects=True),
    )(x)
    return out.reshape((n,) + x.shape)


def gather_rows(x, cid, active):
    n = lax.axis_size("blk")
    _, rows, width = x.shape
    size = rows * width
    tile = 16 * 128
    padded = -(-size // tile) * tile
    flat = x.reshape(size)
    if padded != size:
        flat = jnp.pad(flat, (0, padded - size))
    flat = flat.reshape(padded // 128, 128)
    cid = cid + (0 if active is None else 2 + active) * 2
    out = gather_blk(flat, n, cid, active).reshape(n, padded)
    if padded != size:
        out = out[:, :size]
    return out.reshape(n * rows, width)


def to_blk_order(rows_in_gather_order, n):
    total, cols = rows_in_gather_order.shape
    nz = n // PLANE
    h = nz // 2
    rows = total // n
    part_a = rows_in_gather_order[: h * PLANE * rows].reshape(NY, NX, h, rows, cols)
    part_b = rows_in_gather_order[h * PLANE * rows :].reshape(NX, NY, nz - h, rows, cols)
    ordered = jnp.concatenate(
        [jnp.transpose(part_a, (2, 1, 0, 3, 4)), jnp.transpose(part_b, (2, 0, 1, 3, 4))], axis=0
    )
    return ordered.reshape(1, total, cols)


def from_behind(shard, axis, by):
    count = lax.axis_size(axis)
    pairs = [(i, i + by) for i in range(count) if 0 <= i + by < count]
    return lax.ppermute(shard, axis, pairs)


def attend(layer_in, qkv_cols, out_cols, modulate, fresh_own, old_keys, old_values, live, active):
    n = lax.axis_size("blk")
    stream = layer_in.astype(jnp.float32)
    center = jnp.mean(stream, axis=-1, keepdims=True)
    variance = jnp.mean((stream - center) ** 2, axis=-1, keepdims=True)
    normed = (stream - center) / jnp.sqrt(variance + 1e-06) * (1.0 + modulate[0]) + modulate[1]
    normed_b = normed.astype(jnp.bfloat16)
    columns = jnp.dot(
        gather_rows(normed_b, 0, active), qkv_cols, preferred_element_type=jnp.float32
    ).astype(jnp.bfloat16)
    projected = lax.all_to_all(to_blk_order(columns, n), "blk", split_axis=1, concat_axis=2, tiled=True)
    num_req, num_rows, width = layer_in.shape
    queries = projected[0, :, :width]
    new_keys = projected[:, :, width : 2 * width]
    new_values = projected[:, :, 2 * width :]
    use_fresh = (fresh_own == 1)[:, None, None]
    keys = jnp.where(use_fresh, new_keys, old_keys)
    values = jnp.where(use_fresh, new_values, old_values)
    kv_all = gather_rows(jnp.concatenate([keys, values], axis=2), 1, active)
    key_all = kv_all[:, :width]
    value_all = kv_all[:, width:]
    nz = n // PLANE
    live_zxy = live[0].reshape(nz, NX, NY)
    live_by_slot = jnp.concatenate([
        jnp.transpose(live_zxy[: nz // 2], (2, 1, 0)).reshape(-1),
        jnp.transpose(live_zxy[nz // 2 :], (1, 2, 0)).reshape(-1),
    ])
    usable = (jnp.repeat(live_by_slot, num_rows) == 1)[None, None, :]
    num_heads = width // 64
    head_of_col = jnp.arange(width) // 64
    in_head = head_of_col[None, :] == jnp.arange(num_heads)[:, None]
    q_diag = jnp.where(in_head[None], queries[:, None, :], jnp.zeros((), queries.dtype))
    scores = jnp.einsum("qhc,kc->qhk", q_diag, key_all, preferred_element_type=jnp.float32) * 0.125
    scores = jnp.where(usable, scores, -1e30)
    top = jnp.max(scores, axis=-1, keepdims=True)
    weights = jnp.where(usable, jnp.exp(scores - top), 0.0)
    total = jnp.sum(weights, axis=-1)
    mixed_all = jnp.einsum(
        "qhk,kc->qhc", weights, value_all.astype(jnp.float32), precision=lax.Precision.HIGHEST
    )
    own_head = jnp.sum(jnp.where(in_head[None], mixed_all, 0.0), axis=1)
    total_col = jnp.broadcast_to(total[:, :, None], (num_rows, num_heads, 64)).reshape(num_rows, width)
    attn = (own_head / total_col).astype(jnp.bfloat16)[None]
    out_part = jnp.dot(
        gather_rows(attn, 0, active), out_cols, preferred_element_type=jnp.float32
    ).astype(jnp.bfloat16)
    mixed_back = lax.all_to_all(to_blk_order(out_part, n), "blk", split_axis=1, concat_axis=2, tiled=True)
    return (stream + modulate[2] * mixed_back.astype(jnp.float32)).astype(jnp.bfloat16)


def swap_sections(x):
    return lax.ppermute(x, "section", [(0, 1), (1, 0)])


def per_device(hidden, qkv_weight, out_weight, modulation, timestep, fresh, live, k_stale, v_stale):
    sec = lax.axis_index("section")
    block_idx = lax.axis_index("blk")
    steps_all = modulation.shape[1]
    pick_row = (jnp.arange(steps_all) == timestep[0]).astype(jnp.float32)
    modulate_own = jnp.einsum("t,tcd->cd", pick_row, modulation[0], precision=lax.Precision.HIGHEST)
    num_blocks = fresh.shape[2]
    own_column = (jnp.arange(num_blocks) == block_idx).astype(jnp.int32)
    fresh_own = jnp.sum(fresh[0] * own_column[None, :], axis=1)
    qkv_own = qkv_weight[0]
    out_own = out_weight[0]
    stale_own = jnp.concatenate([k_stale[0], v_stale[0]], axis=2)

    qkv_other = swap_sections(qkv_own)
    out_other = swap_sections(out_own)
    modulate_other = swap_sections(modulate_own)
    fresh_other = swap_sections(fresh_own)
    stale_other = swap_sections(lax.dynamic_index_in_dim(stale_own, 1 - sec, 0, keepdims=True))

    stale_mine = lax.dynamic_index_in_dim(stale_own, sec, 0, keepdims=True)
    fresh_mine = lax.dynamic_index_in_dim(fresh_own, sec, 0, keepdims=True)
    fresh_theirs = lax.dynamic_index_in_dim(fresh_other, sec, 0, keepdims=True)
    live_mine = lax.dynamic_index_in_dim(live, sec, 0, keepdims=True)
    width = hidden.shape[2]

    layer_in = lax.dynamic_index_in_dim(hidden, sec, 0, keepdims=True)
    outs = []
    for layer in range(2):
        own = sec == layer
        stale = jnp.where(own, stale_mine, stale_other)
        layer_in = attend(
            layer_in,
            jnp.where(own, qkv_own, qkv_other),
            jnp.where(own, out_own, out_other),
            jnp.where(own, modulate_own, modulate_other),
            jnp.where(own, fresh_mine, fresh_theirs),
            stale[:, :, :width],
            stale[:, :, width:],
            live_mine,
            None,
        )
        outs.append(layer_in)
    first_req1 = lax.ppermute(outs[0], "section", [(1, 0)])
    second_req0 = lax.ppermute(outs[1], "section", [(0, 1)])
    result = jnp.where(
        sec == 0,
        jnp.concatenate([outs[0], first_req1], axis=0),
        jnp.concatenate([second_req0, outs[1]], axis=0),
    )
    return result[None]


def solution(mesh):
    return jax.shard_map(
        per_device,
        mesh=mesh,
        in_specs=(
            P(None, "blk", None),
            P("section", None, "blk"),
            P("section", None, "blk"),
            P("section", None, None, None),
            P(),
            P("section", None, None),
            P(),
            P("section", None, "blk", None),
            P("section", None, "blk", None),
        ),
        out_specs=P("section", None, "blk", None),
        check_vma=False,
    )
```

```python
import functools

import jax
import jax.numpy as jnp
from jax import lax
from jax.experimental import pallas as pl
from jax.experimental.pallas import tpu as pltpu
from jax.sharding import PartitionSpec as P

MESH = pl.DeviceIdType.MESH


NX = 4
NY = 4
PLANE = NX * NY


def gather_kernel(n, x_ref, o_ref, zbuf, zs, zr, rs, rr, local_sem):
    oa_ref = o_ref.at[0]
    ob_ref = o_ref.at[1]
    sec = lax.axis_index("section")
    nz = n // PLANE
    h = nz // 2
    me = lax.axis_index("blk")
    y = me % NY
    x = (me // NY) % NX
    z = me // PLANE

    def dev(zz, xx, yy):
        return (sec, (zz * NX + xx) * NY + yy)

    xp, xm, x2 = (x + 1) % NX, (x + NX - 1) % NX, (x + 2) % NX
    yp, ym, y2 = (y + 1) % NY, (y + NY - 1) % NY, (y + 2) % NY
    barrier = pltpu.get_barrier_semaphore()

    def z_peer(i):
        return lax.rem(z + 1 + i, nz)

    def greet_z(i, carry):
        pl.semaphore_signal(barrier, inc=1, device_id=dev(z_peer(i), x, y), device_id_type=MESH)
        return carry

    lax.fori_loop(0, nz - 1, greet_z, 0)
    for target in (dev(z, xp, y), dev(z, xm, y), dev(z, x, yp), dev(z, x, ym)):
        pl.semaphore_signal(barrier, inc=1, device_id=target, device_id_type=MESH)
    pl.semaphore_wait(barrier, nz - 1 + 4)

    local = pltpu.make_async_copy(x_ref, zbuf.at[z], local_sem.at[0])
    local.start()

    def copy_z(i, src_z):
        return pltpu.make_async_remote_copy(
            src_ref=x_ref,
            dst_ref=zbuf.at[src_z],
            send_sem=zs.at[i],
            recv_sem=zr.at[src_z],
            device_id=dev(z_peer(i), x, y),
            device_id_type=MESH,
        )

    def send_z(i, carry):
        copy_z(i, z).start()
        return carry

    lax.fori_loop(0, nz - 1, send_z, 0)

    def finish_z(i, carry):
        copy_z(i, z).wait_send()
        copy_z(i, lax.rem(z + nz - 1 - i, nz)).wait_recv()
        return carry

    lax.fori_loop(0, nz - 1, finish_z, 0)
    local.wait()
    own_a = pltpu.make_async_copy(zbuf.at[pl.ds(0, h)], oa_ref.at[y, x], local_sem.at[1])
    own_b = pltpu.make_async_copy(zbuf.at[pl.ds(h, nz - h)], ob_ref.at[x, y], local_sem.at[2])
    own_a.start()
    own_b.start()

    def rcopy(stage, src, dst, k, target):
        return pltpu.make_async_remote_copy(
            src_ref=src, dst_ref=dst, send_sem=rs.at[stage, k], recv_sem=rr.at[stage, k],
            device_id=target, device_id_type=MESH,
        )

    class Ring:
        def __init__(self, stage, mine, block, up, down, far, count, target_up, target_down):
            self.stage, self.mine, self.block = stage, mine, block
            self.up, self.down, self.far, self.count = up, down, far, count
            self.target_up, self.target_down = target_up, target_down

        def step1(self):
            s, me_ref = self.stage, self.block(None)
            self.a = rcopy(s, self.mine, me_ref, 0, self.target_up)
            self.b = rcopy(s, self.mine, me_ref, 1, self.target_down)
            self.a.start()
            self.b.start()

        def wait1(self):
            s = self.stage
            self.a.wait_send()
            self.b.wait_send()
            rcopy(s, self.block(self.down), self.block(self.down), 0, self.target_down).wait_recv()
            rcopy(s, self.block(self.up), self.block(self.up), 1, self.target_up).wait_recv()

        def step2(self):
            s, half = self.stage, self.count // 2
            first = self.block(self.down).at[pl.ds(0, half)]
            second = self.block(self.up).at[pl.ds(half, self.count - half)]
            self.c = rcopy(s, first, first, 2, self.target_up)
            self.d = rcopy(s, second, second, 3, self.target_down)
            self.c.start()
            self.d.start()

        def wait2(self):
            s, half = self.stage, self.count // 2
            self.c.wait_send()
            self.d.wait_send()
            first = self.block(self.far).at[pl.ds(0, half)]
            second = self.block(self.far).at[pl.ds(half, self.count - half)]
            rcopy(s, first, first, 2, self.target_down).wait_recv()
            rcopy(s, second, second, 3, self.target_up).wait_recv()

    x_targets = (dev(z, xp, y), dev(z, xm, y))
    y_targets = (dev(z, x, yp), dev(z, x, ym))
    a_x = Ring(0, zbuf.at[pl.ds(0, h)], lambda p: oa_ref.at[y, x if p is None else p],
               xp, xm, x2, h, *x_targets)
    b_y = Ring(1, zbuf.at[pl.ds(h, nz - h)], lambda p: ob_ref.at[x, y if p is None else p],
               yp, ym, y2, nz - h, *y_targets)
    a_y = Ring(2, oa_ref.at[y], lambda p: oa_ref.at[y if p is None else p],
               yp, ym, y2, NX, *y_targets)
    b_x = Ring(3, ob_ref.at[x], lambda p: ob_ref.at[x if p is None else p],
               xp, xm, x2, NY, *x_targets)
    for first, second in ((a_x, b_y), (a_y, b_x)):
        first.step1()
        second.step1()
        first.wait1()
        second.wait1()
        first.step2()
        second.step2()
        first.wait2()
        second.wait2()
        if first is a_x:
            own_a.wait()
            own_b.wait()


def gather_blk(x, n, cid, active=None):
    nz = n // PLANE
    h = nz // 2
    assert NX == NY and nz == 2 * h
    out = pl.pallas_call(
        functools.partial(gather_kernel, n),
        out_shape=jax.ShapeDtypeStruct((2, NY, NX, h) + x.shape, x.dtype),
        in_specs=[pl.BlockSpec(memory_space=pl.ANY)],
        out_specs=pl.BlockSpec(memory_space=pl.ANY),
        scratch_shapes=[
            pltpu.VMEM((nz,) + x.shape, x.dtype),
            pltpu.SemaphoreType.DMA((nz,)),
            pltpu.SemaphoreType.DMA((nz,)),
            pltpu.SemaphoreType.DMA((4, 4)),
            pltpu.SemaphoreType.DMA((4, 4)),
            pltpu.SemaphoreType.DMA((3,)),
        ],
        compiler_params=pltpu.CompilerParams(collective_id=cid, has_side_effects=True),
    )(x)
    return out.reshape((n,) + x.shape)


def gather_rows(x, cid, active):
    n = lax.axis_size("blk")
    _, rows, width = x.shape
    size = rows * width
    tile = 16 * 128
    padded = -(-size // tile) * tile
    flat = x.reshape(size)
    if padded != size:
        flat = jnp.pad(flat, (0, padded - size))
    flat = flat.reshape(padded // 128, 128)
    cid = cid + (0 if active is None else 2 + active) * 2
    out = gather_blk(flat, n, cid, active).reshape(n, padded)
    if padded != size:
        out = out[:, :size]
    return out.reshape(n * rows, width)


def gather_tokens(x, cid):
    n = lax.axis_size("blk")
    _, rows, width = x.shape
    chunks = width // 128
    per_token = -(-chunks // 16) * 16
    shard = jnp.pad(x.reshape(rows, chunks, 128), ((0, 0), (0, per_token - chunks), (0, 0)))
    out = gather_blk(shard.reshape(rows * per_token, 128), n, cid)
    return out.reshape(n * rows, per_token, 128)[:, :chunks]


def dot_tokens(tokens, weight):
    chunks = tokens.shape[1]
    return jnp.einsum(
        "tal,alc->tc", tokens, weight.reshape(chunks, 128, weight.shape[1]),
        preferred_element_type=jnp.float32,
    ).astype(jnp.bfloat16)


def to_blk_order(rows_in_gather_order, n):
    total, cols = rows_in_gather_order.shape
    nz = n // PLANE
    h = nz // 2
    rows = total // n
    part_a = rows_in_gather_order[: h * PLANE * rows].reshape(NY, NX, h, rows, cols)
    part_b = rows_in_gather_order[h * PLANE * rows :].reshape(NX, NY, nz - h, rows, cols)
    ordered = jnp.concatenate(
        [jnp.transpose(part_a, (2, 1, 0, 3, 4)), jnp.transpose(part_b, (2, 0, 1, 3, 4))], axis=0
    )
    return ordered.reshape(1, total, cols)


def from_behind(shard, axis, by):
    count = lax.axis_size(axis)
    pairs = [(i, i + by) for i in range(count) if 0 <= i + by < count]
    return lax.ppermute(shard, axis, pairs)


def attend(layer_in, qkv_cols, out_cols, modulate, fresh_own, old_keys, old_values, live, active):
    n = lax.axis_size("blk")
    stream = layer_in.astype(jnp.float32)
    center = jnp.mean(stream, axis=-1, keepdims=True)
    variance = jnp.mean((stream - center) ** 2, axis=-1, keepdims=True)
    normed = (stream - center) / jnp.sqrt(variance + 1e-06) * (1.0 + modulate[0]) + modulate[1]
    normed_b = normed.astype(jnp.bfloat16)
    columns = dot_tokens(gather_tokens(normed_b, 2), qkv_cols)
    projected = lax.all_to_all(to_blk_order(columns, n), "blk", split_axis=1, concat_axis=2, tiled=True)
    num_req, num_rows, width = layer_in.shape
    queries = projected[0, :, :width]
    new_keys = projected[:, :, width : 2 * width]
    new_values = projected[:, :, 2 * width :]
    use_fresh = (fresh_own == 1)[:, None, None]
    keys = jnp.where(use_fresh, new_keys, old_keys)
    values = jnp.where(use_fresh, new_values, old_values)
    kv_all = gather_rows(jnp.concatenate([keys, values], axis=2), 1, active)
    key_all = kv_all[:, :width]
    value_all = kv_all[:, width:]
    nz = n // PLANE
    live_zxy = live[0].reshape(nz, NX, NY)
    live_by_slot = jnp.concatenate([
        jnp.transpose(live_zxy[: nz // 2], (2, 1, 0)).reshape(-1),
        jnp.transpose(live_zxy[nz // 2 :], (1, 2, 0)).reshape(-1),
    ])
    usable = (jnp.repeat(live_by_slot, num_rows) == 1)[None, None, :]
    num_heads = width // 64
    head_of_col = jnp.arange(width) // 64
    in_head = head_of_col[None, :] == jnp.arange(num_heads)[:, None]
    q_diag = jnp.where(in_head[None], queries[:, None, :], jnp.zeros((), queries.dtype))
    scores = jnp.einsum("qhc,kc->qhk", q_diag, key_all, preferred_element_type=jnp.float32) * 0.125
    scores = jnp.where(usable, scores, -1e30)
    top = jnp.max(scores, axis=-1, keepdims=True)
    weights = jnp.where(usable, jnp.exp(scores - top), 0.0)
    total = jnp.sum(weights, axis=-1)
    mixed_all = jnp.einsum(
        "qhk,kc->qhc", weights, value_all.astype(jnp.float32), precision=lax.Precision.HIGHEST
    )
    own_head = jnp.sum(jnp.where(in_head[None], mixed_all, 0.0), axis=1)
    total_col = jnp.broadcast_to(total[:, :, None], (num_rows, num_heads, 64)).reshape(num_rows, width)
    attn = (own_head / total_col).astype(jnp.bfloat16)[None]
    out_part = dot_tokens(gather_tokens(attn, 2), out_cols)
    mixed_back = lax.all_to_all(to_blk_order(out_part, n), "blk", split_axis=1, concat_axis=2, tiled=True)
    return (stream + modulate[2] * mixed_back.astype(jnp.float32)).astype(jnp.bfloat16)


def swap_sections(x):
    return lax.ppermute(x, "section", [(0, 1), (1, 0)])


def per_device(hidden, qkv_weight, out_weight, modulation, timestep, fresh, live, k_stale, v_stale):
    sec = lax.axis_index("section")
    block_idx = lax.axis_index("blk")
    steps_all = modulation.shape[1]
    pick_row = (jnp.arange(steps_all) == timestep[0]).astype(jnp.float32)
    modulate_own = jnp.einsum("t,tcd->cd", pick_row, modulation[0], precision=lax.Precision.HIGHEST)
    num_blocks = fresh.shape[2]
    own_column = (jnp.arange(num_blocks) == block_idx).astype(jnp.int32)
    fresh_own = jnp.sum(fresh[0] * own_column[None, :], axis=1)
    qkv_own = qkv_weight[0]
    out_own = out_weight[0]
    stale_own = jnp.concatenate([k_stale[0], v_stale[0]], axis=2)

    qkv_other = swap_sections(qkv_own)
    out_other = swap_sections(out_own)
    modulate_other = swap_sections(modulate_own)
    fresh_other = swap_sections(fresh_own)
    stale_other = swap_sections(lax.dynamic_index_in_dim(stale_own, 1 - sec, 0, keepdims=True))

    stale_mine = lax.dynamic_index_in_dim(stale_own, sec, 0, keepdims=True)
    fresh_mine = lax.dynamic_index_in_dim(fresh_own, sec, 0, keepdims=True)
    fresh_theirs = lax.dynamic_index_in_dim(fresh_other, sec, 0, keepdims=True)
    live_mine = lax.dynamic_index_in_dim(live, sec, 0, keepdims=True)
    width = hidden.shape[2]

    layer_in = lax.dynamic_index_in_dim(hidden, sec, 0, keepdims=True)
    outs = []
    for layer in range(2):
        own = sec == layer
        stale = jnp.where(own, stale_mine, stale_other)
        layer_in = attend(
            layer_in,
            jnp.where(own, qkv_own, qkv_other),
            jnp.where(own, out_own, out_other),
            jnp.where(own, modulate_own, modulate_other),
            jnp.where(own, fresh_mine, fresh_theirs),
            stale[:, :, :width],
            stale[:, :, width:],
            live_mine,
            None,
        )
        outs.append(layer_in)
    first_req1 = lax.ppermute(outs[0], "section", [(1, 0)])
    second_req0 = lax.ppermute(outs[1], "section", [(0, 1)])
    result = jnp.where(
        sec == 0,
        jnp.concatenate([outs[0], first_req1], axis=0),
        jnp.concatenate([second_req0, outs[1]], axis=0),
    )
    return result[None]


def solution(mesh):
    return jax.shard_map(
        per_device,
        mesh=mesh,
        in_specs=(
            P(None, "blk", None),
            P("section", None, "blk"),
            P("section", None, "blk"),
            P("section", None, None, None),
            P(),
            P("section", None, None),
            P(),
            P("section", None, "blk", None),
            P("section", None, "blk", None),
        ),
        out_specs=P("section", None, "blk", None),
        check_vma=False,
    )
```

```python
import functools

import jax
import jax.numpy as jnp
from jax import lax
from jax.experimental import pallas as pl
from jax.experimental.pallas import tpu as pltpu
from jax.sharding import PartitionSpec as P

MESH = pl.DeviceIdType.MESH


NX = 4
NY = 4
PLANE = NX * NY


def gather_kernel(n, x_ref, o_ref, zbuf, zs, zr, rs, rr, local_sem):
    oa_ref = o_ref.at[0]
    ob_ref = o_ref.at[1]
    sec = lax.axis_index("section")
    nz = n // PLANE
    h = nz // 2
    me = lax.axis_index("blk")
    y = me % NY
    x = (me // NY) % NX
    z = me // PLANE

    def dev(zz, xx, yy):
        return (sec, (zz * NX + xx) * NY + yy)

    xp, xm, x2 = (x + 1) % NX, (x + NX - 1) % NX, (x + 2) % NX
    yp, ym, y2 = (y + 1) % NY, (y + NY - 1) % NY, (y + 2) % NY
    barrier = pltpu.get_barrier_semaphore()

    def z_peer(i):
        return lax.rem(z + 1 + i, nz)

    def greet_z(i, carry):
        pl.semaphore_signal(barrier, inc=1, device_id=dev(z_peer(i), x, y), device_id_type=MESH)
        return carry

    lax.fori_loop(0, nz - 1, greet_z, 0)
    for target in (dev(z, xp, y), dev(z, xm, y), dev(z, x, yp), dev(z, x, ym)):
        pl.semaphore_signal(barrier, inc=1, device_id=target, device_id_type=MESH)
    pl.semaphore_wait(barrier, nz - 1 + 4)

    local = pltpu.make_async_copy(x_ref, zbuf.at[z], local_sem.at[0])
    local.start()

    def copy_z(i, src_z):
        return pltpu.make_async_remote_copy(
            src_ref=x_ref,
            dst_ref=zbuf.at[src_z],
            send_sem=zs.at[i],
            recv_sem=zr.at[src_z],
            device_id=dev(z_peer(i), x, y),
            device_id_type=MESH,
        )

    def send_z(i, carry):
        copy_z(i, z).start()
        return carry

    lax.fori_loop(0, nz - 1, send_z, 0)

    def finish_z(i, carry):
        copy_z(i, z).wait_send()
        copy_z(i, lax.rem(z + nz - 1 - i, nz)).wait_recv()
        return carry

    lax.fori_loop(0, nz - 1, finish_z, 0)
    local.wait()
    own_a = pltpu.make_async_copy(zbuf.at[pl.ds(0, h)], oa_ref.at[y, x], local_sem.at[1])
    own_b = pltpu.make_async_copy(zbuf.at[pl.ds(h, nz - h)], ob_ref.at[x, y], local_sem.at[2])
    own_a.start()
    own_b.start()

    def rcopy(stage, src, dst, k, target):
        return pltpu.make_async_remote_copy(
            src_ref=src, dst_ref=dst, send_sem=rs.at[stage, k], recv_sem=rr.at[stage, k],
            device_id=target, device_id_type=MESH,
        )

    class Ring:
        def __init__(self, stage, mine, block, up, down, far, count, target_up, target_down):
            self.stage, self.mine, self.block = stage, mine, block
            self.up, self.down, self.far, self.count = up, down, far, count
            self.target_up, self.target_down = target_up, target_down

        def step1(self):
            s, me_ref = self.stage, self.block(None)
            self.a = rcopy(s, self.mine, me_ref, 0, self.target_up)
            self.b = rcopy(s, self.mine, me_ref, 1, self.target_down)
            self.a.start()
            self.b.start()

        def wait1(self):
            s = self.stage
            self.a.wait_send()
            self.b.wait_send()
            rcopy(s, self.block(self.down), self.block(self.down), 0, self.target_down).wait_recv()
            rcopy(s, self.block(self.up), self.block(self.up), 1, self.target_up).wait_recv()

        def step2(self):
            s, half = self.stage, self.count // 2
            first = self.block(self.down).at[pl.ds(0, half)]
            second = self.block(self.up).at[pl.ds(half, self.count - half)]
            self.c = rcopy(s, first, first, 2, self.target_up)
            self.d = rcopy(s, second, second, 3, self.target_down)
            self.c.start()
            self.d.start()

        def wait2(self):
            s, half = self.stage, self.count // 2
            self.c.wait_send()
            self.d.wait_send()
            first = self.block(self.far).at[pl.ds(0, half)]
            second = self.block(self.far).at[pl.ds(half, self.count - half)]
            rcopy(s, first, first, 2, self.target_down).wait_recv()
            rcopy(s, second, second, 3, self.target_up).wait_recv()

    x_targets = (dev(z, xp, y), dev(z, xm, y))
    y_targets = (dev(z, x, yp), dev(z, x, ym))
    a_x = Ring(0, zbuf.at[pl.ds(0, h)], lambda p: oa_ref.at[y, x if p is None else p],
               xp, xm, x2, h, *x_targets)
    b_y = Ring(1, zbuf.at[pl.ds(h, nz - h)], lambda p: ob_ref.at[x, y if p is None else p],
               yp, ym, y2, nz - h, *y_targets)
    a_y = Ring(2, oa_ref.at[y], lambda p: oa_ref.at[y if p is None else p],
               yp, ym, y2, NX, *y_targets)
    b_x = Ring(3, ob_ref.at[x], lambda p: ob_ref.at[x if p is None else p],
               xp, xm, x2, NY, *x_targets)
    for first, second in ((a_x, b_y), (a_y, b_x)):
        first.step1()
        second.step1()
        first.wait1()
        second.wait1()
        first.step2()
        second.step2()
        first.wait2()
        second.wait2()
        if first is a_x:
            own_a.wait()
            own_b.wait()


def gather_blk(x, n, cid, active=None):
    nz = n // PLANE
    h = nz // 2
    assert NX == NY and nz == 2 * h
    out = pl.pallas_call(
        functools.partial(gather_kernel, n),
        out_shape=jax.ShapeDtypeStruct((2, NY, NX, h) + x.shape, x.dtype),
        in_specs=[pl.BlockSpec(memory_space=pl.ANY)],
        out_specs=pl.BlockSpec(memory_space=pl.ANY),
        scratch_shapes=[
            pltpu.VMEM((nz,) + x.shape, x.dtype),
            pltpu.SemaphoreType.DMA((nz,)),
            pltpu.SemaphoreType.DMA((nz,)),
            pltpu.SemaphoreType.DMA((4, 4)),
            pltpu.SemaphoreType.DMA((4, 4)),
            pltpu.SemaphoreType.DMA((3,)),
        ],
        compiler_params=pltpu.CompilerParams(collective_id=cid, has_side_effects=True),
    )(x)
    return out.reshape((n,) + x.shape)


def gather_rows(x, cid, active):
    n = lax.axis_size("blk")
    _, rows, width = x.shape
    size = rows * width
    tile = 16 * 128
    padded = -(-size // tile) * tile
    flat = x.reshape(size)
    if padded != size:
        flat = jnp.pad(flat, (0, padded - size))
    flat = flat.reshape(padded // 128, 128)
    cid = cid + (0 if active is None else 2 + active) * 2
    out = gather_blk(flat, n, cid, active).reshape(n, padded)
    if padded != size:
        out = out[:, :size]
    return out.reshape(n * rows, width)


def gather_tokens(x, cid):
    n = lax.axis_size("blk")
    _, rows, width = x.shape
    chunks = width // 128
    per_token = -(-chunks // 16) * 16
    shard = jnp.pad(x.reshape(rows, chunks, 128), ((0, 0), (0, per_token - chunks), (0, 0)))
    out = gather_blk(shard.reshape(rows * per_token, 128), n, cid)
    return out.reshape(n * rows, per_token, 128)[:, :chunks]


def dot_tokens(tokens, weight):
    chunks = tokens.shape[1]
    return jnp.einsum(
        "tal,alc->tc", tokens, weight.reshape(chunks, 128, weight.shape[1]),
        preferred_element_type=jnp.float32,
    ).astype(jnp.bfloat16)


def to_blk_order(rows_in_gather_order, n):
    total, cols = rows_in_gather_order.shape
    nz = n // PLANE
    h = nz // 2
    rows = total // n
    part_a = rows_in_gather_order[: h * PLANE * rows].reshape(NY, NX, h, rows, cols)
    part_b = rows_in_gather_order[h * PLANE * rows :].reshape(NX, NY, nz - h, rows, cols)
    ordered = jnp.concatenate(
        [jnp.transpose(part_a, (2, 1, 0, 3, 4)), jnp.transpose(part_b, (2, 0, 1, 3, 4))], axis=0
    )
    return ordered.reshape(1, total, cols)


def from_behind(shard, axis, by):
    count = lax.axis_size(axis)
    pairs = [(i, i + by) for i in range(count) if 0 <= i + by < count]
    return lax.ppermute(shard, axis, pairs)


def attend(layer_in, qkv_cols, out_cols, modulate, fresh_own, old_keys, old_values, live, active):
    n = lax.axis_size("blk")
    stream = layer_in.astype(jnp.float32)
    center = jnp.mean(stream, axis=-1, keepdims=True)
    variance = jnp.mean((stream - center) ** 2, axis=-1, keepdims=True)
    normed = (stream - center) / jnp.sqrt(variance + 1e-06) * (1.0 + modulate[0]) + modulate[1]
    normed_b = normed.astype(jnp.bfloat16)
    columns = dot_tokens(gather_tokens(normed_b, 2), qkv_cols)
    projected = lax.all_to_all(to_blk_order(columns, n), "blk", split_axis=1, concat_axis=2, tiled=True)
    num_req, num_rows, width = layer_in.shape
    queries = projected[0, :, :width]
    new_keys = projected[:, :, width : 2 * width]
    new_values = projected[:, :, 2 * width :]
    use_fresh = (fresh_own == 1)[:, None, None]
    keys = jnp.where(use_fresh, new_keys, old_keys)
    values = jnp.where(use_fresh, new_values, old_values)
    kv_all = gather_tokens(jnp.concatenate([keys, values], axis=2), 3)
    chunks = width // 128
    key_all = kv_all[:, :chunks]
    value_all = kv_all[:, chunks:]
    nz = n // PLANE
    live_zxy = live[0].reshape(nz, NX, NY)
    live_by_slot = jnp.concatenate([
        jnp.transpose(live_zxy[: nz // 2], (2, 1, 0)).reshape(-1),
        jnp.transpose(live_zxy[nz // 2 :], (1, 2, 0)).reshape(-1),
    ])
    usable = (jnp.repeat(live_by_slot, num_rows) == 1)[None, None, :]
    num_heads = width // 64
    head_of_col = jnp.arange(width) // 64
    in_head = head_of_col[None, :] == jnp.arange(num_heads)[:, None]
    q_diag = jnp.where(in_head[None], queries[:, None, :], jnp.zeros((), queries.dtype))
    q_diag = q_diag.reshape(num_rows, num_heads, chunks, 128)
    scores = jnp.einsum("qhal,kal->qhk", q_diag, key_all, preferred_element_type=jnp.float32) * 0.125
    scores = jnp.where(usable, scores, -1e30)
    top = jnp.max(scores, axis=-1, keepdims=True)
    weights = jnp.where(usable, jnp.exp(scores - top), 0.0)
    total = jnp.sum(weights, axis=-1)
    mixed_all = jnp.einsum(
        "qhk,kal->qhal", weights, value_all.astype(jnp.float32), precision=lax.Precision.HIGHEST
    ).reshape(num_rows, num_heads, width)
    own_head = jnp.sum(jnp.where(in_head[None], mixed_all, 0.0), axis=1)
    total_col = jnp.broadcast_to(total[:, :, None], (num_rows, num_heads, 64)).reshape(num_rows, width)
    attn = (own_head / total_col).astype(jnp.bfloat16)[None]
    out_part = dot_tokens(gather_tokens(attn, 2), out_cols)
    mixed_back = lax.all_to_all(to_blk_order(out_part, n), "blk", split_axis=1, concat_axis=2, tiled=True)
    return (stream + modulate[2] * mixed_back.astype(jnp.float32)).astype(jnp.bfloat16)


def swap_sections(x):
    return lax.ppermute(x, "section", [(0, 1), (1, 0)])


def per_device(hidden, qkv_weight, out_weight, modulation, timestep, fresh, live, k_stale, v_stale):
    sec = lax.axis_index("section")
    block_idx = lax.axis_index("blk")
    steps_all = modulation.shape[1]
    pick_row = (jnp.arange(steps_all) == timestep[0]).astype(jnp.float32)
    modulate_own = jnp.einsum("t,tcd->cd", pick_row, modulation[0], precision=lax.Precision.HIGHEST)
    num_blocks = fresh.shape[2]
    own_column = (jnp.arange(num_blocks) == block_idx).astype(jnp.int32)
    fresh_own = jnp.sum(fresh[0] * own_column[None, :], axis=1)
    qkv_own = qkv_weight[0]
    out_own = out_weight[0]
    stale_own = jnp.concatenate([k_stale[0], v_stale[0]], axis=2)

    qkv_other = swap_sections(qkv_own)
    out_other = swap_sections(out_own)
    modulate_other = swap_sections(modulate_own)
    fresh_other = swap_sections(fresh_own)
    stale_other = swap_sections(lax.dynamic_index_in_dim(stale_own, 1 - sec, 0, keepdims=True))

    stale_mine = lax.dynamic_index_in_dim(stale_own, sec, 0, keepdims=True)
    fresh_mine = lax.dynamic_index_in_dim(fresh_own, sec, 0, keepdims=True)
    fresh_theirs = lax.dynamic_index_in_dim(fresh_other, sec, 0, keepdims=True)
    live_mine = lax.dynamic_index_in_dim(live, sec, 0, keepdims=True)
    width = hidden.shape[2]

    layer_in = lax.dynamic_index_in_dim(hidden, sec, 0, keepdims=True)
    outs = []
    for layer in range(2):
        own = sec == layer
        stale = jnp.where(own, stale_mine, stale_other)
        layer_in = attend(
            layer_in,
            jnp.where(own, qkv_own, qkv_other),
            jnp.where(own, out_own, out_other),
            jnp.where(own, modulate_own, modulate_other),
            jnp.where(own, fresh_mine, fresh_theirs),
            stale[:, :, :width],
            stale[:, :, width:],
            live_mine,
            None,
        )
        outs.append(layer_in)
    first_req1 = lax.ppermute(outs[0], "section", [(1, 0)])
    second_req0 = lax.ppermute(outs[1], "section", [(0, 1)])
    result = jnp.where(
        sec == 0,
        jnp.concatenate([outs[0], first_req1], axis=0),
        jnp.concatenate([second_req0, outs[1]], axis=0),
    )
    return result[None]


def solution(mesh):
    return jax.shard_map(
        per_device,
        mesh=mesh,
        in_specs=(
            P(None, "blk", None),
            P("section", None, "blk"),
            P("section", None, "blk"),
            P("section", None, None, None),
            P(),
            P("section", None, None),
            P(),
            P("section", None, "blk", None),
            P("section", None, "blk", None),
        ),
        out_specs=P("section", None, "blk", None),
        check_vma=False,
    )
```

```python
import functools

import jax
import jax.numpy as jnp
from jax import lax
from jax.experimental import pallas as pl
from jax.experimental.pallas import tpu as pltpu
from jax.sharding import PartitionSpec as P

MESH = pl.DeviceIdType.MESH


NX = 4
NY = 4
PLANE = NX * NY


def gather_kernel(n, x_ref, o_ref, zbuf, zs, zr, rs, rr, local_sem):
    oa_ref = o_ref.at[0]
    ob_ref = o_ref.at[1]
    sec = lax.axis_index("section")
    nz = n // PLANE
    h = nz // 2
    me = lax.axis_index("blk")
    y = me % NY
    x = (me // NY) % NX
    z = me // PLANE

    def dev(zz, xx, yy):
        return (sec, (zz * NX + xx) * NY + yy)

    xp, xm, x2 = (x + 1) % NX, (x + NX - 1) % NX, (x + 2) % NX
    yp, ym, y2 = (y + 1) % NY, (y + NY - 1) % NY, (y + 2) % NY
    barrier = pltpu.get_barrier_semaphore()

    def z_peer(i):
        return lax.rem(z + 1 + i, nz)

    def greet_z(i, carry):
        pl.semaphore_signal(barrier, inc=1, device_id=dev(z_peer(i), x, y), device_id_type=MESH)
        return carry

    lax.fori_loop(0, nz - 1, greet_z, 0)
    for target in (dev(z, xp, y), dev(z, xm, y), dev(z, x, yp), dev(z, x, ym)):
        pl.semaphore_signal(barrier, inc=1, device_id=target, device_id_type=MESH)
    pl.semaphore_wait(barrier, nz - 1 + 4)

    local = pltpu.make_async_copy(x_ref, zbuf.at[z], local_sem.at[0])
    local.start()

    def copy_z(i, src_z):
        return pltpu.make_async_remote_copy(
            src_ref=x_ref,
            dst_ref=zbuf.at[src_z],
            send_sem=zs.at[i],
            recv_sem=zr.at[src_z],
            device_id=dev(z_peer(i), x, y),
            device_id_type=MESH,
        )

    def send_z(i, carry):
        copy_z(i, z).start()
        return carry

    lax.fori_loop(0, nz - 1, send_z, 0)

    def finish_z(i, carry):
        copy_z(i, z).wait_send()
        copy_z(i, lax.rem(z + nz - 1 - i, nz)).wait_recv()
        return carry

    lax.fori_loop(0, nz - 1, finish_z, 0)
    local.wait()
    own_a = pltpu.make_async_copy(zbuf.at[pl.ds(0, h)], oa_ref.at[y, x], local_sem.at[1])
    own_b = pltpu.make_async_copy(zbuf.at[pl.ds(h, nz - h)], ob_ref.at[x, y], local_sem.at[2])
    own_a.start()
    own_b.start()

    def rcopy(stage, src, dst, k, target):
        return pltpu.make_async_remote_copy(
            src_ref=src, dst_ref=dst, send_sem=rs.at[stage, k], recv_sem=rr.at[stage, k],
            device_id=target, device_id_type=MESH,
        )

    class Ring:
        def __init__(self, stage, mine, block, up, down, far, count, target_up, target_down):
            self.stage, self.mine, self.block = stage, mine, block
            self.up, self.down, self.far, self.count = up, down, far, count
            self.target_up, self.target_down = target_up, target_down

        def step1(self):
            s, me_ref = self.stage, self.block(None)
            self.a = rcopy(s, self.mine, me_ref, 0, self.target_up)
            self.b = rcopy(s, self.mine, me_ref, 1, self.target_down)
            self.a.start()
            self.b.start()

        def wait1(self):
            s = self.stage
            self.a.wait_send()
            self.b.wait_send()
            rcopy(s, self.block(self.down), self.block(self.down), 0, self.target_down).wait_recv()
            rcopy(s, self.block(self.up), self.block(self.up), 1, self.target_up).wait_recv()

        def step2(self):
            s, half = self.stage, self.count // 2
            first = self.block(self.down).at[pl.ds(0, half)]
            second = self.block(self.up).at[pl.ds(half, self.count - half)]
            self.c = rcopy(s, first, first, 2, self.target_up)
            self.d = rcopy(s, second, second, 3, self.target_down)
            self.c.start()
            self.d.start()

        def wait2(self):
            s, half = self.stage, self.count // 2
            self.c.wait_send()
            self.d.wait_send()
            first = self.block(self.far).at[pl.ds(0, half)]
            second = self.block(self.far).at[pl.ds(half, self.count - half)]
            rcopy(s, first, first, 2, self.target_down).wait_recv()
            rcopy(s, second, second, 3, self.target_up).wait_recv()

    x_targets = (dev(z, xp, y), dev(z, xm, y))
    y_targets = (dev(z, x, yp), dev(z, x, ym))
    a_x = Ring(0, zbuf.at[pl.ds(0, h)], lambda p: oa_ref.at[y, x if p is None else p],
               xp, xm, x2, h, *x_targets)
    b_y = Ring(1, zbuf.at[pl.ds(h, nz - h)], lambda p: ob_ref.at[x, y if p is None else p],
               yp, ym, y2, nz - h, *y_targets)
    a_y = Ring(2, oa_ref.at[y], lambda p: oa_ref.at[y if p is None else p],
               yp, ym, y2, NX, *y_targets)
    b_x = Ring(3, ob_ref.at[x], lambda p: ob_ref.at[x if p is None else p],
               xp, xm, x2, NY, *x_targets)
    for first, second in ((a_x, b_y), (a_y, b_x)):
        first.step1()
        second.step1()
        first.wait1()
        second.wait1()
        first.step2()
        second.step2()
        first.wait2()
        second.wait2()
        if first is a_x:
            own_a.wait()
            own_b.wait()


def gather_blk(x, n, cid, active=None):
    nz = n // PLANE
    h = nz // 2
    assert NX == NY and nz == 2 * h
    out = pl.pallas_call(
        functools.partial(gather_kernel, n),
        out_shape=jax.ShapeDtypeStruct((2, NY, NX, h) + x.shape, x.dtype),
        in_specs=[pl.BlockSpec(memory_space=pl.ANY)],
        out_specs=pl.BlockSpec(memory_space=pl.ANY),
        scratch_shapes=[
            pltpu.VMEM((nz,) + x.shape, x.dtype),
            pltpu.SemaphoreType.DMA((nz,)),
            pltpu.SemaphoreType.DMA((nz,)),
            pltpu.SemaphoreType.DMA((4, 4)),
            pltpu.SemaphoreType.DMA((4, 4)),
            pltpu.SemaphoreType.DMA((3,)),
        ],
        compiler_params=pltpu.CompilerParams(collective_id=cid, has_side_effects=True),
    )(x)
    return out.reshape((n,) + x.shape)


def gather_rows(x, cid, active):
    n = lax.axis_size("blk")
    _, rows, width = x.shape
    size = rows * width
    tile = 16 * 128
    padded = -(-size // tile) * tile
    flat = x.reshape(size)
    if padded != size:
        flat = jnp.pad(flat, (0, padded - size))
    flat = flat.reshape(padded // 128, 128)
    cid = cid + (0 if active is None else 2 + active) * 2
    out = gather_blk(flat, n, cid, active).reshape(n, padded)
    if padded != size:
        out = out[:, :size]
    return out.reshape(n * rows, width)


def gather_tokens(x, cid):
    n = lax.axis_size("blk")
    _, rows, width = x.shape
    chunks = width // 128
    per_token = -(-chunks // 16) * 16
    shard = jnp.pad(x.reshape(rows, chunks, 128), ((0, 0), (0, per_token - chunks), (0, 0)))
    out = gather_blk(shard.reshape(rows * per_token, 128), n, cid)
    return out.reshape(n * rows, per_token, 128)[:, :chunks]


def dot_tokens(tokens, weight):
    chunks = tokens.shape[1]
    return jnp.einsum(
        "tal,alc->tc", tokens, weight.reshape(chunks, 128, weight.shape[1]),
        preferred_element_type=jnp.float32,
    ).astype(jnp.bfloat16)


def to_blk_order(rows_in_gather_order, n):
    total, cols = rows_in_gather_order.shape
    nz = n // PLANE
    h = nz // 2
    rows = total // n
    part_a = rows_in_gather_order[: h * PLANE * rows].reshape(NY, NX, h, rows, cols)
    part_b = rows_in_gather_order[h * PLANE * rows :].reshape(NX, NY, nz - h, rows, cols)
    ordered = jnp.concatenate(
        [jnp.transpose(part_a, (2, 1, 0, 3, 4)), jnp.transpose(part_b, (2, 0, 1, 3, 4))], axis=0
    )
    return ordered.reshape(1, total, cols)


def from_behind(shard, axis, by):
    count = lax.axis_size(axis)
    pairs = [(i, i + by) for i in range(count) if 0 <= i + by < count]
    return lax.ppermute(shard, axis, pairs)


def attend(layer_in, qkv_cols, out_cols, modulate, fresh_own, old_keys, old_values, live, active):
    n = lax.axis_size("blk")
    stream = layer_in.astype(jnp.float32)
    center = jnp.mean(stream, axis=-1, keepdims=True)
    variance = jnp.mean((stream - center) ** 2, axis=-1, keepdims=True)
    normed = (stream - center) / jnp.sqrt(variance + 1e-06) * (1.0 + modulate[0]) + modulate[1]
    normed_b = normed.astype(jnp.bfloat16)
    columns = dot_tokens(gather_tokens(normed_b, 2), qkv_cols)
    projected = lax.all_to_all(to_blk_order(columns, n), "blk", split_axis=1, concat_axis=2, tiled=True)
    num_req, num_rows, width = layer_in.shape
    queries = projected[0, :, :width]
    new_keys = projected[:, :, width : 2 * width]
    new_values = projected[:, :, 2 * width :]
    use_fresh = (fresh_own == 1)[:, None, None]
    keys = jnp.where(use_fresh, new_keys, old_keys)
    values = jnp.where(use_fresh, new_values, old_values)
    kv_all = gather_tokens(jnp.concatenate([keys, values], axis=2), 3)
    chunks = width // 128
    key_all = kv_all[:, :chunks]
    value_all = kv_all[:, chunks:]
    nz = n // PLANE
    live_zxy = live[0].reshape(nz, NX, NY)
    live_by_slot = jnp.concatenate([
        jnp.transpose(live_zxy[: nz // 2], (2, 1, 0)).reshape(-1),
        jnp.transpose(live_zxy[nz // 2 :], (1, 2, 0)).reshape(-1),
    ])
    usable = (jnp.repeat(live_by_slot, num_rows) == 1)[None, None, :]
    num_heads = width // 64
    head_of_col = jnp.arange(width) // 64
    in_head = head_of_col[None, :] == jnp.arange(num_heads)[:, None]
    q_diag = jnp.where(in_head[None], queries[:, None, :], jnp.zeros((), queries.dtype))
    q_diag = q_diag.reshape(num_rows, num_heads, chunks, 128)
    scores = jnp.einsum("qhal,kal->qhk", q_diag, key_all, preferred_element_type=jnp.float32) * 0.125
    scores = jnp.where(usable, scores, -1e30)
    top = jnp.max(scores, axis=-1, keepdims=True)
    weights = jnp.where(usable, jnp.exp(scores - top), 0.0)
    total = jnp.sum(weights, axis=-1)
    mixed_all = jnp.einsum(
        "qhk,kal->qhal", weights, value_all.astype(jnp.float32), precision=lax.Precision.HIGHEST
    ).reshape(num_rows, num_heads, width)
    own_head = jnp.sum(jnp.where(in_head[None], mixed_all, 0.0), axis=1)
    total_col = jnp.broadcast_to(total[:, :, None], (num_rows, num_heads, 64)).reshape(num_rows, width)
    attn = (own_head / total_col).astype(jnp.bfloat16)[None]
    out_part = dot_tokens(gather_tokens(attn, 2), out_cols)
    mixed_back = lax.all_to_all(to_blk_order(out_part, n), "blk", split_axis=1, concat_axis=2, tiled=True)
    return (stream + modulate[2] * mixed_back.astype(jnp.float32)).astype(jnp.bfloat16)


def swap_sections(x):
    return lax.ppermute(x, "section", [(0, 1), (1, 0)])


def per_device(hidden, qkv_weight, out_weight, modulation, timestep, fresh, live, k_stale, v_stale):
    sec = lax.axis_index("section")
    block_idx = lax.axis_index("blk")
    steps_all = modulation.shape[1]
    modulate_own = lax.dynamic_index_in_dim(modulation[0], jnp.clip(timestep[0], 0, steps_all - 1), 0, keepdims=False)
    num_blocks = fresh.shape[2]
    own_column = (jnp.arange(num_blocks) == block_idx).astype(jnp.int32)
    fresh_own = jnp.sum(fresh[0] * own_column[None, :], axis=1)
    qkv_own = qkv_weight[0]
    out_own = out_weight[0]
    stale_own = jnp.concatenate([k_stale[0], v_stale[0]], axis=2)

    qkv_other = swap_sections(qkv_own)
    out_other = swap_sections(out_own)
    modulate_other = swap_sections(modulate_own)
    fresh_other = swap_sections(fresh_own)
    stale_other = swap_sections(lax.dynamic_index_in_dim(stale_own, 1 - sec, 0, keepdims=True))

    stale_mine = lax.dynamic_index_in_dim(stale_own, sec, 0, keepdims=True)
    fresh_mine = lax.dynamic_index_in_dim(fresh_own, sec, 0, keepdims=True)
    fresh_theirs = lax.dynamic_index_in_dim(fresh_other, sec, 0, keepdims=True)
    live_mine = lax.dynamic_index_in_dim(live, sec, 0, keepdims=True)
    width = hidden.shape[2]

    layer_in = lax.dynamic_index_in_dim(hidden, sec, 0, keepdims=True)
    outs = []
    for layer in range(2):
        own = sec == layer
        stale = jnp.where(own, stale_mine, stale_other)
        layer_in = attend(
            layer_in,
            jnp.where(own, qkv_own, qkv_other),
            jnp.where(own, out_own, out_other),
            jnp.where(own, modulate_own, modulate_other),
            jnp.where(own, fresh_mine, fresh_theirs),
            stale[:, :, :width],
            stale[:, :, width:],
            live_mine,
            None,
        )
        outs.append(layer_in)
    first_req1 = lax.ppermute(outs[0], "section", [(1, 0)])
    second_req0 = lax.ppermute(outs[1], "section", [(0, 1)])
    result = jnp.where(
        sec == 0,
        jnp.concatenate([outs[0], first_req1], axis=0),
        jnp.concatenate([second_req0, outs[1]], axis=0),
    )
    return result[None]


def solution(mesh):
    return jax.shard_map(
        per_device,
        mesh=mesh,
        in_specs=(
            P(None, "blk", None),
            P("section", None, "blk"),
            P("section", None, "blk"),
            P("section", None, None, None),
            P(),
            P("section", None, None),
            P(),
            P("section", None, "blk", None),
            P("section", None, "blk", None),
        ),
        out_specs=P("section", None, "blk", None),
        check_vma=False,
    )
```
